32 devices in a mesh: dp: 8 (over z, y), blk: 4 (over x, core).
Axes of the slice: x: 2, y: 2, z: 4, core: 2. Of those that a mesh axis runs over, the one named last changes fastest.
Arguments:
- tokens: bfloat16 [8, 512, 768], P('dp', 'blk'), may hold values from -6 to 6
- early_gain: bfloat16 [768], replicated, may hold values from 0.5 to 1.5
- early_shift: bfloat16 [768], replicated, may hold values from -4 to 4
- query_weight: bfloat16 [768, 768], replicated, may hold values from -0.21875 to 0.21875
- query_bias: bfloat16 [768], replicated, may hold values from -4 to 4
- key_weight: bfloat16 [768, 768], replicated, may hold values from -0.21875 to 0.21875
- value_weight: bfloat16 [768, 768], replicated, may hold values from -0.21875 to 0.21875
- value_bias: bfloat16 [768], replicated, may hold values from -0.75 to 0.75
- output_weight: bfloat16 [768, 768], replicated, may hold values from -2.5 to 2.5
- output_bias: bfloat16 [768], replicated, may hold values from -4 to 4
- late_gain: bfloat16 [768], replicated, may hold values from 0.5 to 1.5
- late_shift: bfloat16 [768], replicated, may hold values from -4 to 4
- expand_weight: bfloat16 [768, 3072], replicated, may hold values from -0.21875 to 0.21875
- expand_bias: bfloat16 [3072], replicated, may hold values from -4 to 4
- contract_weight: bfloat16 [3072, 768], replicated, may hold values from -0.109375 to 0.109375
- contract_bias: bfloat16 [768], replicated, may hold values from -4 to 4
- upstream: bfloat16 [8, 512, 768], P('dp', 'blk'), may hold values from -6 to 6
- clip_ids: int32 [8, 512], P('dp'), may hold values from 0 to 3, never falling along the last dimension, each value on 1 to 256 neighbouring positions
- block_order: int32 [8, 4], P('dp'), may hold values from 0 to 3, each once within a row
Outputs:
- block_out: bfloat16 [8, 512, 768], P('dp', 'blk')
- token_grad: bfloat16 [8, 512, 768], P('dp', 'blk')
- gain_early: float32 [768], P('dp')
- shift_early: float32 [768], P('dp')
- query_grad: float32 [768, 768], P('dp')
- bias_query: float32 [768], P('dp')
- key_grad: float32 [768, 768], P('dp')
- value_grad: float32 [768, 768], P('dp')
- bias_value: float32 [768], P('dp')
- output_grad: float32 [768, 768], P('dp')
- bias_output: float32 [768], P('dp')
- gain_late: float32 [768], P('dp')
- shift_late: float32 [768], P('dp')
- expand_grad: float32 [768, 3072], P('dp')
- bias_expand: float32 [3072], P('dp')
- contract_grad: float32 [3072, 768], P('dp')
- bias_contract: float32 [768], P('dp')
The draws below stay inside these ranges and needn't reach their ends.
Inputs may be any that keep to these rules, and one draw needn't show every extreme that they name: `clip_ids`: along the logical positions of each row the clip number never falls; every row holds clips 0 to 3, each of 1 to 256 tokens, and in each row one clip has exactly 256. Each row is a permutation of 0 to 3; index j of blk holds, of each of its rows, the 128 tokens of logical positions block_order[row, j] * 128 onward.
All inputs are finite; a program needn't handle non-finite values.
Results may differ from the reference program's by a relative error of at most 0.02.
Values may be sent and summed in bfloat16 or wider, within the bound.
A program may use at most 192 MiB of HBM per device.

```python
import math
import jax
import jax.numpy as jnp
import numpy as np
from jax import lax

D = 768
HEADS = 12
HEAD_DIM = 64
FF = 3072
BLK_TOK = 128
CLIPS = 4
ROWS = 8
ROW_LEN = 512
N_BLK = 4


def block_scale(key, shape, cuts, smallest, high):
    def one(position, blocks):
        draws = jax.random.uniform(jax.random.fold_in(jax.random.fold_in(key, 6), position), (blocks,), jnp.float32, smallest / len(cuts), high / len(cuts))
        return jnp.repeat(jnp.exp(draws), shape[position] // blocks).reshape((-1,) + (1,) * (len(shape) - position - 1))

    loudness = one(*cuts[0])
    for cut in cuts[1:]:
        loudness = loudness * one(*cut)
    return loudness


def length_profile(number_of, total, most, lean):
    portions = [(1 << 20) // math.isqrt(grade ** lean) + 1 for grade in range(2, number_of + 1)]
    rest, counts = total - most - (number_of - 1), [1] * (number_of - 1)
    while rest > 0:
        movable = [i for i in range(number_of - 1) if counts[i] < most]
        whole, remaining = sum([portions[i] for i in movable]), rest
        for i in movable:
            addition = min(most - counts[i], max(1, remaining * portions[i] // whole), rest)
            counts[i] = counts[i] + addition
            rest = rest - addition
    return np.array([most] + counts)


def uneven_parts(key, amount, total, most, skew):
    if amount == 2:
        one = jax.random.randint(key, (), max(1, total - most), min(most, total - 1) + 1)
        return jnp.stack([one, total - one])
    tallies = jnp.asarray(length_profile(amount, total, most, skew), jnp.int32)
    twos = (amount - 1) // 2
    giver, taker = tallies[1:1 + 2 * twos:2], tallies[2:2 + 2 * twos:2]
    slack = jnp.minimum(giver - 1, most - taker)
    passed = jax.random.randint(jax.random.fold_in(key, 1), (twos,), 0, 1 << 20) % (slack + 1)
    tallies = tallies.at[1:1 + 2 * twos:2].set(giver - passed).at[2:2 + 2 * twos:2].set(taker + passed)
    return tallies[jax.random.permutation(jax.random.fold_in(key, 2), amount)]


def normal_values(own_key, shape, width, bound, shards=(), dtype=jnp.bfloat16):
    level = block_scale(own_key, shape, shards, -0.22, 0.18) if shards else 1.0
    drawn = jax.random.normal(own_key, shape, jnp.float32) * width * level
    return jnp.minimum(jnp.maximum(drawn, -bound), bound).astype(dtype)


def setup_inputs(seed: int = 0) -> dict:
    splits = jax.random.split(jax.random.key(seed), 20)
    return {
        "tokens": normal_values(splits[0], (ROWS, ROW_LEN, D), 1.0, 6.0, ((0, 8), (1, 4))),
        "early_gain": jnp.clip(1.0 + 0.1 * jax.random.normal(splits[1], (D,), jnp.float32), 0.5, 1.5).astype(jnp.bfloat16),
        "early_shift": normal_values(splits[2], (D,), 0.3, 4.0),
        "query_weight": normal_values(splits[3], (D, D), D ** -0.5, 0.21875),
        "query_bias": normal_values(splits[4], (D,), 0.3, 4.0),
        "key_weight": normal_values(splits[5], (D, D), D ** -0.5, 0.21875),
        "value_weight": normal_values(splits[6], (D, D), D ** -0.5, 0.21875),
        "value_bias": normal_values(splits[7], (D,), 0.05, 0.75),
        "output_weight": normal_values(splits[8], (D, D), (max(D // 128, 4)) ** -0.5, 2.5),
        "output_bias": normal_values(splits[9], (D,), 0.3, 4.0),
        "late_gain": jnp.clip(1.0 + 0.1 * jax.random.normal(splits[10], (D,), jnp.float32), 0.5, 1.5).astype(jnp.bfloat16),
        "late_shift": normal_values(splits[11], (D,), 0.3, 4.0),
        "expand_weight": normal_values(splits[12], (D, FF), D ** -0.5, 0.21875),
        "expand_bias": normal_values(splits[13], (FF,), 0.3, 4.0),
        "contract_weight": normal_values(splits[14], (FF, D), FF ** -0.5, 0.109375),
        "contract_bias": normal_values(splits[15], (D,), 0.3, 4.0),
        "upstream": normal_values(splits[16], (ROWS, ROW_LEN, D), 1.0, 6.0, ((0, 8), (1, 4))),
        "clip_ids": jax.vmap(lambda own: jnp.searchsorted(jnp.cumsum(uneven_parts(own, CLIPS, ROW_LEN, ROW_LEN // 2, 1)), jnp.arange(ROW_LEN), side="right"))(jax.random.split(splits[17], ROWS)).reshape((ROWS, ROW_LEN)).astype(jnp.int32),
        "block_order": jax.vmap(lambda own: jax.random.permutation(own, N_BLK))(jax.random.split(splits[18], ROWS)).reshape((ROWS, N_BLK)).astype(jnp.int32),
    }


EPSILON = 1e-05
MASKED = -1e+30

@jax.custom_vjp
def low(v):
    return lax.optimization_barrier(v.astype(jnp.bfloat16)).astype(jnp.float32)

@jax.custom_vjp
def low_back(v):
    return v

def low_keep(v):
    return (low(v), None)

def low_pass(kept, grad):
    return (grad,)

def back_keep(v):
    return (v, None)

def back_low(kept, grad):
    return (low(grad),)
low.defvjp(low_keep, low_pass)
low_back.defvjp(back_keep, back_low)

def norm_row(inputs, gain, shift):
    average = lax.optimization_barrier(jnp.mean(inputs, axis=-1, keepdims=True))
    centred = inputs - average
    return centred * lax.rsqrt(lax.optimization_barrier(jnp.mean(centred * centred, axis=-1, keepdims=True)) + EPSILON) * gain + shift

def matmul(left, right):
    return jnp.dot(left, right, precision=lax.Precision.HIGHEST, preferred_element_type=jnp.float32)

def row_forward(params, row_in, clips):
    early_gain, early_shift, query_weight, query_bias, key_weight, value_weight, value_bias, output_weight, output_bias, late_gain, late_shift, expand_weight, expand_bias, contract_weight, contract_bias = params
    length = row_in.shape[0]
    first_low = low(norm_row(row_in, early_gain, early_shift))
    queries = low(low_back(matmul(first_low, query_weight) + query_bias)).reshape(length, HEADS, HEAD_DIM)
    key_rows = low(low_back(matmul(first_low, key_weight))).reshape(length, HEADS, HEAD_DIM)
    value_rows = low(low_back(matmul(first_low, value_weight) + value_bias)).reshape(length, HEADS, HEAD_DIM)
    scores = low_back(jnp.einsum('qhe,khe->hqk', queries, key_rows, precision=lax.Precision.HIGHEST) * HEAD_DIM ** (-0.5))
    places = jnp.arange(length)
    allowed = (places[None, :] <= places[:, None]) & (clips[None, :] == clips[:, None])
    scores = jnp.where(allowed[None], scores, MASKED)
    probs = low(jax.nn.softmax(scores, axis=-1))
    attention = jnp.einsum('hqk,khe->qhe', probs, value_rows, precision=lax.Precision.HIGHEST).reshape(length, D)
    attention = low(low_back(attention))
    middle = row_in + low_back(matmul(attention, output_weight) + output_bias)
    second_low = low(norm_row(middle, late_gain, late_shift))
    hidden = low_back(matmul(second_low, expand_weight) + expand_bias)
    active = low(jax.nn.gelu(hidden, approximate=True))
    return middle + low_back(matmul(active, contract_weight) + contract_bias)

def reorder(array, order):
    blocks = array.reshape(array.shape[0], N_BLK, BLK_TOK, D)
    picked = jax.vmap(lambda member, indices: member[indices])(blocks, order)
    return picked.reshape(array.shape[0], N_BLK * BLK_TOK, D)

def reference(tokens, early_gain, early_shift, query_weight, query_bias, key_weight, value_weight, value_bias, output_weight, output_bias, late_gain, late_shift, expand_weight, expand_bias, contract_weight, contract_bias, upstream, clip_ids, block_order):
    params = tuple((member.astype(jnp.float32) for member in (early_gain, early_shift, query_weight, query_bias, key_weight, value_weight, value_bias, output_weight, output_bias, late_gain, late_shift, expand_weight, expand_bias, contract_weight, contract_bias)))
    inverse = jnp.argsort(block_order, axis=1).astype(jnp.int32)
    logical_in = reorder(tokens.astype(jnp.float32), inverse)
    logical_up = reorder(upstream.astype(jnp.float32), inverse)

    def one_row(totals, items):
        row_in, cotangent, clips = items
        output, pullback = jax.vjp(lambda weights, inputs: row_forward(weights, inputs, clips), params, row_in)
        weight_grads, row_grad = pullback(cotangent)
        return (jax.tree.map(jnp.add, totals, weight_grads), (output, row_grad))
    initial = jax.tree.map(jnp.zeros_like, params)
    totals, (outputs, row_grads) = lax.scan(one_row, initial, (logical_in, logical_up, clip_ids))
    return (reorder(outputs, block_order).astype(jnp.bfloat16), reorder(row_grads, block_order).astype(jnp.bfloat16), totals[0], totals[1], totals[2], totals[3], totals[4], totals[5], totals[6], totals[7], totals[8], totals[9], totals[10], totals[11], totals[12], totals[13], totals[14])
```

```python
import functools
import itertools
import types

import jax
import jax.numpy as jnp
from jax import lax
from jax.experimental import pallas as pl
from jax.experimental.pallas import tpu as pltpu
from jax.sharding import PartitionSpec as P

HEADS = 12
EPSILON = 1e-05
MASKED = -1e30
F32 = jnp.float32
BF16 = jnp.bfloat16
MESH = pl.DeviceIdType.MESH
TOK = 128
PIECES = 2


def mm(left, right, left_dim, right_dim):
    return lax.dot_general(
        left, right, (((left_dim,), (right_dim,)), ((), ())), preferred_element_type=F32
    )


def norm_stats(value):
    centred = value - jnp.mean(value, axis=-1, keepdims=True)
    inverse = lax.rsqrt(jnp.mean(centred * centred, axis=-1, keepdims=True) + EPSILON)
    return centred * inverse, inverse


def norm_pull(grad, normed, inverse, gain):
    scaled = grad * gain
    return inverse * (
        scaled
        - jnp.mean(scaled, axis=-1, keepdims=True)
        - normed * jnp.mean(scaled * normed, axis=-1, keepdims=True)
    )


def row_of(ref):
    return ref[...].astype(F32).reshape(1, ref.shape[0])


def by_rows(start, count, step, body):
    @pl.loop(0, count // step)
    def _(index):
        body(pl.multiple_of(start + index * step, step))


def folded(value):
    rows, columns = value.shape
    return jnp.sum(value.reshape(rows // 8, 8, columns), axis=0)


def fast_scratch():
    row, d = 4 * TOK, 768
    vm = pltpu.VMEM
    return dict(
        x_all=vm((row, d), BF16),
        u_all=vm((row, d), BF16),
        wab=vm((d, 576), BF16),
        wb_tile=vm((3, d, 128), BF16),
        wo=vm((d, d), BF16),
        w1=vm((d, d), BF16),
        w2=vm((d, d), BF16),
        first=vm((row, d), BF16),
        first_t=vm((d, row), BF16),
        qh=vm((3, row, 64), BF16),
        kh=vm((3, row, 64), BF16),
        vh=vm((3, row, 64), BF16),
        kt=vm((3, 64, row), BF16),
        vt=vm((3, 64, row), BF16),
        mask=vm((row, row), F32),
        st=vm((row, row), F32),
        pf=vm((3, row, row), F32),
        pb=vm((3, row, row), BF16),
        sg=vm((row, row), BF16),
        at=vm((d, row), BF16),
        mid=vm((row, d), F32),
        second=vm((row, d), BF16),
        hid=vm((row, d), F32),
        ga=vm((row, d), F32),
        act=vm((row, d), BF16),
        gh=vm((row, d), BF16),
        part=vm((row, d), F32),
        part_out=vm((row, d), F32),
        rs_send=vm((3, 3, TOK, d), BF16),
        rs_recv=vm((3, 3, TOK, d), BF16),
        g_mid=vm((TOK, d), F32),
        gb=vm((row, d), BF16),
        gbt=vm((row, 256), BF16),
        go=vm((3, row, 64), BF16),
        gqkv=vm((row, 576), BF16),
        c_send=vm((384, d), BF16),
        c_own=vm((384, d), F32),
        c_recv=vm((3, 384, d), BF16),
        c_sum=vm((2, 384, d), BF16),
        e_buf=vm((8, 96, d), BF16),
        e_r1=vm((4, 96, d), BF16),
        e_s1=vm((4, 96, d), BF16),
        e_r2=vm((3, 96, d), BF16),
        e_s2=vm((2, 96, d), BF16),
        wa_buf=vm((8, 96, 512), BF16),
        wa_r1=vm((4, 96, 512), BF16),
        wa_s1=vm((4, 96, 512), BF16),
        wa_r2=vm((3, 96, 512), BF16),
        wa_s2=vm((2, 96, 512), BF16),
        wb_buf=vm((8, 96, 256), BF16),
        wb_r1=vm((4, 96, 256), BF16),
        wb_s1=vm((4, 96, 256), BF16),
        wb_r2=vm((3, 96, 256), BF16),
        wb_s2=vm((2, 96, 256), BF16),
        sv=vm((4, 8, d), F32),
        sv_recv=vm((3, 8, d), F32),
        local_sem=pltpu.SemaphoreType.DMA((12,)),
        send_sem=pltpu.SemaphoreType.DMA((96,)),
        recv_sem=pltpu.SemaphoreType.DMA((96,)),
    )


INPUTS = [
    "tokens",
    "early_gain",
    "early_shift",
    "query_weight",
    "query_bias",
    "key_weight",
    "value_weight",
    "value_bias",
    "output_weight",
    "output_bias",
    "late_gain",
    "late_shift",
    "expand_weight",
    "expand_bias",
    "contract_weight",
    "contract_bias",
    "upstream",
    "clip_ids",
    "block_order",
]
RESULTS = ["block_out", "token_grad", "ffc", "eg", "wag", "wbg", "svg"]


def layer_kernel(names, *refs):
    r = types.SimpleNamespace(**dict(zip(names, refs)))
    d_model = 768
    row = 4 * TOK
    dp, blk = lax.axis_index("dp"), lax.axis_index("blk")
    core, chip = blk % 2, blk // 2
    sibling, across = blk + 1 - 2 * core, (blk + 2) % 4
    y, z = dp % 2, dp // 2
    z0, z1 = z % 2, z // 2
    to_core = {"dp": dp, "blk": sibling}
    to_x = {"dp": dp, "blk": across}
    to_y = {"dp": dp + 1 - 2 * y, "blk": blk}
    to_z0 = {"dp": dp + 2 - 4 * z0, "blk": blk}
    to_z1 = {"dp": (dp + 4) % 8, "blk": blk}
    peers = (to_core, to_x, to_y, to_z0, to_z1)
    numbers = itertools.count()
    sent = []

    def remote(source, target, peer):
        number = next(numbers)
        return pltpu.make_async_remote_copy(
            src_ref=source,
            dst_ref=target,
            send_sem=r.send_sem.at[number],
            recv_sem=r.recv_sem.at[number],
            device_id=peer,
            device_id_type=MESH,
        )

    def send(source, target, peer):
        copy = remote(source, target, peer)
        copy.start()
        sent.append(copy)
        return copy

    def rows_at(ref, size, base=0):
        return lambda index: ref.at[pl.ds(pl.multiple_of(base + index * size, size), size)]

    def gather(source, place):
        over_x = send(source, place(blk), to_x)
        over_core = send(source, place(blk), to_core)
        return over_x, over_core, place

    def forward(gathering):
        over_x, over_core, place = gathering
        over_x.wait_recv()
        return send(place(across), place(across), to_core)

    half = 512 + 128 * chip
    tile_at = pl.ds(pl.multiple_of(128 * blk, 128), 128)
    half_at = pl.ds(pl.multiple_of(half, 128), 128)
    ff_at = pl.ds(pl.multiple_of(768 * blk, 128), 768)
    own_rows = pl.ds(pl.multiple_of(TOK * blk, TOK), TOK)
    local = [
        (r.tokens.at[0], r.x_all.at[own_rows]),
        (r.query_weight.at[:, tile_at], r.wab.at[:, 0:128]),
        (r.key_weight.at[:, tile_at], r.wab.at[:, 128:256]),
        (r.value_weight.at[:, tile_at], r.wab.at[:, 256:384]),
        (r.query_weight.at[:, half_at], r.wb_tile.at[0]),
        (r.key_weight.at[:, half_at], r.wb_tile.at[1]),
        (r.value_weight.at[:, half_at], r.wb_tile.at[2]),
        (r.output_weight, r.wo),
        (r.upstream.at[0], r.u_all.at[own_rows]),
        (r.contract_weight.at[ff_at], r.w2),
        (r.expand_weight.at[:, ff_at], r.w1),
    ]
    loads = []
    for number, (source, target) in enumerate(local):
        copy = pltpu.make_async_copy(source, target, r.local_sem.at[number])
        copy.start()
        loads.append(copy)

    barrier = pltpu.get_barrier_semaphore()
    for peer in peers:
        pl.semaphore_signal(barrier, inc=1, device_id=peer, device_id_type=MESH)
    pl.semaphore_wait(barrier, len(peers))

    tokens_in = gather(r.tokens.at[0], rows_at(r.x_all, TOK))
    upstream_in = gather(r.upstream.at[0], rows_at(r.u_all, TOK))

    early_gain, early_shift = row_of(r.early_gain), row_of(r.early_shift)
    late_gain, late_shift = row_of(r.late_gain), row_of(r.late_shift)

    def picked(vector, size, base, width):
        total = jnp.zeros((1, width), F32)
        for index in range(4):
            begin = base + size * index
            total = total + jnp.where(blk == index, vector[:, begin : begin + width], 0.0)
        return total

    query_bias, value_bias = row_of(r.query_bias), row_of(r.value_bias)
    bias_qkv = jnp.concatenate(
        [
            picked(query_bias, 128, 0, 128),
            jnp.zeros((1, 128), F32),
            picked(value_bias, 128, 0, 128),
            picked(query_bias, 64, 512, 64),
            jnp.zeros((1, 64), F32),
            picked(value_bias, 64, 512, 64),
        ],
        axis=1,
    )

    lane = lax.broadcasted_iota(jnp.int32, (1, TOK), 1)
    keys_of, low_of = [], []
    for index in range(4):
        place = r.block_order[0, index]
        clip = jnp.zeros((1, TOK), jnp.int32)
        for other in range(4):
            clip = clip + jnp.where(
                place == other, r.clip_ids[0:1, other * TOK : (other + 1) * TOK], 0
            )
        low_of.append((clip * row).astype(F32))
        keys_of.append((clip * row + place * TOK + lane).astype(F32))
    for key in range(4):
        column = jnp.broadcast_to(keys_of[key], (TOK, TOK)).T
        for query in range(4):
            allowed = (column <= keys_of[query]) & (column >= low_of[query])
            r.mask[key * TOK : (key + 1) * TOK, query * TOK : (query + 1) * TOK] = jnp.where(
                allowed, 0.0, MASKED
            )

    for copy in loads[1:7]:
        copy.wait()
    for index in range(3):
        tile = r.wb_tile[index].astype(F32)
        piece = jnp.where(core == 1, tile[:, 64:128], tile[:, 0:64])
        r.wab[:, 384 + 64 * index : 448 + 64 * index] = piece.astype(BF16)

    def early_norm(start):
        def body(at):
            normed, _ = norm_stats(r.x_all[pl.ds(at, 32), :].astype(F32))
            r.first[pl.ds(at, 32), :] = (normed * early_gain + early_shift).astype(BF16)

        by_rows(start, TOK, 32, body)

    def project(start):
        at = pl.ds(pl.multiple_of(start, 2 * TOK), 2 * TOK)
        out = mm(r.first[at, :], r.wab[...], 1, 0) + bias_qkv
        for head, offset, step in ((0, 0, 128), (1, 64, 128), (2, 384, 64)):
            query = out[:, offset : offset + 64]
            r.qh[head, at, :] = (query * 0.125).astype(BF16)
            r.kh[head, at, :] = out[:, offset + step : offset + step + 64].astype(BF16)
            r.vh[head, at, :] = out[:, offset + 2 * step : offset + 2 * step + 64].astype(BF16)

    loads[0].wait()
    early_norm(TOK * blk)
    tokens_in[1].wait_recv()
    early_norm(TOK * sibling)
    project(2 * TOK * chip)
    token_forward = forward(tokens_in)
    early_norm(TOK * across)
    token_forward.wait_recv()
    early_norm(TOK * ((sibling + 2) % 4))
    project(2 * TOK * (1 - chip))

    def attend(head):
        r.st[...] = mm(r.kh[head], r.qh[head], 1, 1)

        @pl.loop(0, 4)
        def _(strip):
            at = pl.ds(pl.multiple_of(strip * TOK, TOK), TOK)
            scores = r.st[:, at] + r.mask[:, at]
            powers = jnp.exp(scores - jnp.max(scores, axis=0, keepdims=True))
            probs = powers * (1.0 / jnp.sum(powers, axis=0, keepdims=True))
            r.pf[head, :, at] = probs
            r.pb[head, :, at] = probs.astype(BF16)

        r.vt[head] = r.vh[head].T
        return mm(r.vt[head], r.pb[head], 1, 0).astype(BF16)

    pair_at, third_at = rows_at(r.at, 128), rows_at(r.at, 64, 512)
    start_pair = pl.multiple_of(128 * blk, 128)
    r.at[pl.ds(start_pair, 64), :] = attend(0)
    upstream_forward = forward(upstream_in)
    r.at[pl.ds(start_pair + 64, 64), :] = attend(1)
    pair_in = gather(pair_at(blk), pair_at)
    r.at[pl.ds(pl.multiple_of(512 + 64 * blk, 64), 64), :] = attend(2)
    third_in = gather(third_at(blk), third_at)

    loads[8].wait()
    loads[9].wait()
    upstream_in[1].wait_recv()
    upstream_forward.wait_recv()

    @pl.loop(0, 3)
    def _(tile):
        at = pl.ds(pl.multiple_of(tile * 256, 256), 256)
        r.ga[:, at] = mm(r.u_all[...], r.w2[at, :], 1, 1)

    pair_forward = forward(pair_in)
    third_forward = forward(third_in)
    r.first_t[...] = r.first[...].T
    for head in range(3):
        r.kt[head] = r.kh[head].T
    loads[7].wait()
    loads[10].wait()
    pair_in[1].wait_recv()
    third_in[1].wait_recv()
    pair_forward.wait_recv()
    third_forward.wait_recv()

    output_bias = row_of(r.output_bias)

    @pl.loop(0, 2)
    def _(tile):
        at = pl.ds(pl.multiple_of(tile * 256, 256), 256)
        r.mid[at, :] = mm(r.at[:, at], r.wo[...], 0, 0)

    def late_norm(at):
        at = pl.ds(at, 32)
        middle = r.mid[at, :] + r.x_all[at, :].astype(F32) + output_bias
        r.mid[at, :] = middle
        normed, _ = norm_stats(middle)
        r.second[at, :] = (normed * late_gain + late_shift).astype(BF16)

    by_rows(0, row, 32, late_norm)

    @pl.loop(0, 3)
    def _(tile):
        at = pl.ds(pl.multiple_of(tile * 256, 256), 256)
        r.hid[:, at] = mm(r.second[...], r.w1[:, at], 1, 0)

    expand_bias = picked(row_of(r.expand_bias), 768, 0, 768)
    first_factor = 0.7978845608028654
    third_factor = 0.044715

    def gelu(at):
        at = pl.ds(at, 16)
        hidden = r.hid[at, :] + expand_bias
        square = hidden * hidden
        bent = jnp.tanh(first_factor * hidden * (1.0 + third_factor * square))
        grown = 0.5 * (1.0 + bent)
        r.act[at, :] = (hidden * grown).astype(BF16)
        slope = grown + (0.5 * first_factor) * hidden * (1.0 - bent * bent) * (
            1.0 + (3.0 * third_factor) * square
        )
        r.gh[at, :] = (r.ga[at, :] * slope).astype(BF16)

    by_rows(0, row, 16, gelu)

    far = (sibling + 2) % 4

    def scatter_start(number, part):
        copies = [None, None]
        for index, block in ((1, far), (0, sibling)):
            at = pl.ds(pl.multiple_of(block * TOK, TOK), TOK)
            r.rs_send[number, index] = part[at, :].astype(BF16)
            copies[index] = send(r.rs_send.at[number, index], r.rs_recv.at[number, index], to_core)
        return copies

    def scatter_middle(number, part, copies):
        at = pl.ds(pl.multiple_of(across * TOK, TOK), TOK)
        copies[1].wait_recv()
        r.rs_send[number, 2] = (part[at, :] + r.rs_recv[number, 1].astype(F32)).astype(BF16)
        copies.append(send(r.rs_send.at[number, 2], r.rs_recv.at[number, 2], to_x))

    def scatter_end(copies):
        copies[0].wait_recv()
        copies[2].wait_recv()

    def scattered(number, part, at, size):
        own = pl.ds(pl.multiple_of(blk * TOK + at, size), size)
        here = pl.ds(at, size)
        return (
            part[own, :]
            + r.rs_recv[number, 0, here, :].astype(F32)
            + r.rs_recv[number, 2, here, :].astype(F32)
        )

    @pl.loop(0, 3)
    def _(tile):
        at = pl.ds(pl.multiple_of(tile * 256, 256), 256)
        r.part[:, at] = mm(r.gh[...], r.w1[at, :], 1, 1)

    second_sum = scatter_start(0, r.part)

    def contract_half(which):
        at = pl.ds(pl.multiple_of(384 * which, 384), 384)
        return mm(r.act[:, at], r.u_all[...], 0, 0)

    piece = 384 // PIECES
    r.c_send[...] = contract_half(1 - y).astype(BF16)
    c_y = [
        send(r.c_send.at[pl.ds(p * piece, piece)], r.c_recv.at[0, pl.ds(p * piece, piece)], to_y)
        for p in range(PIECES)
    ]
    scatter_middle(0, r.part, second_sum)
    r.c_own[...] = contract_half(y)

    order = (
        (1 - z0) + 2 * (1 - z1),
        (1 - z0) + 2 * z1,
        z0 + 2 * (1 - z1),
        z0 + 2 * z1,
    )

    def y_start(buf, first_recv):
        return [
            send(buf.at[2 * order[index] + 1 - y], first_recv.at[index], to_y)
            for index in range(4)
        ]

    def added(target, left, right):
        rows = target.shape[0]

        @pl.loop(0, rows // 32)
        def _(index):
            at = pl.ds(pl.multiple_of(index * 32, 32), 32)
            target[at, :] = (left[at, :].astype(F32) + right[at, :].astype(F32)).astype(target.dtype)

    def y_end(copies, buf, first_recv, first_sum, index):
        copies[index].wait_recv()
        added(first_sum.at[index], buf.at[2 * order[index] + y], first_recv.at[index])

    def z0_start(first_sum, second_recv):
        return [send(first_sum.at[index], second_recv.at[index], to_z0) for index in range(2)]

    def z1_start(copies, first_sum, second_recv, second_sums):
        copies[0].wait_recv()
        added(second_sums.at[0], first_sum.at[2], second_recv.at[0])
        copy = send(second_sums.at[0], second_recv.at[2], to_z1)
        copies[1].wait_recv()
        added(second_sums.at[1], first_sum.at[3], second_recv.at[1])
        return copy

    def z1_end(copy, second_sums, second_recv, target):
        copy.wait_recv()
        added(target, second_sums.at[1], second_recv.at[2])

    for which in range(2):
        block = mm(r.second[:, 384 * which : 384 * (which + 1)], r.gh[...], 0, 0)
        r.e_buf[4 * which : 4 * which + 4] = block.astype(BF16).reshape(4, 96, d_model)
    e_y = y_start(r.e_buf, r.e_r1)

    @pl.loop(0, 3)
    def _(tile):
        at = pl.ds(pl.multiple_of(tile * 256, 256), 256)
        r.part_out[:, at] = mm(r.act[...], r.w2[:, at], 1, 0)

    out_sum = scatter_start(1, r.part_out)

    scatter_end(second_sum)
    own_start = blk * TOK
    r.sv[0] = jnp.zeros((8, d_model), F32)

    def late_pull(index, carry):
        gain_sum, shift_sum, output_sum, contract_sum = carry
        at = pl.multiple_of(index * 32, 32)
        own = pl.ds(pl.multiple_of(own_start + at, 32), 32)
        grad = scattered(0, r.part, at, 32)
        normed, inverse = norm_stats(r.mid[own, :])
        upstream = r.u_all[own, :].astype(F32)
        middle = upstream + norm_pull(grad, normed, inverse, late_gain)
        r.g_mid[pl.ds(at, 32), :] = middle
        low = middle.astype(BF16)
        r.gb[own, :] = low
        return (
            gain_sum + folded(grad * normed),
            shift_sum + folded(grad),
            output_sum + folded(low.astype(F32)),
            contract_sum + folded(upstream),
        )

    nothing = jnp.zeros((8, d_model), F32)
    sums = lax.fori_loop(0, TOK // 32, late_pull, (nothing,) * 4)
    branch_at = rows_at(r.gb, TOK)
    branch_in = gather(branch_at(blk), branch_at)
    for index, value in zip((3, 4, 2, 5), sums):
        r.sv[0, index : index + 1, :] = jnp.sum(value, axis=0, keepdims=True)

    def expand_sum(index, carry):
        at = pl.ds(pl.multiple_of(index * 32, 32), 32)
        return carry + folded(r.gh[at, :].astype(F32))

    r.sv[0, 6:7, :] = jnp.sum(
        lax.fori_loop(0, row // 32, expand_sum, nothing), axis=0, keepdims=True
    )
    branch_forward = forward(branch_in)
    branch_in[1].wait_recv()
    branch_forward.wait_recv()

    pair = pl.ds(start_pair, 128)
    pair_grad = mm(r.gb[...], r.wo[pair, :], 1, 1)
    r.go[0] = pair_grad[:, 0:64].astype(BF16)
    r.go[1] = pair_grad[:, 64:128].astype(BF16)
    third = pl.ds(pl.multiple_of(512 + 64 * blk, 64), 64)
    r.go[2] = mm(r.gb[...], r.wo[third, :], 1, 1).astype(BF16)

    def attend_back(head, offset, step):
        r.st[...] = mm(r.vh[head], r.go[head], 1, 1)

        @pl.loop(0, 4)
        def _(strip):
            at = pl.ds(pl.multiple_of(strip * TOK, TOK), TOK)
            probs, grad = r.pf[head, :, at], r.st[:, at]
            delta = jnp.sum(probs * grad, axis=0, keepdims=True)
            r.sg[:, at] = (probs * (grad - delta)).astype(BF16)

        query = mm(r.kt[head], r.sg[...], 1, 0) * 0.125
        r.gqkv[:, offset : offset + 64] = query.T.astype(BF16)
        r.gqkv[:, offset + step : offset + step + 64] = mm(
            r.sg[...], r.qh[head], 1, 0
        ).astype(BF16)
        r.gqkv[:, offset + 2 * step : offset + 2 * step + 64] = mm(
            r.pb[head], r.go[head], 1, 0
        ).astype(BF16)

    attend_back(0, 0, 128)
    attend_back(1, 64, 128)

    r.gbt[:, 0:128] = r.gb[:, tile_at]
    r.gbt[:, 128:256] = r.gb[:, half_at]
    for which in range(2):
        at = slice(384 * which, 384 * (which + 1))
        block = mm(r.first_t[at, :], r.gqkv[:, 0:384], 1, 0)
        blocks = slice(4 * which, 4 * which + 4)
        r.wa_buf[blocks, :, 0:384] = block.astype(BF16).reshape(4, 96, 384)
        block = mm(r.at[at, :], r.gbt[...], 1, 0)
        r.wa_buf[blocks, :, 384:512] = block[:, 0:128].astype(BF16).reshape(4, 96, 128)
        chosen = jnp.where(core == 1, block[:, 192:256], block[:, 128:192])
        r.wb_buf[blocks, :, 192:256] = chosen.astype(BF16).reshape(4, 96, 64)
    wa_y = y_start(r.wa_buf, r.wa_r1)

    root0, root1 = blk % 2, blk // 2
    keeps0 = z0 == root0
    keeps1 = z1 == root1
    for p in range(PIECES):
        c_y[p].wait_recv()
        at = pl.ds(p * piece, piece)
        added(r.c_sum.at[0, at], r.c_own.at[at], r.c_recv.at[0, at])
    c_z0 = [
        remote(r.c_sum.at[0, pl.ds(p * piece, piece)], r.c_recv.at[1, pl.ds(p * piece, piece)], to_z0)
        for p in range(PIECES)
    ]
    c_z1 = [
        remote(r.c_sum.at[1, pl.ds(p * piece, piece)], r.c_recv.at[2, pl.ds(p * piece, piece)], to_z1)
        for p in range(PIECES)
    ]

    @pl.when(jnp.logical_not(keeps0))
    def _():
        for copy in c_z0:
            copy.start()

    attend_back(2, 384, 64)
    for which in range(2):
        at = slice(384 * which, 384 * (which + 1))
        block = mm(r.first_t[at, :], r.gqkv[:, 384:576], 1, 0)
        r.wb_buf[4 * which : 4 * which + 4, :, 0:192] = block.astype(BF16).reshape(4, 96, 192)
    wb_y = y_start(r.wb_buf, r.wb_r1)

    @pl.loop(0, 3)
    def _(tile):
        at = pl.ds(pl.multiple_of(tile * 256, 256), 256)
        r.part[:, at] = mm(r.gqkv[...], r.wab[at, :], 1, 1)

    first_sum = scatter_start(2, r.part)

    def qkv_sum(index, carry):
        at = pl.ds(pl.multiple_of(index * 32, 32), 32)
        return carry + folded(r.gqkv[at, :].astype(F32))

    total = jnp.sum(
        lax.fori_loop(0, row // 32, qkv_sum, jnp.zeros((8, 576), F32)), axis=0, keepdims=True
    )
    r.sv[0, 7:8, 0:384] = total[:, 0:384]
    r.sv[0, 7:8, 512:704] = total[:, 384:576]
    scatter_middle(2, r.part, first_sum)

    y_end(e_y, r.e_buf, r.e_r1, r.e_s1, 0)
    y_end(e_y, r.e_buf, r.e_r1, r.e_s1, 1)
    e_z0 = z0_start(r.e_s1, r.e_r2)

    @pl.when(keeps0)
    def _():
        for p in range(PIECES):
            c_z0[p].wait_recv()
            at = pl.ds(p * piece, piece)
            added(r.c_sum.at[1, at], r.c_sum.at[0, at], r.c_recv.at[1, at])

    @pl.when(jnp.logical_and(keeps0, jnp.logical_not(keeps1)))
    def _():
        for copy in c_z1:
            copy.start()

    scatter_middle(1, r.part_out, out_sum)
    y_end(e_y, r.e_buf, r.e_r1, r.e_s1, 2)
    y_end(e_y, r.e_buf, r.e_r1, r.e_s1, 3)

    scatter_end(first_sum)

    def early_pull(index, carry):
        gain_sum, shift_sum = carry
        at = pl.multiple_of(index * 32, 32)
        own = pl.ds(pl.multiple_of(own_start + at, 32), 32)
        here = pl.ds(at, 32)
        grad = scattered(2, r.part, at, 32)
        normed, inverse = norm_stats(r.x_all[own, :].astype(F32))
        pulled = norm_pull(grad, normed, inverse, early_gain)
        r.token_grad[here, :] = (r.g_mid[here, :] + pulled).astype(BF16)
        return gain_sum + folded(grad * normed), shift_sum + folded(grad)

    sums = lax.fori_loop(0, TOK // 32, early_pull, (nothing,) * 2)
    for index, value in enumerate(sums):
        r.sv[0, index : index + 1, :] = jnp.sum(value, axis=0, keepdims=True)
    v_y = send(r.sv.at[0], r.sv_recv.at[0], to_y)

    e_z1 = z1_start(e_z0, r.e_s1, r.e_r2, r.e_s2)
    for index in range(4):
        y_end(wa_y, r.wa_buf, r.wa_r1, r.wa_s1, index)
        if index == 1:
            wa_z0 = z0_start(r.wa_s1, r.wa_r2)

    scatter_end(out_sum)
    contract_bias = row_of(r.contract_bias)

    @pl.loop(0, TOK // 32)
    def _(index):
        at = pl.multiple_of(index * 32, 32)
        own = pl.ds(pl.multiple_of(own_start + at, 32), 32)
        value = scattered(1, r.part_out, at, 32) + r.mid[own, :] + contract_bias
        r.block_out[pl.ds(at, 32), :] = value.astype(BF16)

    v_y.wait_recv()
    r.sv[1] = r.sv[0] + r.sv_recv[0]
    v_z0 = send(r.sv.at[1], r.sv_recv.at[1], to_z0)
    for index in range(4):
        y_end(wb_y, r.wb_buf, r.wb_r1, r.wb_s1, index)
        if index == 1:
            wb_z0 = z0_start(r.wb_s1, r.wb_r2)

    is_root = z == blk
    is_across = z == across
    near_root = z == sibling
    c_x = [remote(r.ffc.at[pl.ds(p * piece, piece)], r.ffc.at[pl.ds(p * piece, piece)], to_x) for p in range(PIECES)]
    c_core = [remote(r.ffc.at[pl.ds(p * piece, piece)], r.ffc.at[pl.ds(p * piece, piece)], to_core) for p in range(PIECES)]

    @pl.when(is_root)
    def _():
        for p in range(PIECES):
            c_z1[p].wait_recv()
            at = pl.ds(p * piece, piece)
            added(r.ffc.at[at], r.c_sum.at[1, at], r.c_recv.at[2, at])
            c_x[p].start()
            c_core[p].start()

    e_at = lambda index: r.eg.at[index]
    z1_end(e_z1, r.e_s2, r.e_r2, r.eg.at[blk])
    e_in = gather(e_at(blk), e_at)

    v_z0.wait_recv()
    r.sv[2] = r.sv[1] + r.sv_recv[1]
    v_z1 = send(r.sv.at[2], r.sv_recv.at[2], to_z1)

    wa_z1 = z1_start(wa_z0, r.wa_s1, r.wa_r2, r.wa_s2)
    wb_z1 = z1_start(wb_z0, r.wb_s1, r.wb_r2, r.wb_s2)

    @pl.when(is_across)
    def _():
        for p in range(PIECES):
            c_x[p].wait_recv()
            c_core[p].start()

    e_forward = forward(e_in)

    v_z1.wait_recv()
    r.svg[blk] = r.sv[2] + r.sv_recv[2]
    v_at = lambda index: r.svg.at[index]
    v_in = gather(v_at(blk), v_at)

    wa_at = lambda index: r.wag.at[index]
    z1_end(wa_z1, r.wa_s2, r.wa_r2, r.wag.at[blk])
    wa_in = gather(wa_at(blk), wa_at)
    wb_at = lambda index: r.wbg.at[index]
    z1_end(wb_z1, r.wb_s2, r.wb_r2, r.wbg.at[blk])
    wb_in = gather(wb_at(blk), wb_at)

    v_forward = forward(v_in)
    wa_forward = forward(wa_in)
    wb_forward = forward(wb_in)

    @pl.when(jnp.logical_not(jnp.logical_or(is_root, is_across)))
    def _():
        for p in range(PIECES):
            c_core[p].wait_recv()

    for gathering in (e_in, v_in, wa_in, wb_in):
        gathering[1].wait_recv()
    for copy in (e_forward, v_forward, wa_forward, wb_forward):
        copy.wait_recv()

    for copy in sent:
        copy.wait_send()

    @pl.when(jnp.logical_not(keeps0))
    def _():
        for copy in c_z0:
            copy.wait_send()

    @pl.when(jnp.logical_and(keeps0, jnp.logical_not(keeps1)))
    def _():
        for copy in c_z1:
            copy.wait_send()

    @pl.when(is_root)
    def _():
        for copy in c_x:
            copy.wait_send()

    @pl.when(jnp.logical_or(is_root, is_across))
    def _():
        for copy in c_core:
            copy.wait_send()


def write_kernel(block_in, grad_in, ffc, eg, wag, wbg, svg, *outs):
    (block_out, token_grad, gain_early, shift_early, query_grad, bias_query, key_grad, value_grad) = outs[:8]
    (bias_value, output_grad, bias_output, gain_late, shift_late, expand_grad, bias_expand) = outs[8:15]
    contract_grad, bias_contract = outs[15:]
    dp = lax.axis_index("dp")
    block_out[0] = block_in[...]
    token_grad[0] = grad_in[...]
    for index in range(4):
        wide = slice(128 * index, 128 * (index + 1))
        narrow = slice(512 + 64 * index, 576 + 64 * index)
        for number, target in enumerate((query_grad, key_grad, value_grad, output_grad)):
            target[:, wide] = wag[index, :, 128 * number : 128 * (number + 1)].astype(F32)
            target[:, narrow] = wbg[index, :, 64 * number : 64 * (number + 1)].astype(F32)
        expand_grad[:, 768 * index : 768 * (index + 1)] = eg[index].astype(F32)
    contract_grad[...] = ffc[...].astype(F32)
    summed = svg[0] + svg[1] + svg[2] + svg[3]
    query_row = jnp.concatenate(
        [svg[i, 7:8, 0:128] for i in range(4)] + [svg[i, 7:8, 512:576] for i in range(4)], axis=1
    )
    value_row = jnp.concatenate(
        [svg[i, 7:8, 256:384] for i in range(4)] + [svg[i, 7:8, 640:704] for i in range(4)], axis=1
    )
    rows = jnp.concatenate([summed[0:6], query_row, value_row], axis=0)
    turned = pltpu.roll(rows, 768 - 96 * dp, 1)
    targets = (gain_early, shift_early, bias_output, gain_late, shift_late, bias_contract)
    for number, target in enumerate(targets + (bias_query, bias_value)):
        target[...] = turned[number, 0:96]
    hidden = jnp.zeros((8, 768), F32)
    for index in range(4):
        hidden = hidden + jnp.where(dp // 2 == index, svg[index], 0.0)
    bias_expand[...] = pltpu.roll(hidden, 768 - 384 * (dp % 2), 1)[6, 0:384]


def fast_local(*arguments):
    scratch = fast_scratch()
    vmem = pl.BlockSpec(memory_space=pltpu.VMEM)
    away = pl.BlockSpec(memory_space=pl.ANY)
    large = [
        "tokens",
        "query_weight",
        "key_weight",
        "value_weight",
        "output_weight",
        "expand_weight",
        "contract_weight",
        "upstream",
    ]
    specs = [away if name in large else vmem for name in INPUTS]
    specs[-1] = pl.BlockSpec(memory_space=pltpu.SMEM)
    shape = jax.ShapeDtypeStruct
    results = (
        shape((TOK, 768), BF16),
        shape((TOK, 768), BF16),
        shape((384, 768), BF16),
        shape((4, 96, 768), BF16),
        shape((4, 96, 512), BF16),
        shape((4, 96, 256), BF16),
        shape((4, 8, 768), F32),
    )
    names = INPUTS + RESULTS + list(scratch)
    moved = pl.pallas_call(
        functools.partial(layer_kernel, names),
        name="layer",
        out_shape=results,
        in_specs=specs,
        out_specs=(vmem,) * len(results),
        scratch_shapes=list(scratch.values()),
        compiler_params=pltpu.CompilerParams(
            collective_id=0, has_side_effects=True, vmem_limit_bytes=56 << 20
        ),
    )(*arguments)
    outs = (
        [shape((1, TOK, 768), BF16)] * 2
        + [shape((96,), F32)] * 2
        + [shape((96, 768), F32), shape((96,), F32), shape((96, 768), F32), shape((96, 768), F32)]
        + [shape((96,), F32), shape((96, 768), F32)]
        + [shape((96,), F32)] * 3
        + [shape((96, 3072), F32), shape((384,), F32), shape((384, 768), F32), shape((96,), F32)]
    )
    return pl.pallas_call(
        write_kernel,
        name="write",
        out_shape=tuple(outs),
        in_specs=[vmem] * 7,
        out_specs=(vmem,) * len(outs),
        compiler_params=pltpu.CompilerParams(vmem_limit_bytes=32 << 20),
    )(*moved)


def passed_along(value, axis, steps):
    count = lax.axis_size(axis)
    pairs = [(source, (source + steps) % count) for source in range(count)]
    return lax.ppermute(value, axis, pairs)


def layer_norm(inputs, gain, shift):
    average = jnp.mean(inputs, axis=-1, keepdims=True)
    centred = inputs - average
    inverse = lax.rsqrt(jnp.mean(centred * centred, axis=-1, keepdims=True) + EPSILON)
    normed = centred * inverse
    return (normed * gain + shift, normed, inverse)


def norm_back(grad_out, normed, inverse, gain):
    scaled = grad_out * gain
    inner = (
        scaled
        - jnp.mean(scaled, axis=-1, keepdims=True)
        - normed * jnp.mean(scaled * normed, axis=-1, keepdims=True)
    )
    return (
        inverse * inner,
        jnp.sum(grad_out * normed, axis=(0, 1)),
        jnp.sum(grad_out, axis=(0, 1)),
    )


def project(inputs, weight):
    return jnp.einsum("rtd,de->rte", inputs, weight, preferred_element_type=jnp.float32)


def project_back(grad_rows, weight):
    return jnp.einsum("rte,de->rtd", grad_rows, weight, preferred_element_type=jnp.float32)


def weight_grad(inputs, grad_rows):
    return jnp.einsum("rtd,rte->de", inputs, grad_rows, preferred_element_type=jnp.float32)


def column_sum(grad_rows):
    return jnp.sum(grad_rows.astype(jnp.float32), axis=(0, 1))


def general_local(
    tokens,
    early_gain,
    early_shift,
    query_weight,
    query_bias,
    key_weight,
    value_weight,
    value_bias,
    output_weight,
    output_bias,
    late_gain,
    late_shift,
    expand_weight,
    expand_bias,
    contract_weight,
    contract_bias,
    upstream,
    clip_ids,
    block_order,
):
    row_count, block_len, features = tokens.shape
    head_count = HEADS
    head_size = features // head_count
    scale_factor = float(head_size) ** (-0.5)
    my_index = lax.axis_index("blk")
    group_size = lax.axis_size("blk")

    def positions(begin, length):
        stored = begin + jnp.arange(length, dtype=jnp.int32)
        logical = (
            jnp.take(block_order, stored // block_len, axis=1) * block_len + stored % block_len
        )
        return (logical, jnp.take_along_axis(clip_ids, logical, axis=1))

    query_pos, query_clip = positions(my_index * block_len, block_len)

    def visible(begin, length):
        key_pos, key_clip = positions(begin, length)
        allowed = (key_pos[:, None, :] <= query_pos[:, :, None]) & (
            key_clip[:, None, :] == query_clip[:, :, None]
        )
        return allowed[:, None]

    def split_heads(array):
        return array.reshape(row_count, array.shape[1], head_count, head_size)

    inputs = tokens.astype(jnp.float32)
    first_full, first_normed, first_inverse = layer_norm(
        inputs, early_gain.astype(jnp.float32), early_shift.astype(jnp.float32)
    )
    first_low = first_full.astype(jnp.bfloat16)
    queries = (project(first_low, query_weight) + query_bias.astype(jnp.float32)).astype(
        jnp.bfloat16
    )
    key_rows = project(first_low, key_weight).astype(jnp.bfloat16)
    value_rows = (project(first_low, value_weight) + value_bias.astype(jnp.float32)).astype(
        jnp.bfloat16
    )
    query_heads = split_heads(queries)

    def scores_of(key_block):
        return (
            jnp.einsum(
                "rqhe,rkhe->rhqk",
                query_heads,
                split_heads(key_block),
                preferred_element_type=jnp.float32,
            )
            * scale_factor
        )

    def absorb(carry, key_block, value_block, begin):
        allowed = visible(begin, key_block.shape[1])
        maximum, denominator, numerator = carry
        scores = jnp.where(allowed, scores_of(key_block), MASKED)
        new_max = jnp.maximum(maximum, jnp.max(scores, axis=-1))
        weights = jnp.where(allowed, jnp.exp(scores - new_max[..., None]), 0.0)
        factor = jnp.exp(maximum - new_max)
        update = jnp.einsum(
            "rhqk,rkhe->rqhe",
            weights.astype(jnp.bfloat16),
            split_heads(value_block),
            preferred_element_type=jnp.float32,
        )
        numerator = numerator * jnp.transpose(factor, (0, 2, 1))[..., None] + update
        return (new_max, denominator * factor + jnp.sum(weights, axis=-1), numerator)

    start_state = (
        jnp.full((row_count, head_count, block_len), MASKED, jnp.float32),
        jnp.zeros((row_count, head_count, block_len), jnp.float32),
        jnp.zeros((row_count, block_len, head_count, head_size), jnp.float32),
    )
    key_piece = lax.all_gather(key_rows, "blk", axis=1, tiled=True)
    value_piece = lax.all_gather(value_rows, "blk", axis=1, tiled=True)
    length = key_piece.shape[1]
    stride = min(length, block_len)

    def one_block(number, running):
        offset = number * stride
        return absorb(
            running,
            lax.dynamic_slice_in_dim(key_piece, offset, stride, 1),
            lax.dynamic_slice_in_dim(value_piece, offset, stride, 1),
            offset,
        )

    maximum, denominator, numerator = lax.fori_loop(0, length // stride, one_block, start_state)
    log_total = maximum + jnp.log(denominator)
    attention = numerator / jnp.transpose(denominator, (0, 2, 1))[..., None]
    attention_low = attention.reshape(row_count, block_len, features).astype(jnp.bfloat16)
    middle = inputs + project(attention_low, output_weight) + output_bias.astype(jnp.float32)
    second_full, second_normed, second_inverse = layer_norm(
        middle, late_gain.astype(jnp.float32), late_shift.astype(jnp.float32)
    )
    second_low = second_full.astype(jnp.bfloat16)
    hidden = project(second_low, expand_weight) + expand_bias.astype(jnp.float32)
    active_full, gelu_pull = jax.vjp(
        lambda values_in: jax.nn.gelu(values_in, approximate=True), hidden
    )
    active_low = active_full.astype(jnp.bfloat16)
    block_out = (
        middle + project(active_low, contract_weight) + contract_bias.astype(jnp.float32)
    ).astype(jnp.bfloat16)
    grad_out = upstream.astype(jnp.float32)
    contract_g = weight_grad(active_low, upstream)
    contract_b = column_sum(upstream)
    hidden_low = gelu_pull(project_back(upstream, contract_weight))[0].astype(jnp.bfloat16)
    expand_g = weight_grad(second_low, hidden_low)
    expand_b = column_sum(hidden_low)
    norm_grad, late_gain_g, late_shift_g = norm_back(
        project_back(hidden_low, expand_weight),
        second_normed,
        second_inverse,
        late_gain.astype(jnp.float32),
    )
    middle_grad = grad_out + norm_grad
    branch_low = middle_grad.astype(jnp.bfloat16)
    output_g = weight_grad(attention_low, branch_low)
    output_b = column_sum(branch_low)
    grad_heads = split_heads(project_back(branch_low, output_weight).astype(jnp.bfloat16))
    delta = jnp.transpose(jnp.sum(grad_heads.astype(jnp.float32) * attention, axis=-1), (0, 2, 1))

    def turn_step(number, carried):
        key_block, value_block, key_acc, value_acc, query_acc = carried
        source = (my_index - number) % group_size
        allowed = visible(source * block_len, block_len)
        use_key, use_value = (key_block, value_block)
        key_sum = key_acc
        value_sum = value_acc
        query_sum = query_acc
        probs = jnp.where(allowed, jnp.exp(scores_of(use_key) - log_total[..., None]), 0.0)
        value_sum = value_sum + jnp.einsum(
            "rhqk,rqhe->rkhe",
            probs.astype(jnp.bfloat16),
            grad_heads,
            preferred_element_type=jnp.float32,
        ).reshape(row_count, block_len, features)
        prob_grad = jnp.einsum(
            "rqhe,rkhe->rhqk",
            grad_heads,
            split_heads(use_value),
            preferred_element_type=jnp.float32,
        )
        score_grad = (probs * (prob_grad - delta[..., None])).astype(jnp.bfloat16)
        query_sum = (
            query_sum
            + jnp.einsum(
                "rhqk,rkhe->rqhe",
                score_grad,
                split_heads(use_key),
                preferred_element_type=jnp.float32,
            )
            * scale_factor
        )
        key_sum = key_sum + (
            jnp.einsum(
                "rhqk,rqhe->rkhe", score_grad, query_heads, preferred_element_type=jnp.float32
            )
            * scale_factor
        ).reshape(row_count, block_len, features)
        key_acc = key_sum
        value_acc = value_sum
        key_block, value_block = passed_along((key_block, value_block), "blk", 1)
        key_acc, value_acc = (
            passed_along(key_acc.astype(jnp.bfloat16), "blk", 1).astype(key_acc.dtype),
            passed_along(value_acc.astype(jnp.bfloat16), "blk", 1).astype(value_acc.dtype),
        )
        return (key_block, value_block, key_acc, value_acc, query_sum)

    zero_rows = jnp.zeros((row_count, block_len, features), jnp.float32)
    carried = (
        key_rows,
        value_rows,
        zero_rows,
        zero_rows,
        jnp.zeros((row_count, block_len, head_count, head_size), jnp.float32),
    )
    carried = lax.fori_loop(0, group_size, turn_step, carried)
    query_low = carried[4].reshape(row_count, block_len, features).astype(jnp.bfloat16)
    key_low = carried[2].astype(jnp.bfloat16)
    value_low = carried[3].astype(jnp.bfloat16)
    query_g = weight_grad(first_low, query_low)
    key_g = weight_grad(first_low, key_low)
    value_g = weight_grad(first_low, value_low)
    query_b = column_sum(query_low)
    value_b = column_sum(value_low)
    first_grad = (
        project_back(query_low, query_weight)
        + project_back(key_low, key_weight)
        + project_back(value_low, value_weight)
    )
    input_grad, early_gain_g, early_shift_g = norm_back(
        first_grad, first_normed, first_inverse, early_gain.astype(jnp.float32)
    )
    token_grad = (middle_grad + input_grad).astype(jnp.bfloat16)
    local_grads = (
        early_gain_g,
        early_shift_g,
        query_g,
        query_b,
        key_g,
        value_g,
        value_b,
        output_g,
        output_b,
        late_gain_g,
        late_shift_g,
        expand_g,
        expand_b,
        contract_g,
        contract_b,
    )
    owners = lax.axis_size("dp")
    laid_out = jnp.concatenate([member.reshape(owners, -1) for member in local_grads], axis=1)
    shares = lax.psum_scatter(laid_out.astype(jnp.bfloat16), "dp", scatter_dimension=0, tiled=True)
    summed = lax.psum(shares, "blk").astype(jnp.float32)
    pieces = []
    offset = 0
    for member in local_grads:
        width = member.size // owners
        own_shape = (member.shape[0] // owners,) + member.shape[1:]
        pieces.append(summed[0, offset : offset + width].reshape(own_shape))
        offset = offset + width
    return (block_out, token_grad) + tuple(pieces)


def solution(mesh):
    placed = (
        P("dp", "blk", None),
        P(),
        P(),
        P(),
        P(),
        P(),
        P(),
        P(),
        P(),
        P(),
        P(),
        P(),
        P(),
        P(),
        P(),
        P(),
        P("dp", "blk", None),
        P("dp", None),
        P("dp", None),
    )
    narrow = mesh.shape["dp"] == 8 and mesh.shape["blk"] == 4
    return jax.shard_map(
        fast_local if narrow else general_local,
        mesh=mesh,
        in_specs=placed,
        out_specs=(
            P("dp", "blk", None),
            P("dp", "blk", None),
            P("dp"),
            P("dp"),
            P("dp", None),
            P("dp"),
            P("dp", None),
            P("dp", None),
            P("dp"),
            P("dp", None),
            P("dp"),
            P("dp"),
            P("dp"),
            P("dp", None),
            P("dp"),
            P("dp", None),
            P("dp"),
        ),
        check_vma=False,
    )
```

```python
import functools
import itertools
import types

import jax
import jax.numpy as jnp
from jax import lax
from jax.experimental import pallas as pl
from jax.experimental.pallas import tpu as pltpu
from jax.sharding import PartitionSpec as P

HEADS = 12
EPSILON = 1e-05
MASKED = -1e30
F32 = jnp.float32
BF16 = jnp.bfloat16
MESH = pl.DeviceIdType.MESH
TOK = 128
PIECES = 2


def mm(left, right, left_dim, right_dim):
    return lax.dot_general(
        left, right, (((left_dim,), (right_dim,)), ((), ())), preferred_element_type=F32
    )


def norm_stats(value):
    centred = value - jnp.mean(value, axis=-1, keepdims=True)
    inverse = lax.rsqrt(jnp.mean(centred * centred, axis=-1, keepdims=True) + EPSILON)
    return centred * inverse, inverse


def norm_pull(grad, normed, inverse, gain):
    scaled = grad * gain
    return inverse * (
        scaled
        - jnp.mean(scaled, axis=-1, keepdims=True)
        - normed * jnp.mean(scaled * normed, axis=-1, keepdims=True)
    )


def row_of(ref):
    return ref[...].astype(F32).reshape(1, ref.shape[0])


def by_rows(start, count, step, body, unroll=2):
    @pl.loop(0, count // step, unroll=unroll)
    def _(index):
        body(pl.multiple_of(start + index * step, step))


def folded(value):
    rows, columns = value.shape
    return jnp.sum(value.reshape(rows // 8, 8, columns), axis=0)


def halving_scratch(name, width):
    sizes = {"_buf": 8, "_r1": 4, "_s1": 4, "_r2": 3, "_s2": 2}
    return {name + key: pltpu.VMEM((size, 96, width), BF16) for key, size in sizes.items()}


def fast_scratch():
    row, d = 4 * TOK, 768
    vm = pltpu.VMEM
    return dict(
        x_all=vm((row, d), BF16),
        u_all=vm((row, d), BF16),
        wab=vm((d, 576), BF16),
        wb_tile=vm((3, d, 128), BF16),
        wo=vm((d, d), BF16),
        w1=vm((d, d), BF16),
        w2=vm((d, d), BF16),
        first=vm((row, d), BF16),
        normed=vm((row, d), F32),
        first_t=vm((d, row), BF16),
        qh=vm((3, row, 64), BF16),
        kh=vm((3, row, 64), BF16),
        vh=vm((3, row, 64), BF16),
        kt=vm((3, 64, row), BF16),
        vt=vm((3, 64, row), BF16),
        mask=vm((row, row), F32),
        st=vm((row, row), F32),
        pf=vm((3, row, row), F32),
        pb=vm((3, row, row), BF16),
        sg=vm((row, row), BF16),
        at=vm((d, row), BF16),
        mid=vm((row, d), F32),
        second=vm((row, d), BF16),
        hid=vm((row, d), F32),
        ga=vm((row, d), F32),
        act=vm((row, d), BF16),
        gh=vm((row, d), BF16),
        part=vm((row, d), F32),
        part_out=vm((row, d), F32),
        rs_send=vm((3, 3, TOK, d), BF16),
        rs_recv=vm((3, 3, TOK, d), BF16),
        g_mid=vm((TOK, d), F32),
        gb=vm((row, d), BF16),
        gbt=vm((row, 256), BF16),
        go=vm((3, row, 64), BF16),
        go_pair=vm((row, 128), BF16),
        go_send=vm((TOK, 512), BF16),
        third_send=vm((4, TOK, 64), BF16),
        gqkv=vm((row, 576), BF16),
        c_send=vm((384, d), BF16),
        c_own=vm((384, d), F32),
        c_recv=vm((3, 384, d), BF16),
        c_sum=vm((2, 384, d), BF16),
        **halving_scratch("e1", 384),
        **halving_scratch("e2", 384),
        **halving_scratch("wa", 512),
        **halving_scratch("wb", 256),
        sv=vm((4, 8, d), F32),
        sv_recv=vm((3, 8, d), F32),
        **{"v_" + name: vm((4 * d if name == "expand_bias" else d,), BF16) for name in VECTORS},
        v_clip_ids=vm((1, row), jnp.int32),
        v_block_order=pltpu.SMEM((1, 4), jnp.int32),
        local_sem=pltpu.SemaphoreType.DMA((24,)),
        send_sem=pltpu.SemaphoreType.DMA((128,)),
        recv_sem=pltpu.SemaphoreType.DMA((128,)),
    )


INPUTS = [
    "tokens",
    "early_gain",
    "early_shift",
    "query_weight",
    "query_bias",
    "key_weight",
    "value_weight",
    "value_bias",
    "output_weight",
    "output_bias",
    "late_gain",
    "late_shift",
    "expand_weight",
    "expand_bias",
    "contract_weight",
    "contract_bias",
    "upstream",
    "clip_ids",
    "block_order",
]
VECTORS = [
    "early_gain",
    "early_shift",
    "query_bias",
    "value_bias",
    "output_bias",
    "late_gain",
    "late_shift",
    "expand_bias",
    "contract_bias",
]
RESULTS = ["block_out", "token_grad", "ffc", "e1g", "e2g", "wag", "wbg", "svg"]


def layer_kernel(names, *refs):
    r = types.SimpleNamespace(**dict(zip(names, refs)))
    d_model = 768
    row = 4 * TOK
    dp, blk = lax.axis_index("dp"), lax.axis_index("blk")
    core, chip = blk % 2, blk // 2
    sibling, across = blk + 1 - 2 * core, (blk + 2) % 4
    y, z = dp % 2, dp // 2
    z0, z1 = z % 2, z // 2
    to_core = {"dp": dp, "blk": sibling}
    to_x = {"dp": dp, "blk": across}
    to_y = {"dp": dp + 1 - 2 * y, "blk": blk}
    to_z0 = {"dp": dp + 2 - 4 * z0, "blk": blk}
    to_z1 = {"dp": (dp + 4) % 8, "blk": blk}
    far = (sibling + 2) % 4
    to_far = {"dp": dp, "blk": far}
    peers = (to_core, to_x, to_far, to_y, to_z0, to_z1)
    numbers = itertools.count()
    sent = []

    def remote(source, target, peer):
        number = next(numbers)
        return pltpu.make_async_remote_copy(
            src_ref=source,
            dst_ref=target,
            send_sem=r.send_sem.at[number],
            recv_sem=r.recv_sem.at[number],
            device_id=peer,
            device_id_type=MESH,
        )

    def send(source, target, peer):
        copy = remote(source, target, peer)
        copy.start()
        sent.append(copy)
        return copy

    def rows_at(ref, size, base=0):
        return lambda index: ref.at[pl.ds(pl.multiple_of(base + index * size, size), size)]

    def gather(source, place):
        over_x = send(source, place(blk), to_x)
        over_core = send(source, place(blk), to_core)
        return over_x, over_core, place

    def forward(gathering):
        over_x, over_core, place = gathering
        over_x.wait_recv()
        return send(place(across), place(across), to_core)

    half = 512 + 128 * chip
    tile_at = pl.ds(pl.multiple_of(128 * blk, 128), 128)
    half_at = pl.ds(pl.multiple_of(half, 128), 128)
    ff_at = pl.ds(pl.multiple_of(768 * blk, 128), 768)
    own_rows = pl.ds(pl.multiple_of(TOK * blk, TOK), TOK)
    local = [
        (r.tokens.at[0], r.x_all.at[own_rows]),
        (r.query_weight.at[:, tile_at], r.wab.at[:, 0:128]),
        (r.key_weight.at[:, tile_at], r.wab.at[:, 128:256]),
        (r.value_weight.at[:, tile_at], r.wab.at[:, 256:384]),
        (r.query_weight.at[:, half_at], r.wb_tile.at[0]),
        (r.key_weight.at[:, half_at], r.wb_tile.at[1]),
        (r.value_weight.at[:, half_at], r.wb_tile.at[2]),
        (r.output_weight, r.wo),
        (r.upstream.at[0], r.u_all.at[own_rows]),
        (r.contract_weight.at[ff_at], r.w2),
        (r.expand_weight.at[:, ff_at], r.w1),
    ]
    local += [
        (getattr(r, name), getattr(r, "v_" + name))
        for name in VECTORS + ["clip_ids", "block_order"]
    ]
    loads = []
    for number, (source, target) in enumerate(local):
        copy = pltpu.make_async_copy(source, target, r.local_sem.at[number])
        copy.start()
        loads.append(copy)

    barrier = pltpu.get_barrier_semaphore()
    for peer in peers:
        pl.semaphore_signal(barrier, inc=1, device_id=peer, device_id_type=MESH)
    pl.semaphore_wait(barrier, len(peers))

    tokens_in = gather(r.tokens.at[0], rows_at(r.x_all, TOK))
    upstream_in = gather(r.upstream.at[0], rows_at(r.u_all, TOK))

    for copy in loads[11:]:
        copy.wait()
    early_gain, early_shift = row_of(r.v_early_gain), row_of(r.v_early_shift)
    late_gain, late_shift = row_of(r.v_late_gain), row_of(r.v_late_shift)

    def picked(vector, size, base, width):
        total = jnp.zeros((1, width), F32)
        for index in range(4):
            begin = base + size * index
            total = total + jnp.where(blk == index, vector[:, begin : begin + width], 0.0)
        return total

    query_bias, value_bias = row_of(r.v_query_bias), row_of(r.v_value_bias)
    bias_qkv = jnp.concatenate(
        [
            picked(query_bias, 128, 0, 128),
            jnp.zeros((1, 128), F32),
            picked(value_bias, 128, 0, 128),
            picked(query_bias, 64, 512, 64),
            jnp.zeros((1, 64), F32),
            picked(value_bias, 64, 512, 64),
        ],
        axis=1,
    )

    lane = lax.broadcasted_iota(jnp.int32, (1, TOK), 1)
    keys_of, low_of = [], []
    for index in range(4):
        place = r.v_block_order[0, index]
        clip = jnp.zeros((1, TOK), jnp.int32)
        for other in range(4):
            clip = clip + jnp.where(
                place == other, r.v_clip_ids[0:1, other * TOK : (other + 1) * TOK], 0
            )
        low_of.append((clip * row).astype(F32))
        keys_of.append((clip * row + place * TOK + lane).astype(F32))
    for key in range(4):
        column = jnp.broadcast_to(keys_of[key], (TOK, TOK)).T
        for query in range(4):
            allowed = (column <= keys_of[query]) & (column >= low_of[query])
            r.mask[key * TOK : (key + 1) * TOK, query * TOK : (query + 1) * TOK] = jnp.where(
                allowed, 0.0, MASKED
            )

    for copy in loads[1:7]:
        copy.wait()
    for index in range(3):
        tile = r.wb_tile[index].astype(F32)
        piece = jnp.where(core == 1, tile[:, 64:128], tile[:, 0:64])
        r.wab[:, 384 + 64 * index : 448 + 64 * index] = piece.astype(BF16)

    def early_norm(start):
        def body(at):
            normed, _ = norm_stats(r.x_all[pl.ds(at, 32), :].astype(F32))
            r.normed[pl.ds(at, 32), :] = normed
            r.first[pl.ds(at, 32), :] = (normed * early_gain + early_shift).astype(BF16)

        by_rows(start, TOK, 32, body, 4)

    def project(start):
        at = pl.ds(pl.multiple_of(start, 2 * TOK), 2 * TOK)
        out = mm(r.first[at, :], r.wab[...], 1, 0) + bias_qkv
        for head, offset, step in ((0, 0, 128), (1, 64, 128), (2, 384, 64)):
            query = out[:, offset : offset + 64]
            r.qh[head, at, :] = (query * 0.125).astype(BF16)
            r.kh[head, at, :] = out[:, offset + step : offset + step + 64].astype(BF16)
            r.vh[head, at, :] = out[:, offset + 2 * step : offset + 2 * step + 64].astype(BF16)

    loads[0].wait()
    early_norm(TOK * blk)
    tokens_in[1].wait_recv()
    early_norm(TOK * sibling)
    project(2 * TOK * chip)
    token_forward = forward(tokens_in)
    early_norm(TOK * across)
    token_forward.wait_recv()
    early_norm(TOK * ((sibling + 2) % 4))
    project(2 * TOK * (1 - chip))

    def attend(head):
        r.st[...] = mm(r.kh[head], r.qh[head], 1, 1)

        @pl.loop(0, 4)
        def _(strip):
            at = pl.ds(pl.multiple_of(strip * TOK, TOK), TOK)
            scores = r.st[:, at] + r.mask[:, at]
            powers = jnp.exp(scores - jnp.max(scores, axis=0, keepdims=True))
            probs = powers * (1.0 / jnp.sum(powers, axis=0, keepdims=True))
            r.pf[head, :, at] = probs
            r.pb[head, :, at] = probs.astype(BF16)

        r.vt[head] = r.vh[head].T
        return mm(r.vt[head], r.pb[head], 1, 0).astype(BF16)

    places = (
        lambda index: pl.multiple_of(128 * index, 64),
        lambda index: pl.multiple_of(128 * index + 64, 64),
        lambda index: pl.multiple_of(512 + 64 * index, 64),
    )

    def head_at(head):
        return lambda index: r.at.at[pl.ds(places[head](index), 64)]

    def attend_and_send(head):
        r.at[pl.ds(places[head](blk), 64), :] = attend(head)
        return gather(head_at(head)(blk), head_at(head))

    start_pair = pl.multiple_of(128 * blk, 128)
    heads_in = [attend_and_send(0)]
    upstream_forward = forward(upstream_in)
    heads_in += [attend_and_send(1), attend_and_send(2)]

    loads[8].wait()
    loads[9].wait()
    upstream_in[1].wait_recv()
    upstream_forward.wait_recv()
    head_forwards = []
    for tile in range(3):
        at = slice(256 * tile, 256 * (tile + 1))
        r.ga[:, at] = mm(r.u_all[...], r.w2[at, :], 1, 1)
        head_forwards.append(forward(heads_in[tile]))
    r.first_t[...] = r.first[...].T
    for head in range(3):
        r.kt[head] = r.kh[head].T
    loads[7].wait()
    loads[10].wait()
    for head in range(3):
        heads_in[head][1].wait_recv()
        head_forwards[head].wait_recv()

    output_bias = row_of(r.v_output_bias)

    @pl.loop(0, 2)
    def _(tile):
        at = pl.ds(pl.multiple_of(tile * 256, 256), 256)
        r.mid[at, :] = mm(r.at[:, at], r.wo[...], 0, 0)

    def late_norm(at):
        at = pl.ds(at, 32)
        middle = r.mid[at, :] + r.x_all[at, :].astype(F32) + output_bias
        r.mid[at, :] = middle
        normed, _ = norm_stats(middle)
        r.second[at, :] = (normed * late_gain + late_shift).astype(BF16)

    by_rows(0, row, 32, late_norm, 4)

    @pl.loop(0, 3)
    def _(tile):
        at = pl.ds(pl.multiple_of(tile * 256, 256), 256)
        r.hid[:, at] = mm(r.second[...], r.w1[:, at], 1, 0)

    expand_bias = picked(row_of(r.v_expand_bias), 768, 0, 768)
    first_factor = 0.7978845608028654
    third_factor = 0.044715

    def gelu(at):
        at = pl.ds(at, 16)
        hidden = r.hid[at, :] + expand_bias
        square = hidden * hidden
        bent = jnp.tanh(first_factor * hidden * (1.0 + third_factor * square))
        grown = 0.5 * (1.0 + bent)
        r.act[at, :] = (hidden * grown).astype(BF16)
        slope = grown + (0.5 * first_factor) * hidden * (1.0 - bent * bent) * (
            1.0 + (3.0 * third_factor) * square
        )
        r.gh[at, :] = (r.ga[at, :] * slope).astype(BF16)

    by_rows(0, row, 16, gelu)

    def contract_half(which):
        at = pl.ds(pl.multiple_of(384 * which, 384), 384)
        return mm(r.act[:, at], r.u_all[...], 0, 0)

    piece = 384 // PIECES
    pieces = [pl.ds(p * piece, piece) for p in range(PIECES)]
    r.c_send[...] = contract_half(1 - y).astype(BF16)
    c_y = [send(r.c_send.at[at], r.c_recv.at[0, at], to_y) for at in pieces]

    def scatter_start(number, part):
        copies = [None, None]
        for index, block in ((1, far), (0, sibling)):
            at = pl.ds(pl.multiple_of(block * TOK, TOK), TOK)
            r.rs_send[number, index] = part[at, :].astype(BF16)
            copies[index] = send(r.rs_send.at[number, index], r.rs_recv.at[number, index], to_core)
        return copies

    def scatter_middle(number, part, copies):
        at = pl.ds(pl.multiple_of(across * TOK, TOK), TOK)
        copies[1].wait_recv()
        r.rs_send[number, 2] = (part[at, :] + r.rs_recv[number, 1].astype(F32)).astype(BF16)
        copies.append(send(r.rs_send.at[number, 2], r.rs_recv.at[number, 2], to_x))

    def scatter_end(copies):
        copies[0].wait_recv()
        copies[2].wait_recv()

    def scattered(number, part, at, size):
        own = pl.ds(pl.multiple_of(blk * TOK + at, size), size)
        here = pl.ds(at, size)
        return (
            part[own, :]
            + r.rs_recv[number, 0, here, :].astype(F32)
            + r.rs_recv[number, 2, here, :].astype(F32)
        )

    def added(target, left, right):
        rows = target.shape[0]

        @pl.loop(0, rows // 32)
        def _(index):
            at = pl.ds(pl.multiple_of(index * 32, 32), 32)
            target[at, :] = (left[at, :].astype(F32) + right[at, :].astype(F32)).astype(target.dtype)

    along_y, along_z0, along_z1 = (y, 1, to_y), (z0, 2, to_z0), (z1, 4, to_z1)

    def halving(name, stages):
        buf, r1, s1, r2, s2 = (
            getattr(r, name + key) for key in ("_buf", "_r1", "_s1", "_r2", "_s2")
        )
        own = [bit * weight for bit, weight, _ in stages]
        other = [(1 - bit) * weight for bit, weight, _ in stages]
        rest = [
            later + last
            for later in (other[1], own[1])
            for last in (other[2], own[2])
        ]
        copies = {}

        def start1():
            copies[1] = [
                send(buf.at[other[0] + rest[index]], r1.at[index], stages[0][2])
                for index in range(4)
            ]

        def end1(*indices):
            for index in indices:
                copies[1][index].wait_recv()
                added(s1.at[index], buf.at[own[0] + rest[index]], r1.at[index])

        def start2():
            copies[2] = [send(s1.at[index], r2.at[index], stages[1][2]) for index in range(2)]

        def start3():
            copies[2][0].wait_recv()
            added(s2.at[0], s1.at[2], r2.at[0])
            copies[3] = send(s2.at[0], r2.at[2], stages[2][2])
            copies[2][1].wait_recv()
            added(s2.at[1], s1.at[3], r2.at[1])

        def finish(target):
            copies[3].wait_recv()
            added(target.at[blk], s2.at[1], r2.at[2])
            place = lambda index: target.at[index]
            return gather(place(blk), place)

        return types.SimpleNamespace(
            start1=start1, end1=end1, start2=start2, start3=start3, finish=finish
        )

    e1 = halving("e1", (along_z0, along_z1, along_y))
    e2 = halving("e2", (along_y, along_z0, along_z1))
    wa = halving("wa", (along_y, along_z0, along_z1))
    wb = halving("wb", (along_y, along_z0, along_z1))

    def expand_part(target, columns):
        for which in range(2):
            block = mm(r.second[:, 384 * which : 384 * (which + 1)], r.gh[:, columns], 0, 0)
            target[4 * which : 4 * which + 4] = block.astype(BF16).reshape(4, 96, 384)

    @pl.loop(0, 3)
    def _(tile):
        at = pl.ds(pl.multiple_of(tile * 256, 256), 256)
        r.part[:, at] = mm(r.gh[...], r.w1[at, :], 1, 1)

    second_sum = scatter_start(0, r.part)
    expand_part(r.e1_buf, slice(0, 384))
    e1.start1()
    scatter_middle(0, r.part, second_sum)
    r.c_own[...] = contract_half(y)
    expand_part(r.e2_buf, slice(384, 768))
    e2.start1()

    @pl.loop(0, 3)
    def _(tile):
        at = pl.ds(pl.multiple_of(tile * 256, 256), 256)
        r.part_out[:, at] = mm(r.act[...], r.w2[:, at], 1, 0)

    out_sum = scatter_start(1, r.part_out)

    scatter_end(second_sum)
    own_start = blk * TOK
    r.sv[0] = jnp.zeros((8, d_model), F32)

    def late_pull(index, carry):
        gain_sum, shift_sum, output_sum, contract_sum = carry
        at = pl.multiple_of(index * 32, 32)
        own = pl.ds(pl.multiple_of(own_start + at, 32), 32)
        grad = scattered(0, r.part, at, 32)
        normed, inverse = norm_stats(r.mid[own, :])
        upstream = r.u_all[own, :].astype(F32)
        middle = upstream + norm_pull(grad, normed, inverse, late_gain)
        r.g_mid[pl.ds(at, 32), :] = middle
        low = middle.astype(BF16)
        r.gb[own, :] = low
        return (
            gain_sum + folded(grad * normed),
            shift_sum + folded(grad),
            output_sum + folded(low.astype(F32)),
            contract_sum + folded(upstream),
        )

    nothing = jnp.zeros((8, d_model), F32)
    sums = lax.fori_loop(0, TOK // 32, late_pull, (nothing,) * 4)

    pulled = mm(r.gb[own_rows, :], r.wo[...], 1, 1)
    r.go_send[...] = pulled[:, 0:512].astype(BF16)
    for index in range(4):
        r.third_send[index] = pulled[:, 512 + 64 * index : 576 + 64 * index].astype(BF16)
    head_grads = []
    for block, peer in ((far, to_far), (across, to_x), (sibling, to_core)):
        lanes = pl.ds(pl.multiple_of(128 * block, 128), 128)
        head_grads.append(send(r.go_send.at[:, lanes], r.go_pair.at[own_rows], peer))
        head_grads.append(send(r.third_send.at[block], r.go.at[2, own_rows], peer))
    r.go_pair[own_rows, :] = r.go_send[:, tile_at]
    r.go[2, own_rows, :] = r.third_send[blk]
    branch_at = rows_at(r.gb, TOK)
    branch_in = gather(branch_at(blk), branch_at)
    for index, value in zip((3, 4, 2, 5), sums):
        r.sv[0, index : index + 1, :] = jnp.sum(value, axis=0, keepdims=True)

    e1.end1(0, 1)
    e1.start2()

    root0, root1 = blk % 2, blk // 2
    keeps0 = z0 == root0
    keeps1 = z1 == root1
    is_root = z == blk
    is_across = z == across
    c_z0 = [remote(r.c_sum.at[0, at], r.c_recv.at[1, at], to_z0) for at in pieces]
    c_z1 = [remote(r.c_sum.at[1, at], r.c_recv.at[2, at], to_z1) for at in pieces]
    c_x = [remote(r.ffc.at[at], r.ffc.at[at], to_x) for at in pieces]
    c_core = [remote(r.ffc.at[at], r.ffc.at[at], to_core) for at in pieces]

    def contract_y_end(p):
        c_y[p].wait_recv()
        added(r.c_sum.at[0, pieces[p]], r.c_own.at[pieces[p]], r.c_recv.at[0, pieces[p]])

        @pl.when(jnp.logical_not(keeps0))
        def _():
            c_z0[p].start()

    def contract_z0_end(p):
        @pl.when(keeps0)
        def _():
            c_z0[p].wait_recv()
            added(r.c_sum.at[1, pieces[p]], r.c_sum.at[0, pieces[p]], r.c_recv.at[1, pieces[p]])

            @pl.when(jnp.logical_not(keeps1))
            def _():
                c_z1[p].start()

    def contract_z1_end(p):
        @pl.when(is_root)
        def _():
            c_z1[p].wait_recv()
            added(r.ffc.at[pieces[p]], r.c_sum.at[1, pieces[p]], r.c_recv.at[2, pieces[p]])
            c_x[p].start()
            c_core[p].start()

    contract_y_end(0)
    e1.end1(2, 3)

    def expand_sum(index, carry):
        at = pl.ds(pl.multiple_of(index * 32, 32), 32)
        return carry + folded(r.gh[at, :].astype(F32))

    r.sv[0, 6:7, :] = jnp.sum(
        lax.fori_loop(0, row // 32, expand_sum, nothing), axis=0, keepdims=True
    )
    for copy in head_grads:
        copy.wait_recv()
    r.go[0] = r.go_pair[:, 0:64]
    r.go[1] = r.go_pair[:, 64:128]

    def attend_back(head, offset, step):
        r.st[...] = mm(r.vh[head], r.go[head], 1, 1)

        @pl.loop(0, 4)
        def _(strip):
            at = pl.ds(pl.multiple_of(strip * TOK, TOK), TOK)
            probs, grad = r.pf[head, :, at], r.st[:, at]
            delta = jnp.sum(probs * grad, axis=0, keepdims=True)
            r.sg[:, at] = (probs * (grad - delta)).astype(BF16)

        query = mm(r.kt[head], r.sg[...], 1, 0) * 0.125
        r.gqkv[:, offset : offset + 64] = query.T.astype(BF16)
        r.gqkv[:, offset + step : offset + step + 64] = mm(
            r.sg[...], r.qh[head], 1, 0
        ).astype(BF16)
        r.gqkv[:, offset + 2 * step : offset + 2 * step + 64] = mm(
            r.pb[head], r.go[head], 1, 0
        ).astype(BF16)

    attend_back(0, 0, 128)
    branch_forward = forward(branch_in)
    attend_back(1, 64, 128)
    contract_y_end(1)
    halves = [(slice(4 * w, 4 * w + 4), slice(384 * w, 384 * (w + 1))) for w in range(2)]
    for blocks, at in halves:
        block = mm(r.first_t[at, :], r.gqkv[:, 0:384], 1, 0)
        r.wa_buf[blocks, :, 0:384] = block.astype(BF16).reshape(4, 96, 384)
    branch_in[1].wait_recv()
    branch_forward.wait_recv()
    r.gbt[:, 0:128] = r.gb[:, tile_at]
    r.gbt[:, 128:256] = r.gb[:, half_at]
    for blocks, at in halves:
        block = mm(r.at[at, :], r.gbt[...], 1, 0)
        r.wa_buf[blocks, :, 384:512] = block[:, 0:128].astype(BF16).reshape(4, 96, 128)
        chosen = jnp.where(core == 1, block[:, 192:256], block[:, 128:192])
        r.wb_buf[blocks, :, 192:256] = chosen.astype(BF16).reshape(4, 96, 64)
    wa.start1()
    contract_z0_end(0)
    e1.start3()
    attend_back(2, 384, 64)
    for blocks, at in halves:
        block = mm(r.first_t[at, :], r.gqkv[:, 384:576], 1, 0)
        r.wb_buf[blocks, :, 0:192] = block.astype(BF16).reshape(4, 96, 192)
    wb.start1()

    @pl.loop(0, 3)
    def _(tile):
        at = pl.ds(pl.multiple_of(tile * 256, 256), 256)
        r.part[:, at] = mm(r.gqkv[...], r.wab[at, :], 1, 1)

    first_sum = scatter_start(2, r.part)

    def qkv_sum(index, carry):
        gain_sum, shift_sum, bias_sum = carry
        at = pl.ds(pl.multiple_of(index * 32, 32), 32)
        part = r.part[at, :]
        return (
            gain_sum + folded(part * r.normed[at, :]),
            shift_sum + folded(part),
            bias_sum + folded(r.gqkv[at, :].astype(F32)),
        )

    sums = lax.fori_loop(
        0, row // 32, qkv_sum, (nothing, nothing, jnp.zeros((8, 576), F32))
    )
    for index in range(2):
        r.sv[0, index : index + 1, :] = jnp.sum(sums[index], axis=0, keepdims=True)
    total = jnp.sum(sums[2], axis=0, keepdims=True)
    r.sv[0, 7:8, 0:384] = total[:, 0:384]
    r.sv[0, 7:8, 512:704] = total[:, 384:576]
    v_y = send(r.sv.at[0], r.sv_recv.at[0], to_y)
    scatter_middle(2, r.part, first_sum)
    contract_z0_end(1)
    e2.end1(0, 1)
    e2.start2()
    e2.end1(2, 3)
    scatter_middle(1, r.part_out, out_sum)
    e2.start3()

    scatter_end(first_sum)

    @pl.loop(0, TOK // 32)
    def _(index):
        at = pl.multiple_of(index * 32, 32)
        own = pl.ds(pl.multiple_of(own_start + at, 32), 32)
        here = pl.ds(at, 32)
        grad = scattered(2, r.part, at, 32)
        normed, inverse = norm_stats(r.x_all[own, :].astype(F32))
        pulled = norm_pull(grad, normed, inverse, early_gain)
        r.token_grad[here, :] = (r.g_mid[here, :] + pulled).astype(BF16)

    contract_z1_end(0)
    wa.end1(0, 1)
    wa.start2()
    e1_in = e1.finish(r.e1g)
    wa.end1(2, 3)
    contract_z1_end(1)
    e2_in = e2.finish(r.e2g)
    v_y.wait_recv()
    r.sv[1] = r.sv[0] + r.sv_recv[0]
    v_z0 = send(r.sv.at[1], r.sv_recv.at[1], to_z0)
    wb.end1(0, 1)
    wb.start2()
    wb.end1(2, 3)
    e1_forward = forward(e1_in)
    wa.start3()

    scatter_end(out_sum)
    contract_bias = row_of(r.v_contract_bias)

    @pl.loop(0, TOK // 32)
    def _(index):
        at = pl.multiple_of(index * 32, 32)
        own = pl.ds(pl.multiple_of(own_start + at, 32), 32)
        value = scattered(1, r.part_out, at, 32) + r.mid[own, :] + contract_bias
        r.block_out[pl.ds(at, 32), :] = value.astype(BF16)

    @pl.when(is_across)
    def _():
        for p in range(PIECES):
            c_x[p].wait_recv()
            c_core[p].start()

    v_z0.wait_recv()
    r.sv[2] = r.sv[1] + r.sv_recv[1]
    v_z1 = send(r.sv.at[2], r.sv_recv.at[2], to_z1)
    wb.start3()
    e2_forward = forward(e2_in)
    wa_in = wa.finish(r.wag)
    v_z1.wait_recv()
    r.svg[blk] = r.sv[2] + r.sv_recv[2]
    v_at = lambda index: r.svg.at[index]
    v_in = gather(v_at(blk), v_at)
    wb_in = wb.finish(r.wbg)
    forwards = [e1_forward, e2_forward, forward(wa_in), forward(v_in), forward(wb_in)]

    @pl.when(jnp.logical_not(jnp.logical_or(is_root, is_across)))
    def _():
        for p in range(PIECES):
            c_core[p].wait_recv()

    for gathering in (e1_in, e2_in, wa_in, v_in, wb_in):
        gathering[1].wait_recv()
    for copy in forwards:
        copy.wait_recv()

    for copy in sent:
        copy.wait_send()

    @pl.when(jnp.logical_not(keeps0))
    def _():
        for copy in c_z0:
            copy.wait_send()

    @pl.when(jnp.logical_and(keeps0, jnp.logical_not(keeps1)))
    def _():
        for copy in c_z1:
            copy.wait_send()

    @pl.when(is_root)
    def _():
        for copy in c_x:
            copy.wait_send()

    @pl.when(jnp.logical_or(is_root, is_across))
    def _():
        for copy in c_core:
            copy.wait_send()


def write_kernel(*refs):
    sources, outs, held, sem = refs[:8], refs[8:25], refs[25:33], refs[33]
    copies = [
        pltpu.make_async_copy(source, target, sem.at[number])
        for number, (source, target) in enumerate(zip(sources, held))
    ]
    for copy in copies:
        copy.start()
    for copy in copies:
        copy.wait()
    block_in, grad_in, ffc, e1g, e2g, wag, wbg, svg = held
    (block_out, token_grad, gain_early, shift_early, query_grad, bias_query, key_grad, value_grad) = outs[:8]
    (bias_value, output_grad, bias_output, gain_late, shift_late, expand_grad, bias_expand) = outs[8:15]
    contract_grad, bias_contract = outs[15:]
    dp = lax.axis_index("dp")
    block_out[0] = block_in[...]
    token_grad[0] = grad_in[...]
    for index in range(4):
        wide = slice(128 * index, 128 * (index + 1))
        narrow = slice(512 + 64 * index, 576 + 64 * index)
        for number, target in enumerate((query_grad, key_grad, value_grad, output_grad)):
            target[:, wide] = wag[index, :, 128 * number : 128 * (number + 1)].astype(F32)
            target[:, narrow] = wbg[index, :, 64 * number : 64 * (number + 1)].astype(F32)
        expand_grad[:, 768 * index : 768 * index + 384] = e1g[index].astype(F32)
        expand_grad[:, 768 * index + 384 : 768 * (index + 1)] = e2g[index].astype(F32)
    contract_grad[...] = ffc[...].astype(F32)
    summed = svg[0] + svg[1] + svg[2] + svg[3]
    query_row = jnp.concatenate(
        [svg[i, 7:8, 0:128] for i in range(4)] + [svg[i, 7:8, 512:576] for i in range(4)], axis=1
    )
    value_row = jnp.concatenate(
        [svg[i, 7:8, 256:384] for i in range(4)] + [svg[i, 7:8, 640:704] for i in range(4)], axis=1
    )
    rows = jnp.concatenate([summed[0:6], query_row, value_row], axis=0)
    turned = pltpu.roll(rows, 768 - 96 * dp, 1)
    targets = (gain_early, shift_early, bias_output, gain_late, shift_late, bias_contract)
    for number, target in enumerate(targets + (bias_query, bias_value)):
        target[...] = turned[number, 0:96]
    hidden = jnp.zeros((8, 768), F32)
    for index in range(4):
        hidden = hidden + jnp.where(dp // 2 == index, svg[index], 0.0)
    bias_expand[...] = pltpu.roll(hidden, 768 - 384 * (dp % 2), 1)[6, 0:384]


def fast_local(*arguments):
    scratch = fast_scratch()
    vmem = pl.BlockSpec(memory_space=pltpu.VMEM)
    away = pl.BlockSpec(memory_space=pl.ANY)
    shape = jax.ShapeDtypeStruct
    results = (
        shape((TOK, 768), BF16),
        shape((TOK, 768), BF16),
        shape((384, 768), BF16),
        shape((4, 96, 384), BF16),
        shape((4, 96, 384), BF16),
        shape((4, 96, 512), BF16),
        shape((4, 96, 256), BF16),
        shape((4, 8, 768), F32),
    )
    names = INPUTS + RESULTS + list(scratch)
    moved = pl.pallas_call(
        functools.partial(layer_kernel, names),
        name="layer",
        out_shape=results,
        in_specs=[away] * len(INPUTS),
        out_specs=(vmem,) * len(results),
        scratch_shapes=list(scratch.values()),
        compiler_params=pltpu.CompilerParams(
            collective_id=0, has_side_effects=True, vmem_limit_bytes=56 << 20
        ),
    )(*arguments)
    outs = (
        [shape((1, TOK, 768), BF16)] * 2
        + [shape((96,), F32)] * 2
        + [shape((96, 768), F32), shape((96,), F32), shape((96, 768), F32), shape((96, 768), F32)]
        + [shape((96,), F32), shape((96, 768), F32)]
        + [shape((96,), F32)] * 3
        + [shape((96, 3072), F32), shape((384,), F32), shape((384, 768), F32), shape((96,), F32)]
    )
    return pl.pallas_call(
        write_kernel,
        name="write",
        out_shape=tuple(outs),
        in_specs=[away] * 8,
        out_specs=(vmem,) * len(outs),
        scratch_shapes=[pltpu.VMEM(item.shape, item.dtype) for item in results]
        + [pltpu.SemaphoreType.DMA((8,))],
        compiler_params=pltpu.CompilerParams(vmem_limit_bytes=60 << 20),
    )(*moved)


def passed_along(value, axis, steps):
    count = lax.axis_size(axis)
    pairs = [(source, (source + steps) % count) for source in range(count)]
    return lax.ppermute(value, axis, pairs)


def layer_norm(inputs, gain, shift):
    average = jnp.mean(inputs, axis=-1, keepdims=True)
    centred = inputs - average
    inverse = lax.rsqrt(jnp.mean(centred * centred, axis=-1, keepdims=True) + EPSILON)
    normed = centred * inverse
    return (normed * gain + shift, normed, inverse)


def norm_back(grad_out, normed, inverse, gain):
    scaled = grad_out * gain
    inner = (
        scaled
        - jnp.mean(scaled, axis=-1, keepdims=True)
        - normed * jnp.mean(scaled * normed, axis=-1, keepdims=True)
    )
    return (
        inverse * inner,
        jnp.sum(grad_out * normed, axis=(0, 1)),
        jnp.sum(grad_out, axis=(0, 1)),
    )


def project(inputs, weight):
    return jnp.einsum("rtd,de->rte", inputs, weight, preferred_element_type=jnp.float32)


def project_back(grad_rows, weight):
    return jnp.einsum("rte,de->rtd", grad_rows, weight, preferred_element_type=jnp.float32)


def weight_grad(inputs, grad_rows):
    return jnp.einsum("rtd,rte->de", inputs, grad_rows, preferred_element_type=jnp.float32)


def column_sum(grad_rows):
    return jnp.sum(grad_rows.astype(jnp.float32), axis=(0, 1))


def general_local(
    tokens,
    early_gain,
    early_shift,
    query_weight,
    query_bias,
    key_weight,
    value_weight,
    value_bias,
    output_weight,
    output_bias,
    late_gain,
    late_shift,
    expand_weight,
    expand_bias,
    contract_weight,
    contract_bias,
    upstream,
    clip_ids,
    block_order,
):
    row_count, block_len, features = tokens.shape
    head_count = HEADS
    head_size = features // head_count
    scale_factor = float(head_size) ** (-0.5)
    my_index = lax.axis_index("blk")
    group_size = lax.axis_size("blk")

    def positions(begin, length):
        stored = begin + jnp.arange(length, dtype=jnp.int32)
        logical = (
            jnp.take(block_order, stored // block_len, axis=1) * block_len + stored % block_len
        )
        return (logical, jnp.take_along_axis(clip_ids, logical, axis=1))

    query_pos, query_clip = positions(my_index * block_len, block_len)

    def visible(begin, length):
        key_pos, key_clip = positions(begin, length)
        allowed = (key_pos[:, None, :] <= query_pos[:, :, None]) & (
            key_clip[:, None, :] == query_clip[:, :, None]
        )
        return allowed[:, None]

    def split_heads(array):
        return array.reshape(row_count, array.shape[1], head_count, head_size)

    inputs = tokens.astype(jnp.float32)
    first_full, first_normed, first_inverse = layer_norm(
        inputs, early_gain.astype(jnp.float32), early_shift.astype(jnp.float32)
    )
    first_low = first_full.astype(jnp.bfloat16)
    queries = (project(first_low, query_weight) + query_bias.astype(jnp.float32)).astype(
        jnp.bfloat16
    )
    key_rows = project(first_low, key_weight).astype(jnp.bfloat16)
    value_rows = (project(first_low, value_weight) + value_bias.astype(jnp.float32)).astype(
        jnp.bfloat16
    )
    query_heads = split_heads(queries)

    def scores_of(key_block):
        return (
            jnp.einsum(
                "rqhe,rkhe->rhqk",
                query_heads,
                split_heads(key_block),
                preferred_element_type=jnp.float32,
            )
            * scale_factor
        )

    def absorb(carry, key_block, value_block, begin):
        allowed = visible(begin, key_block.shape[1])
        maximum, denominator, numerator = carry
        scores = jnp.where(allowed, scores_of(key_block), MASKED)
        new_max = jnp.maximum(maximum, jnp.max(scores, axis=-1))
        weights = jnp.where(allowed, jnp.exp(scores - new_max[..., None]), 0.0)
        factor = jnp.exp(maximum - new_max)
        update = jnp.einsum(
            "rhqk,rkhe->rqhe",
            weights.astype(jnp.bfloat16),
            split_heads(value_block),
            preferred_element_type=jnp.float32,
        )
        numerator = numerator * jnp.transpose(factor, (0, 2, 1))[..., None] + update
        return (new_max, denominator * factor + jnp.sum(weights, axis=-1), numerator)

    start_state = (
        jnp.full((row_count, head_count, block_len), MASKED, jnp.float32),
        jnp.zeros((row_count, head_count, block_len), jnp.float32),
        jnp.zeros((row_count, block_len, head_count, head_size), jnp.float32),
    )
    key_piece = lax.all_gather(key_rows, "blk", axis=1, tiled=True)
    value_piece = lax.all_gather(value_rows, "blk", axis=1, tiled=True)
    length = key_piece.shape[1]
    stride = min(length, block_len)

    def one_block(number, running):
        offset = number * stride
        return absorb(
            running,
            lax.dynamic_slice_in_dim(key_piece, offset, stride, 1),
            lax.dynamic_slice_in_dim(value_piece, offset, stride, 1),
            offset,
        )

    maximum, denominator, numerator = lax.fori_loop(0, length // stride, one_block, start_state)
    log_total = maximum + jnp.log(denominator)
    attention = numerator / jnp.transpose(denominator, (0, 2, 1))[..., None]
    attention_low = attention.reshape(row_count, block_len, features).astype(jnp.bfloat16)
    middle = inputs + project(attention_low, output_weight) + output_bias.astype(jnp.float32)
    second_full, second_normed, second_inverse = layer_norm(
        middle, late_gain.astype(jnp.float32), late_shift.astype(jnp.float32)
    )
    second_low = second_full.astype(jnp.bfloat16)
    hidden = project(second_low, expand_weight) + expand_bias.astype(jnp.float32)
    active_full, gelu_pull = jax.vjp(
        lambda values_in: jax.nn.gelu(values_in, approximate=True), hidden
    )
    active_low = active_full.astype(jnp.bfloat16)
    block_out = (
        middle + project(active_low, contract_weight) + contract_bias.astype(jnp.float32)
    ).astype(jnp.bfloat16)
    grad_out = upstream.astype(jnp.float32)
    contract_g = weight_grad(active_low, upstream)
    contract_b = column_sum(upstream)
    hidden_low = gelu_pull(project_back(upstream, contract_weight))[0].astype(jnp.bfloat16)
    expand_g = weight_grad(second_low, hidden_low)
    expand_b = column_sum(hidden_low)
    norm_grad, late_gain_g, late_shift_g = norm_back(
        project_back(hidden_low, expand_weight),
        second_normed,
        second_inverse,
        late_gain.astype(jnp.float32),
    )
    middle_grad = grad_out + norm_grad
    branch_low = middle_grad.astype(jnp.bfloat16)
    output_g = weight_grad(attention_low, branch_low)
    output_b = column_sum(branch_low)
    grad_heads = split_heads(project_back(branch_low, output_weight).astype(jnp.bfloat16))
    delta = jnp.transpose(jnp.sum(grad_heads.astype(jnp.float32) * attention, axis=-1), (0, 2, 1))

    def turn_step(number, carried):
        key_block, value_block, key_acc, value_acc, query_acc = carried
        source = (my_index - number) % group_size
        allowed = visible(source * block_len, block_len)
        use_key, use_value = (key_block, value_block)
        key_sum = key_acc
        value_sum = value_acc
        query_sum = query_acc
        probs = jnp.where(allowed, jnp.exp(scores_of(use_key) - log_total[..., None]), 0.0)
        value_sum = value_sum + jnp.einsum(
            "rhqk,rqhe->rkhe",
            probs.astype(jnp.bfloat16),
            grad_heads,
            preferred_element_type=jnp.float32,
        ).reshape(row_count, block_len, features)
        prob_grad = jnp.einsum(
            "rqhe,rkhe->rhqk",
            grad_heads,
            split_heads(use_value),
            preferred_element_type=jnp.float32,
        )
        score_grad = (probs * (prob_grad - delta[..., None])).astype(jnp.bfloat16)
        query_sum = (
            query_sum
            + jnp.einsum(
                "rhqk,rkhe->rqhe",
                score_grad,
                split_heads(use_key),
                preferred_element_type=jnp.float32,
            )
            * scale_factor
        )
        key_sum = key_sum + (
            jnp.einsum(
                "rhqk,rqhe->rkhe", score_grad, query_heads, preferred_element_type=jnp.float32
            )
            * scale_factor
        ).reshape(row_count, block_len, features)
        key_acc = key_sum
        value_acc = value_sum
        key_block, value_block = passed_along((key_block, value_block), "blk", 1)
        key_acc, value_acc = (
            passed_along(key_acc.astype(jnp.bfloat16), "blk", 1).astype(key_acc.dtype),
            passed_along(value_acc.astype(jnp.bfloat16), "blk", 1).astype(value_acc.dtype),
        )
        return (key_block, value_block, key_acc, value_acc, query_sum)

    zero_rows = jnp.zeros((row_count, block_len, features), jnp.float32)
    carried = (
        key_rows,
        value_rows,
        zero_rows,
        zero_rows,
        jnp.zeros((row_count, block_len, head_count, head_size), jnp.float32),
    )
    carried = lax.fori_loop(0, group_size, turn_step, carried)
    query_low = carried[4].reshape(row_count, block_len, features).astype(jnp.bfloat16)
    key_low = carried[2].astype(jnp.bfloat16)
    value_low = carried[3].astype(jnp.bfloat16)
    query_g = weight_grad(first_low, query_low)
    key_g = weight_grad(first_low, key_low)
    value_g = weight_grad(first_low, value_low)
    query_b = column_sum(query_low)
    value_b = column_sum(value_low)
    first_grad = (
        project_back(query_low, query_weight)
        + project_back(key_low, key_weight)
        + project_back(value_low, value_weight)
    )
    input_grad, early_gain_g, early_shift_g = norm_back(
        first_grad, first_normed, first_inverse, early_gain.astype(jnp.float32)
    )
    token_grad = (middle_grad + input_grad).astype(jnp.bfloat16)
    local_grads = (
        early_gain_g,
        early_shift_g,
        query_g,
        query_b,
        key_g,
        value_g,
        value_b,
        output_g,
        output_b,
        late_gain_g,
        late_shift_g,
        expand_g,
        expand_b,
        contract_g,
        contract_b,
    )
    owners = lax.axis_size("dp")
    laid_out = jnp.concatenate([member.reshape(owners, -1) for member in local_grads], axis=1)
    shares = lax.psum_scatter(laid_out.astype(jnp.bfloat16), "dp", scatter_dimension=0, tiled=True)
    summed = lax.psum(shares, "blk").astype(jnp.float32)
    pieces = []
    offset = 0
    for member in local_grads:
        width = member.size // owners
        own_shape = (member.shape[0] // owners,) + member.shape[1:]
        pieces.append(summed[0, offset : offset + width].reshape(own_shape))
        offset = offset + width
    return (block_out, token_grad) + tuple(pieces)


def solution(mesh):
    placed = (
        P("dp", "blk", None),
        P(),
        P(),
        P(),
        P(),
        P(),
        P(),
        P(),
        P(),
        P(),
        P(),
        P(),
        P(),
        P(),
        P(),
        P(),
        P("dp", "blk", None),
        P("dp", None),
        P("dp", None),
    )
    narrow = mesh.shape["dp"] == 8 and mesh.shape["blk"] == 4
    return jax.shard_map(
        fast_local if narrow else general_local,
        mesh=mesh,
        in_specs=placed,
        out_specs=(
            P("dp", "blk", None),
            P("dp", "blk", None),
            P("dp"),
            P("dp"),
            P("dp", None),
            P("dp"),
            P("dp", None),
            P("dp", None),
            P("dp"),
            P("dp", None),
            P("dp"),
            P("dp"),
            P("dp"),
            P("dp", None),
            P("dp"),
            P("dp", None),
            P("dp"),
        ),
        check_vma=False,
    )
```

```python
import functools
import itertools
import types

import jax
import jax.numpy as jnp
from jax import lax
from jax.experimental import pallas as pl
from jax.experimental.pallas import tpu as pltpu
from jax.sharding import PartitionSpec as P

HEADS = 12
EPSILON = 1e-05
MASKED = -1e30
F32 = jnp.float32
BF16 = jnp.bfloat16
MESH = pl.DeviceIdType.MESH
TOK = 128
PIECES = 2


def mm(left, right, left_dim, right_dim):
    return lax.dot_general(
        left, right, (((left_dim,), (right_dim,)), ((), ())), preferred_element_type=F32
    )


def norm_stats(value):
    centred = value - jnp.mean(value, axis=-1, keepdims=True)
    inverse = lax.rsqrt(jnp.mean(centred * centred, axis=-1, keepdims=True) + EPSILON)
    return centred * inverse, inverse


def norm_pull(grad, normed, inverse, gain):
    scaled = grad * gain
    return inverse * (
        scaled
        - jnp.mean(scaled, axis=-1, keepdims=True)
        - normed * jnp.mean(scaled * normed, axis=-1, keepdims=True)
    )


def row_of(ref):
    return ref[...].astype(F32).reshape(1, ref.shape[0])


def by_rows(start, count, step, body, unroll=2):
    @pl.loop(0, count // step, unroll=unroll)
    def _(index):
        body(pl.multiple_of(start + index * step, step))


def folded(value):
    rows, columns = value.shape
    return jnp.sum(value.reshape(rows // 8, 8, columns), axis=0)


def halving_scratch(name, width):
    sizes = {"_buf": 8, "_r1": 4, "_s1": 4, "_r2": 3, "_s2": 2}
    return {name + key: pltpu.VMEM((size, 96, width), BF16) for key, size in sizes.items()}


def fast_scratch():
    row, d = 4 * TOK, 768
    vm = pltpu.VMEM
    return dict(
        x_all=vm((row, d), BF16),
        u_all=vm((row, d), BF16),
        wab=vm((d, 576), BF16),
        wb_tile=vm((3, d, 128), BF16),
        wo=vm((d, d), BF16),
        w1=vm((d, d), BF16),
        w2=vm((d, d), BF16),
        first=vm((row, d), BF16),
        normed=vm((row, d), F32),
        first_t=vm((d, row), BF16),
        qh=vm((3, row, 64), BF16),
        kh=vm((3, row, 64), BF16),
        vh=vm((3, row, 64), BF16),
        kt=vm((3, 64, row), BF16),
        vt=vm((3, 64, row), BF16),
        mask=vm((row, row), F32),
        st=vm((row, row), F32),
        pf=vm((3, row, row), F32),
        pb=vm((3, row, row), BF16),
        sg=vm((row, row), BF16),
        at=vm((d, row), BF16),
        mid=vm((row, d), F32),
        second=vm((row, d), BF16),
        hid=vm((row, d), F32),
        ga=vm((row, d), F32),
        act=vm((row, d), BF16),
        gh=vm((row, d), BF16),
        part=vm((row, d), F32),
        part_out=vm((row, d), F32),
        rs_send=vm((3, 3, TOK, d), BF16),
        rs_recv=vm((3, 3, TOK, d), BF16),
        g_mid=vm((TOK, d), F32),
        gb=vm((row, d), BF16),
        gbt=vm((row, 256), BF16),
        go=vm((3, row, 64), BF16),
        go_pair=vm((row, 128), BF16),
        go_send=vm((TOK, 512), BF16),
        third_send=vm((4, TOK, 64), BF16),
        gqkv=vm((row, 576), BF16),
        c_send=vm((384, d), BF16),
        c_own=vm((384, d), F32),
        c_recv=vm((3, 384, d), BF16),
        c_sum=vm((2, 384, d), BF16),
        **halving_scratch("e1", 384),
        **halving_scratch("e2", 384),
        **halving_scratch("wa", 384),
        **halving_scratch("wb", 384),
        sv=vm((4, 8, d), F32),
        sv_recv=vm((3, 8, d), F32),
        **{"v_" + name: vm((4 * d if name == "expand_bias" else d,), BF16) for name in VECTORS},
        v_clip_ids=vm((1, row), jnp.int32),
        v_block_order=pltpu.SMEM((1, 4), jnp.int32),
        block_out=vm((TOK, d), BF16),
        token_grad=vm((TOK, d), BF16),
        ffc=vm((384, d), BF16),
        e1g=vm((4, 96, 384), BF16),
        e2g=vm((4, 96, 384), BF16),
        wag=vm((4, 96, 384), BF16),
        wbg=vm((4, 96, 384), BF16),
        svg=vm((4, 8, d), F32),
        local_sem=pltpu.SemaphoreType.DMA((32,)),
        send_sem=pltpu.SemaphoreType.DMA((128,)),
        recv_sem=pltpu.SemaphoreType.DMA((128,)),
    )


INPUTS = [
    "tokens",
    "early_gain",
    "early_shift",
    "query_weight",
    "query_bias",
    "key_weight",
    "value_weight",
    "value_bias",
    "output_weight",
    "output_bias",
    "late_gain",
    "late_shift",
    "expand_weight",
    "expand_bias",
    "contract_weight",
    "contract_bias",
    "upstream",
    "clip_ids",
    "block_order",
]
VECTORS = [
    "early_gain",
    "early_shift",
    "query_bias",
    "value_bias",
    "output_bias",
    "late_gain",
    "late_shift",
    "expand_bias",
    "contract_bias",
]
RESULTS = ["block_out", "token_grad", "ffc", "e1g", "e2g", "wag", "wbg", "svg"]


def layer_kernel(names, *refs):
    r = types.SimpleNamespace(**dict(zip(names, refs)))
    d_model = 768
    row = 4 * TOK
    dp, blk = lax.axis_index("dp"), lax.axis_index("blk")
    core, chip = blk % 2, blk // 2
    sibling, across = blk + 1 - 2 * core, (blk + 2) % 4
    y, z = dp % 2, dp // 2
    z0, z1 = z % 2, z // 2
    to_core = {"dp": dp, "blk": sibling}
    to_x = {"dp": dp, "blk": across}
    to_y = {"dp": dp + 1 - 2 * y, "blk": blk}
    to_z0 = {"dp": dp + 2 - 4 * z0, "blk": blk}
    to_z1 = {"dp": (dp + 4) % 8, "blk": blk}
    far = (sibling + 2) % 4
    to_far = {"dp": dp, "blk": far}
    peers = (to_core, to_x, to_far, to_y, to_z0, to_z1)
    numbers = itertools.count()
    sent = []

    def remote(source, target, peer):
        number = next(numbers)
        assert number < 128
        return pltpu.make_async_remote_copy(
            src_ref=source,
            dst_ref=target,
            send_sem=r.send_sem.at[number],
            recv_sem=r.recv_sem.at[number],
            device_id=peer,
            device_id_type=MESH,
        )

    def send(source, target, peer):
        copy = remote(source, target, peer)
        copy.start()
        sent.append(copy)
        return copy

    def rows_at(ref, size, base=0):
        return lambda index: ref.at[pl.ds(pl.multiple_of(base + index * size, size), size)]

    def gather(source, place):
        over_x = send(source, place(blk), to_x)
        over_core = send(source, place(blk), to_core)
        return over_x, over_core, place

    def forward(gathering):
        over_x, over_core, place = gathering
        over_x.wait_recv()
        return send(place(across), place(across), to_core)

    written = []

    def write_out(name):
        copy = pltpu.make_async_copy(
            getattr(r, name), getattr(r, "out_" + name), r.local_sem.at[24 + len(written)]
        )
        copy.start()
        written.append(copy)

    half = 512 + 128 * chip
    tile_at = pl.ds(pl.multiple_of(128 * blk, 128), 128)
    half_at = pl.ds(pl.multiple_of(half, 128), 128)
    ff_at = pl.ds(pl.multiple_of(768 * blk, 128), 768)
    own_rows = pl.ds(pl.multiple_of(TOK * blk, TOK), TOK)
    local = [
        (r.tokens.at[0], r.x_all.at[own_rows]),
        (r.query_weight.at[:, tile_at], r.wab.at[:, 0:128]),
        (r.key_weight.at[:, tile_at], r.wab.at[:, 128:256]),
        (r.value_weight.at[:, tile_at], r.wab.at[:, 256:384]),
        (r.query_weight.at[:, half_at], r.wb_tile.at[0]),
        (r.key_weight.at[:, half_at], r.wb_tile.at[1]),
        (r.value_weight.at[:, half_at], r.wb_tile.at[2]),
        (r.output_weight, r.wo),
        (r.upstream.at[0], r.u_all.at[own_rows]),
        (r.contract_weight.at[ff_at], r.w2),
        (r.expand_weight.at[:, ff_at], r.w1),
    ]
    local += [
        (getattr(r, name), getattr(r, "v_" + name))
        for name in VECTORS + ["clip_ids", "block_order"]
    ]
    loads = []
    for number, (source, target) in enumerate(local):
        copy = pltpu.make_async_copy(source, target, r.local_sem.at[number])
        copy.start()
        loads.append(copy)

    barrier = pltpu.get_barrier_semaphore()
    for peer in peers:
        pl.semaphore_signal(barrier, inc=1, device_id=peer, device_id_type=MESH)
    pl.semaphore_wait(barrier, len(peers))

    tokens_in = gather(r.tokens.at[0], rows_at(r.x_all, TOK))
    upstream_in = gather(r.upstream.at[0], rows_at(r.u_all, TOK))

    for copy in loads[11:]:
        copy.wait()
    early_gain, early_shift = row_of(r.v_early_gain), row_of(r.v_early_shift)
    late_gain, late_shift = row_of(r.v_late_gain), row_of(r.v_late_shift)

    def picked(vector, size, base, width):
        total = jnp.zeros((1, width), F32)
        for index in range(4):
            begin = base + size * index
            total = total + jnp.where(blk == index, vector[:, begin : begin + width], 0.0)
        return total

    query_bias, value_bias = row_of(r.v_query_bias), row_of(r.v_value_bias)
    bias_qkv = jnp.concatenate(
        [
            picked(query_bias, 128, 0, 128),
            jnp.zeros((1, 128), F32),
            picked(value_bias, 128, 0, 128),
            picked(query_bias, 64, 512, 64),
            jnp.zeros((1, 64), F32),
            picked(value_bias, 64, 512, 64),
        ],
        axis=1,
    )

    lane = lax.broadcasted_iota(jnp.int32, (1, TOK), 1)
    keys_of, low_of = [], []
    for index in range(4):
        place = r.v_block_order[0, index]
        clip = jnp.zeros((1, TOK), jnp.int32)
        for other in range(4):
            clip = clip + jnp.where(
                place == other, r.v_clip_ids[0:1, other * TOK : (other + 1) * TOK], 0
            )
        low_of.append((clip * row).astype(F32))
        keys_of.append((clip * row + place * TOK + lane).astype(F32))
    for key in range(4):
        column = jnp.broadcast_to(keys_of[key], (TOK, TOK)).T
        for query in range(4):
            allowed = (column <= keys_of[query]) & (column >= low_of[query])
            r.mask[key * TOK : (key + 1) * TOK, query * TOK : (query + 1) * TOK] = jnp.where(
                allowed, 0.0, MASKED
            )

    for copy in loads[1:7]:
        copy.wait()
    for index in range(3):
        tile = r.wb_tile[index].astype(F32)
        piece = jnp.where(core == 1, tile[:, 64:128], tile[:, 0:64])
        r.wab[:, 384 + 64 * index : 448 + 64 * index] = piece.astype(BF16)

    def early_norm(start):
        def body(at):
            normed, _ = norm_stats(r.x_all[pl.ds(at, 32), :].astype(F32))
            r.normed[pl.ds(at, 32), :] = normed
            r.first[pl.ds(at, 32), :] = (normed * early_gain + early_shift).astype(BF16)

        by_rows(start, TOK, 32, body, 4)

    def project(start):
        at = pl.ds(pl.multiple_of(start, 2 * TOK), 2 * TOK)
        out = mm(r.first[at, :], r.wab[...], 1, 0) + bias_qkv
        for head, offset, step in ((0, 0, 128), (1, 64, 128), (2, 384, 64)):
            query = out[:, offset : offset + 64]
            r.qh[head, at, :] = (query * 0.125).astype(BF16)
            r.kh[head, at, :] = out[:, offset + step : offset + step + 64].astype(BF16)
            r.vh[head, at, :] = out[:, offset + 2 * step : offset + 2 * step + 64].astype(BF16)

    loads[0].wait()
    early_norm(TOK * blk)
    tokens_in[1].wait_recv()
    early_norm(TOK * sibling)
    project(2 * TOK * chip)
    token_forward = forward(tokens_in)
    early_norm(TOK * across)
    token_forward.wait_recv()
    early_norm(TOK * ((sibling + 2) % 4))
    project(2 * TOK * (1 - chip))

    def attend(head):
        r.st[...] = mm(r.kh[head], r.qh[head], 1, 1)

        @pl.loop(0, 4)
        def _(strip):
            at = pl.ds(pl.multiple_of(strip * TOK, TOK), TOK)
            scores = r.st[:, at] + r.mask[:, at]
            powers = jnp.exp(scores - jnp.max(scores, axis=0, keepdims=True))
            probs = powers * (1.0 / jnp.sum(powers, axis=0, keepdims=True))
            r.pf[head, :, at] = probs
            r.pb[head, :, at] = probs.astype(BF16)

        r.vt[head] = r.vh[head].T
        return mm(r.vt[head], r.pb[head], 1, 0).astype(BF16)

    places = (
        lambda index: pl.multiple_of(128 * index, 64),
        lambda index: pl.multiple_of(128 * index + 64, 64),
        lambda index: pl.multiple_of(512 + 64 * index, 64),
    )

    def head_at(head):
        return lambda index: r.at.at[pl.ds(places[head](index), 64)]

    def attend_and_send(head):
        r.at[pl.ds(places[head](blk), 64), :] = attend(head)
        return gather(head_at(head)(blk), head_at(head))

    start_pair = pl.multiple_of(128 * blk, 128)
    heads_in = [attend_and_send(0)]
    upstream_forward = forward(upstream_in)
    heads_in += [attend_and_send(1), attend_and_send(2)]

    loads[8].wait()
    loads[9].wait()
    upstream_in[1].wait_recv()
    upstream_forward.wait_recv()
    head_forwards = []
    for tile in range(3):
        at = slice(256 * tile, 256 * (tile + 1))
        r.ga[:, at] = mm(r.u_all[...], r.w2[at, :], 1, 1)
        head_forwards.append(forward(heads_in[tile]))
    r.first_t[...] = r.first[...].T
    for head in range(3):
        r.kt[head] = r.kh[head].T
    loads[7].wait()
    loads[10].wait()
    for head in range(3):
        heads_in[head][1].wait_recv()
        head_forwards[head].wait_recv()

    output_bias = row_of(r.v_output_bias)

    @pl.loop(0, 2)
    def _(tile):
        at = pl.ds(pl.multiple_of(tile * 256, 256), 256)
        r.mid[at, :] = mm(r.at[:, at], r.wo[...], 0, 0)

    def late_norm(at):
        at = pl.ds(at, 32)
        middle = r.mid[at, :] + r.x_all[at, :].astype(F32) + output_bias
        r.mid[at, :] = middle
        normed, _ = norm_stats(middle)
        r.second[at, :] = (normed * late_gain + late_shift).astype(BF16)

    by_rows(0, row, 32, late_norm, 4)

    for tile in range(3):
        at = slice(256 * tile, 256 * (tile + 1))
        r.hid[:, at] = mm(r.second[...], r.w1[:, at], 1, 0)

    expand_bias = picked(row_of(r.v_expand_bias), 768, 0, 768)
    first_factor = 0.7978845608028654
    third_factor = 0.044715

    def gelu(at):
        at = pl.ds(at, 16)
        hidden = r.hid[at, :] + expand_bias
        square = hidden * hidden
        bent = jnp.tanh(first_factor * hidden * (1.0 + third_factor * square))
        grown = 0.5 * (1.0 + bent)
        r.act[at, :] = (hidden * grown).astype(BF16)
        slope = grown + (0.5 * first_factor) * hidden * (1.0 - bent * bent) * (
            1.0 + (3.0 * third_factor) * square
        )
        r.gh[at, :] = (r.ga[at, :] * slope).astype(BF16)

    by_rows(0, row, 16, gelu)

    def contract_half(which):
        at = pl.ds(pl.multiple_of(384 * which, 384), 384)
        return mm(r.act[:, at], r.u_all[...], 0, 0)

    piece = 384 // PIECES
    pieces = [pl.ds(p * piece, piece) for p in range(PIECES)]

    r.c_send[...] = contract_half(1 - y).astype(BF16)
    c_y = [send(r.c_send.at[at], r.c_recv.at[0, at], to_y) for at in pieces]

    def block_rows(block):
        return pl.ds(pl.multiple_of(block * TOK, TOK), TOK)

    def two_blocks(ref, first, second):
        return jnp.concatenate([ref[block_rows(first), :], ref[block_rows(second), :]], axis=0)

    def scatter_send(number, index):
        return send(r.rs_send.at[number, index], r.rs_recv.at[number, index], to_core)

    def part_pair(grads, weight, first, second):
        @pl.loop(0, 3)
        def _(tile):
            at = pl.ds(pl.multiple_of(tile * 256, 256), 256)
            value = mm(two_blocks(grads, first, second), weight[at, :], 1, 1)
            r.part[block_rows(first), at] = value[0:TOK]
            r.part[block_rows(second), at] = value[TOK : 2 * TOK]

    def part_start(number, grads, weight):
        part_pair(grads, weight, far, sibling)
        copies = scatter_start(number, r.part)
        part_pair(grads, weight, across, blk)
        return copies

    def scatter_start(number, part):
        copies = [None, None]
        for index, block in ((1, far), (0, sibling)):
            r.rs_send[number, index] = part[block_rows(block), :].astype(BF16)
            copies[index] = scatter_send(number, index)
        return copies

    def scatter_middle(number, part, copies):
        at = pl.ds(pl.multiple_of(across * TOK, TOK), TOK)
        copies[1].wait_recv()
        r.rs_send[number, 2] = (part[at, :] + r.rs_recv[number, 1].astype(F32)).astype(BF16)
        copies.append(send(r.rs_send.at[number, 2], r.rs_recv.at[number, 2], to_x))

    def scatter_end(copies):
        copies[0].wait_recv()
        copies[2].wait_recv()

    def scattered(number, part, at, size):
        own = pl.ds(pl.multiple_of(blk * TOK + at, size), size)
        here = pl.ds(at, size)
        return (
            part[own, :]
            + r.rs_recv[number, 0, here, :].astype(F32)
            + r.rs_recv[number, 2, here, :].astype(F32)
        )

    def added(target, left, right):
        rows = target.shape[0]

        @pl.loop(0, rows // 32)
        def _(index):
            at = pl.ds(pl.multiple_of(index * 32, 32), 32)
            target[at, :] = (left[at, :].astype(F32) + right[at, :].astype(F32)).astype(target.dtype)

    along_y, along_z0, along_z1 = (y, 1, to_y), (z0, 2, to_z0), (z1, 4, to_z1)

    def halving(name, stages):
        buf, r1, s1, r2, s2 = (
            getattr(r, name + key) for key in ("_buf", "_r1", "_s1", "_r2", "_s2")
        )
        own = [bit * weight for bit, weight, _ in stages]
        other = [(1 - bit) * weight for bit, weight, _ in stages]
        rest = [
            later + last
            for later in (other[1], own[1])
            for last in (other[2], own[2])
        ]
        copies = {}

        def start1():
            copies[1] = [
                send(buf.at[other[0] + rest[index]], r1.at[index], stages[0][2])
                for index in range(4)
            ]

        def end1(*indices):
            for index in indices:
                copies[1][index].wait_recv()
                added(s1.at[index], buf.at[own[0] + rest[index]], r1.at[index])

        def start2():
            copies[2] = [send(s1.at[index], r2.at[index], stages[1][2]) for index in range(2)]

        def start3():
            copies[2][0].wait_recv()
            added(s2.at[0], s1.at[2], r2.at[0])
            copies[3] = send(s2.at[0], r2.at[2], stages[2][2])
            copies[2][1].wait_recv()
            added(s2.at[1], s1.at[3], r2.at[1])

        def finish(target):
            copies[3].wait_recv()
            added(target.at[blk], s2.at[1], r2.at[2])
            place = lambda index: target.at[index]
            return gather(place(blk), place)

        return types.SimpleNamespace(
            start1=start1, end1=end1, start2=start2, start3=start3, finish=finish
        )

    e1 = halving("e1", (along_z0, along_z1, along_y))
    e2 = halving("e2", (along_y, along_z0, along_z1))
    wa = halving("wa", (along_y, along_z0, along_z1))
    wb = halving("wb", (along_y, along_z0, along_z1))

    def expand_part(target, columns):
        for which in range(2):
            block = mm(r.second[:, 384 * which : 384 * (which + 1)], r.gh[:, columns], 0, 0)
            target[4 * which : 4 * which + 4] = block.astype(BF16).reshape(4, 96, 384)

    second_sum = part_start(0, r.gh, r.w1)
    scatter_middle(0, r.part, second_sum)
    expand_part(r.e1_buf, slice(0, 384))
    e1.start1()
    r.c_own[...] = contract_half(y)
    expand_part(r.e2_buf, slice(384, 768))
    e2.start1()

    for tile in range(3):
        at = slice(256 * tile, 256 * (tile + 1))
        r.part_out[:, at] = mm(r.act[...], r.w2[:, at], 1, 0)

    out_sum = scatter_start(1, r.part_out)

    scatter_end(second_sum)
    own_start = blk * TOK
    r.sv[0] = jnp.zeros((8, d_model), F32)

    def late_pull(index, carry):
        gain_sum, shift_sum, output_sum, contract_sum = carry
        at = pl.multiple_of(index * 32, 32)
        own = pl.ds(pl.multiple_of(own_start + at, 32), 32)
        grad = scattered(0, r.part, at, 32)
        normed, inverse = norm_stats(r.mid[own, :])
        upstream = r.u_all[own, :].astype(F32)
        middle = upstream + norm_pull(grad, normed, inverse, late_gain)
        r.g_mid[pl.ds(at, 32), :] = middle
        low = middle.astype(BF16)
        r.gb[own, :] = low
        return (
            gain_sum + folded(grad * normed),
            shift_sum + folded(grad),
            output_sum + folded(low.astype(F32)),
            contract_sum + folded(upstream),
        )

    nothing = jnp.zeros((8, d_model), F32)
    sums = lax.fori_loop(0, TOK // 32, late_pull, (nothing,) * 4)

    pulled = mm(r.gb[own_rows, :], r.wo[...], 1, 1)
    r.go_send[...] = pulled[:, 0:512].astype(BF16)
    for index in range(4):
        r.third_send[index] = pulled[:, 512 + 64 * index : 576 + 64 * index].astype(BF16)
    head_grads = []
    for block, peer in ((far, to_far), (across, to_x), (sibling, to_core)):
        lanes = pl.ds(pl.multiple_of(128 * block, 128), 128)
        head_grads.append(send(r.go_send.at[:, lanes], r.go_pair.at[own_rows], peer))
        head_grads.append(send(r.third_send.at[block], r.go.at[2, own_rows], peer))
    r.go_pair[own_rows, :] = r.go_send[:, tile_at]
    r.go[2, own_rows, :] = r.third_send[blk]
    branch_at = rows_at(r.gb, TOK)
    branch_in = gather(branch_at(blk), branch_at)
    for index, value in zip((3, 4, 2, 5), sums):
        r.sv[0, index : index + 1, :] = jnp.sum(value, axis=0, keepdims=True)

    e1.end1(0, 1)
    e1.start2()

    root0, root1 = blk % 2, blk // 2
    keeps0 = z0 == root0
    keeps1 = z1 == root1
    is_root = z == blk
    is_across = z == across
    c_z0 = [remote(r.c_sum.at[0, at], r.c_recv.at[1, at], to_z0) for at in pieces]
    c_z1 = [remote(r.c_sum.at[1, at], r.c_recv.at[2, at], to_z1) for at in pieces]
    c_x = [remote(r.ffc.at[at], r.ffc.at[at], to_x) for at in pieces]
    c_core = [remote(r.ffc.at[at], r.ffc.at[at], to_core) for at in pieces]

    def contract_y_end(p):
        c_y[p].wait_recv()
        added(r.c_sum.at[0, pieces[p]], r.c_own.at[pieces[p]], r.c_recv.at[0, pieces[p]])

        @pl.when(jnp.logical_not(keeps0))
        def _():
            c_z0[p].start()

    def contract_z0_end(p):
        @pl.when(keeps0)
        def _():
            c_z0[p].wait_recv()
            added(r.c_sum.at[1, pieces[p]], r.c_sum.at[0, pieces[p]], r.c_recv.at[1, pieces[p]])

            @pl.when(jnp.logical_not(keeps1))
            def _():
                c_z1[p].start()

    def contract_z1_end(p):
        @pl.when(is_root)
        def _():
            c_z1[p].wait_recv()
            added(r.ffc.at[pieces[p]], r.c_sum.at[1, pieces[p]], r.c_recv.at[2, pieces[p]])
            c_x[p].start()
            c_core[p].start()

    e1.end1(2, 3)
    contract_y_end(0)

    def expand_sum(index, carry):
        at = pl.ds(pl.multiple_of(index * 32, 32), 32)
        return carry + folded(r.gh[at, :].astype(F32))

    r.sv[0, 6:7, :] = jnp.sum(
        lax.fori_loop(0, row // 32, expand_sum, nothing), axis=0, keepdims=True
    )
    for copy in head_grads:
        copy.wait_recv()
    r.go[0] = r.go_pair[:, 0:64]
    r.go[1] = r.go_pair[:, 64:128]

    def attend_back(head, offset, step):
        r.st[...] = mm(r.vh[head], r.go[head], 1, 1)

        @pl.loop(0, 4)
        def _(strip):
            at = pl.ds(pl.multiple_of(strip * TOK, TOK), TOK)
            probs, grad = r.pf[head, :, at], r.st[:, at]
            delta = jnp.sum(probs * grad, axis=0, keepdims=True)
            r.sg[:, at] = (probs * (grad - delta)).astype(BF16)

        query = mm(r.kt[head], r.sg[...], 1, 0) * 0.125
        r.gqkv[:, offset : offset + 64] = query.T.astype(BF16)
        r.gqkv[:, offset + step : offset + step + 64] = mm(
            r.sg[...], r.qh[head], 1, 0
        ).astype(BF16)
        r.gqkv[:, offset + 2 * step : offset + 2 * step + 64] = mm(
            r.pb[head], r.go[head], 1, 0
        ).astype(BF16)

    halves = [(slice(4 * w, 4 * w + 4), slice(384 * w, 384 * (w + 1))) for w in range(2)]
    attend_back(0, 0, 128)
    contract_y_end(1)
    contract_z0_end(0)
    attend_back(1, 64, 128)
    for blocks, at in halves:
        block = mm(r.first_t[at, :], r.gqkv[:, 0:384], 1, 0)
        r.wa_buf[blocks] = block.astype(BF16).reshape(4, 96, 384)
    wa.start1()
    scatter_middle(1, r.part_out, out_sum)
    branch_forward = forward(branch_in)
    e1.start3()
    attend_back(2, 384, 64)
    contract_z0_end(1)
    e2.end1(0, 1)
    e2.start2()

    def qkv_sum(index, carry):
        gain_sum, shift_sum, bias_sum = carry
        at = pl.ds(pl.multiple_of(index * 32, 32), 32)
        part = r.part[at, :]
        return (
            gain_sum + folded(part * r.normed[at, :]),
            shift_sum + folded(part),
            bias_sum + folded(r.gqkv[at, :].astype(F32)),
        )

    first_sum = part_start(2, r.gqkv, r.wab)
    scatter_middle(2, r.part, first_sum)
    sums = lax.fori_loop(
        0, row // 32, qkv_sum, (nothing, nothing, jnp.zeros((8, 576), F32))
    )
    for index in range(2):
        r.sv[0, index : index + 1, :] = jnp.sum(sums[index], axis=0, keepdims=True)
    total = jnp.sum(sums[2], axis=0, keepdims=True)
    r.sv[0, 7:8, 0:384] = total[:, 0:384]
    r.sv[0, 7:8, 512:704] = total[:, 384:576]
    v_y = send(r.sv.at[0], r.sv_recv.at[0], to_y)

    branch_in[1].wait_recv()
    branch_forward.wait_recv()
    r.gbt[:, 0:128] = r.gb[:, tile_at]
    r.gbt[:, 128:256] = r.gb[:, half_at]
    for blocks, at in halves:
        block = mm(r.first_t[at, :], r.gqkv[:, 384:576], 1, 0)
        r.wb_buf[blocks, :, 0:192] = block.astype(BF16).reshape(4, 96, 192)
        block = mm(r.at[at, :], r.gbt[...], 1, 0)
        chosen = jnp.where(core == 1, block[:, 192:256], block[:, 128:192])
        r.wb_buf[blocks, :, 192:256] = chosen.astype(BF16).reshape(4, 96, 64)
        r.wb_buf[blocks, :, 256:384] = block[:, 0:128].astype(BF16).reshape(4, 96, 128)
    wb.start1()
    contract_z1_end(0)
    e2.end1(2, 3)

    scatter_end(out_sum)
    contract_bias = row_of(r.v_contract_bias)

    @pl.loop(0, TOK // 32)
    def _(index):
        at = pl.multiple_of(index * 32, 32)
        own = pl.ds(pl.multiple_of(own_start + at, 32), 32)
        value = scattered(1, r.part_out, at, 32) + r.mid[own, :] + contract_bias
        r.block_out[pl.ds(at, 32), :] = value.astype(BF16)

    write_out("block_out")
    v_y.wait_recv()
    r.sv[1] = r.sv[0] + r.sv_recv[0]
    v_z0 = send(r.sv.at[1], r.sv_recv.at[1], to_z0)
    wa.end1(0, 1)
    wa.start2()
    wa.end1(2, 3)
    e2.start3()

    scatter_end(first_sum)

    @pl.loop(0, TOK // 32)
    def _(index):
        at = pl.multiple_of(index * 32, 32)
        own = pl.ds(pl.multiple_of(own_start + at, 32), 32)
        here = pl.ds(at, 32)
        grad = scattered(2, r.part, at, 32)
        normed, inverse = norm_stats(r.x_all[own, :].astype(F32))
        pulled = norm_pull(grad, normed, inverse, early_gain)
        r.token_grad[here, :] = (r.g_mid[here, :] + pulled).astype(BF16)

    write_out("token_grad")
    e1_in = e1.finish(r.e1g)
    v_z0.wait_recv()
    r.sv[2] = r.sv[1] + r.sv_recv[1]
    v_z1 = send(r.sv.at[2], r.sv_recv.at[2], to_z1)
    contract_z1_end(1)
    wb.end1(0, 1)
    wb.start2()
    wb.end1(2, 3)
    e2_in = e2.finish(r.e2g)
    wa.start3()

    @pl.when(is_across)
    def _():
        for p in range(PIECES):
            c_x[p].wait_recv()
            c_core[p].start()

    e1_forward = forward(e1_in)
    v_z1.wait_recv()
    r.svg[blk] = r.sv[2] + r.sv_recv[2]
    v_at = lambda index: r.svg.at[index]
    v_in = gather(v_at(blk), v_at)
    wb.start3()
    e2_forward = forward(e2_in)
    wa_in = wa.finish(r.wag)

    @pl.when(jnp.logical_not(jnp.logical_or(is_root, is_across)))
    def _():
        for p in range(PIECES):
            c_core[p].wait_recv()

    write_out("ffc")
    v_forward = forward(v_in)
    wb_in = wb.finish(r.wbg)
    wa_forward = forward(wa_in)
    wb_forward = forward(wb_in)
    for name, gathering, copy in (
        ("e1g", e1_in, e1_forward),
        ("e2g", e2_in, e2_forward),
        ("svg", v_in, v_forward),
        ("wag", wa_in, wa_forward),
        ("wbg", wb_in, wb_forward),
    ):
        gathering[1].wait_recv()
        copy.wait_recv()
        write_out(name)

    for copy in written:
        copy.wait()

    for copy in sent:
        copy.wait_send()

    @pl.when(jnp.logical_not(keeps0))
    def _():
        for copy in c_z0:
            copy.wait_send()

    @pl.when(jnp.logical_and(keeps0, jnp.logical_not(keeps1)))
    def _():
        for copy in c_z1:
            copy.wait_send()

    @pl.when(is_root)
    def _():
        for copy in c_x:
            copy.wait_send()

    @pl.when(jnp.logical_or(is_root, is_across))
    def _():
        for copy in c_core:
            copy.wait_send()


def write_kernel(*refs):
    count, sources, outs = len(RESULTS), refs[: len(RESULTS)], refs[len(RESULTS) :][:17]
    held, made = refs[count + 17 :][:count], refs[2 * count + 17 :][:15]
    in_sem, out_sem = refs[-2:]
    (gain_early, shift_early, query_grad, bias_query, key_grad, value_grad) = made[:6]
    (bias_value, output_grad, bias_output, gain_late, shift_late, expand_grad, bias_expand) = made[6:13]
    contract_grad, bias_contract = made[13:]
    dp = lax.axis_index("dp")
    loads = [
        pltpu.make_async_copy(source, target, in_sem.at[number])
        for number, (source, target) in enumerate(zip(sources, held))
    ]
    for number in (3, 4, 2, 5, 6, 7, 0, 1):
        loads[number].start()
    block_out, token_grad, ffc, e1g, e2g, wag, wbg, svg = held
    left = []

    def leave(target):
        number = [item is target for item in made].index(True)
        copy = pltpu.make_async_copy(target, outs[number + 2], out_sem.at[number + 2])
        copy.start()
        left.append(copy)

    for copy in loads[3:5]:
        copy.wait()
    for index in range(4):
        expand_grad[:, 768 * index : 768 * index + 384] = e1g[index].astype(F32)
        expand_grad[:, 768 * index + 384 : 768 * (index + 1)] = e2g[index].astype(F32)
    leave(expand_grad)
    loads[2].wait()
    contract_grad[...] = ffc[...].astype(F32)
    leave(contract_grad)
    for copy in loads[5:7]:
        copy.wait()
    for number, target in enumerate((query_grad, key_grad, value_grad, output_grad)):
        for index in range(4):
            wide = slice(128 * index, 128 * (index + 1))
            narrow = slice(512 + 64 * index, 576 + 64 * index)
            if number < 3:
                target[:, wide] = wag[index, :, 128 * number : 128 * (number + 1)].astype(F32)
            else:
                target[:, wide] = wbg[index, :, 256:384].astype(F32)
            target[:, narrow] = wbg[index, :, 64 * number : 64 * (number + 1)].astype(F32)
        leave(target)
    loads[7].wait()
    summed = svg[0] + svg[1] + svg[2] + svg[3]
    query_row = jnp.concatenate(
        [svg[i, 7:8, 0:128] for i in range(4)] + [svg[i, 7:8, 512:576] for i in range(4)], axis=1
    )
    value_row = jnp.concatenate(
        [svg[i, 7:8, 256:384] for i in range(4)] + [svg[i, 7:8, 640:704] for i in range(4)], axis=1
    )
    rows = jnp.concatenate([summed[0:6], query_row, value_row], axis=0)
    turned = pltpu.roll(rows, 768 - 96 * dp, 1)
    targets = (gain_early, shift_early, bias_output, gain_late, shift_late, bias_contract)
    for number, target in enumerate(targets + (bias_query, bias_value)):
        target[...] = turned[number, 0:96]
        leave(target)
    hidden = jnp.zeros((8, 768), F32)
    for index in range(4):
        hidden = hidden + jnp.where(dp // 2 == index, svg[index], 0.0)
    bias_expand[...] = pltpu.roll(hidden, 768 - 384 * (dp % 2), 1)[6, 0:384]
    leave(bias_expand)
    for number, value in enumerate((block_out, token_grad)):
        loads[number].wait()
        copy = pltpu.make_async_copy(value, outs[number].at[0], out_sem.at[number])
        copy.start()
        left.append(copy)
    for copy in left:
        copy.wait()


def fast_local(*arguments):
    scratch = fast_scratch()
    away = pl.BlockSpec(memory_space=pl.ANY)
    shape = jax.ShapeDtypeStruct
    results = (
        shape((TOK, 768), BF16),
        shape((TOK, 768), BF16),
        shape((384, 768), BF16),
        shape((4, 96, 384), BF16),
        shape((4, 96, 384), BF16),
        shape((4, 96, 384), BF16),
        shape((4, 96, 384), BF16),
        shape((4, 8, 768), F32),
    )
    names = INPUTS + ["out_" + name for name in RESULTS] + list(scratch)
    moved = pl.pallas_call(
        functools.partial(layer_kernel, names),
        name="layer",
        out_shape=results,
        in_specs=[away] * len(INPUTS),
        out_specs=(away,) * len(results),
        scratch_shapes=list(scratch.values()),
        compiler_params=pltpu.CompilerParams(
            collective_id=0, has_side_effects=True, vmem_limit_bytes=56 << 20
        ),
    )(*arguments)
    outs = (
        [shape((1, TOK, 768), BF16)] * 2
        + [shape((96,), F32)] * 2
        + [shape((96, 768), F32), shape((96,), F32), shape((96, 768), F32), shape((96, 768), F32)]
        + [shape((96,), F32), shape((96, 768), F32)]
        + [shape((96,), F32)] * 3
        + [shape((96, 3072), F32), shape((384,), F32), shape((384, 768), F32), shape((96,), F32)]
    )
    return pl.pallas_call(
        write_kernel,
        name="write",
        out_shape=tuple(outs),
        in_specs=[away] * len(results),
        out_specs=(away,) * len(outs),
        scratch_shapes=[pltpu.VMEM(item.shape, item.dtype) for item in results]
        + [pltpu.VMEM(item.shape, item.dtype) for item in outs[2:]]
        + [pltpu.SemaphoreType.DMA((8,)), pltpu.SemaphoreType.DMA((17,))],
        compiler_params=pltpu.CompilerParams(vmem_limit_bytes=60 << 20),
    )(*moved)


def passed_along(value, axis, steps):
    count = lax.axis_size(axis)
    pairs = [(source, (source + steps) % count) for source in range(count)]
    return lax.ppermute(value, axis, pairs)


def layer_norm(inputs, gain, shift):
    average = jnp.mean(inputs, axis=-1, keepdims=True)
    centred = inputs - average
    inverse = lax.rsqrt(jnp.mean(centred * centred, axis=-1, keepdims=True) + EPSILON)
    normed = centred * inverse
    return (normed * gain + shift, normed, inverse)


def norm_back(grad_out, normed, inverse, gain):
    scaled = grad_out * gain
    inner = (
        scaled
        - jnp.mean(scaled, axis=-1, keepdims=True)
        - normed * jnp.mean(scaled * normed, axis=-1, keepdims=True)
    )
    return (
        inverse * inner,
        jnp.sum(grad_out * normed, axis=(0, 1)),
        jnp.sum(grad_out, axis=(0, 1)),
    )


def project(inputs, weight):
    return jnp.einsum("rtd,de->rte", inputs, weight, preferred_element_type=jnp.float32)


def project_back(grad_rows, weight):
    return jnp.einsum("rte,de->rtd", grad_rows, weight, preferred_element_type=jnp.float32)


def weight_grad(inputs, grad_rows):
    return jnp.einsum("rtd,rte->de", inputs, grad_rows, preferred_element_type=jnp.float32)


def column_sum(grad_rows):
    return jnp.sum(grad_rows.astype(jnp.float32), axis=(0, 1))


def general_local(
    tokens,
    early_gain,
    early_shift,
    query_weight,
    query_bias,
    key_weight,
    value_weight,
    value_bias,
    output_weight,
    output_bias,
    late_gain,
    late_shift,
    expand_weight,
    expand_bias,
    contract_weight,
    contract_bias,
    upstream,
    clip_ids,
    block_order,
):
    row_count, block_len, features = tokens.shape
    head_count = HEADS
    head_size = features // head_count
    scale_factor = float(head_size) ** (-0.5)
    my_index = lax.axis_index("blk")
    group_size = lax.axis_size("blk")

    def positions(begin, length):
        stored = begin + jnp.arange(length, dtype=jnp.int32)
        logical = (
            jnp.take(block_order, stored // block_len, axis=1) * block_len + stored % block_len
        )
        return (logical, jnp.take_along_axis(clip_ids, logical, axis=1))

    query_pos, query_clip = positions(my_index * block_len, block_len)

    def visible(begin, length):
        key_pos, key_clip = positions(begin, length)
        allowed = (key_pos[:, None, :] <= query_pos[:, :, None]) & (
            key_clip[:, None, :] == query_clip[:, :, None]
        )
        return allowed[:, None]

    def split_heads(array):
        return array.reshape(row_count, array.shape[1], head_count, head_size)

    inputs = tokens.astype(jnp.float32)
    first_full, first_normed, first_inverse = layer_norm(
        inputs, early_gain.astype(jnp.float32), early_shift.astype(jnp.float32)
    )
    first_low = first_full.astype(jnp.bfloat16)
    queries = (project(first_low, query_weight) + query_bias.astype(jnp.float32)).astype(
        jnp.bfloat16
    )
    key_rows = project(first_low, key_weight).astype(jnp.bfloat16)
    value_rows = (project(first_low, value_weight) + value_bias.astype(jnp.float32)).astype(
        jnp.bfloat16
    )
    query_heads = split_heads(queries)

    def scores_of(key_block):
        return (
            jnp.einsum(
                "rqhe,rkhe->rhqk",
                query_heads,
                split_heads(key_block),
                preferred_element_type=jnp.float32,
            )
            * scale_factor
        )

    def absorb(carry, key_block, value_block, begin):
        allowed = visible(begin, key_block.shape[1])
        maximum, denominator, numerator = carry
        scores = jnp.where(allowed, scores_of(key_block), MASKED)
        new_max = jnp.maximum(maximum, jnp.max(scores, axis=-1))
        weights = jnp.where(allowed, jnp.exp(scores - new_max[..., None]), 0.0)
        factor = jnp.exp(maximum - new_max)
        update = jnp.einsum(
            "rhqk,rkhe->rqhe",
            weights.astype(jnp.bfloat16),
            split_heads(value_block),
            preferred_element_type=jnp.float32,
        )
        numerator = numerator * jnp.transpose(factor, (0, 2, 1))[..., None] + update
        return (new_max, denominator * factor + jnp.sum(weights, axis=-1), numerator)

    start_state = (
        jnp.full((row_count, head_count, block_len), MASKED, jnp.float32),
        jnp.zeros((row_count, head_count, block_len), jnp.float32),
        jnp.zeros((row_count, block_len, head_count, head_size), jnp.float32),
    )
    key_piece = lax.all_gather(key_rows, "blk", axis=1, tiled=True)
    value_piece = lax.all_gather(value_rows, "blk", axis=1, tiled=True)
    length = key_piece.shape[1]
    stride = min(length, block_len)

    def one_block(number, running):
        offset = number * stride
        return absorb(
            running,
            lax.dynamic_slice_in_dim(key_piece, offset, stride, 1),
            lax.dynamic_slice_in_dim(value_piece, offset, stride, 1),
            offset,
        )

    maximum, denominator, numerator = lax.fori_loop(0, length // stride, one_block, start_state)
    log_total = maximum + jnp.log(denominator)
    attention = numerator / jnp.transpose(denominator, (0, 2, 1))[..., None]
    attention_low = attention.reshape(row_count, block_len, features).astype(jnp.bfloat16)
    middle = inputs + project(attention_low, output_weight) + output_bias.astype(jnp.float32)
    second_full, second_normed, second_inverse = layer_norm(
        middle, late_gain.astype(jnp.float32), late_shift.astype(jnp.float32)
    )
    second_low = second_full.astype(jnp.bfloat16)
    hidden = project(second_low, expand_weight) + expand_bias.astype(jnp.float32)
    active_full, gelu_pull = jax.vjp(
        lambda values_in: jax.nn.gelu(values_in, approximate=True), hidden
    )
    active_low = active_full.astype(jnp.bfloat16)
    block_out = (
        middle + project(active_low, contract_weight) + contract_bias.astype(jnp.float32)
    ).astype(jnp.bfloat16)
    grad_out = upstream.astype(jnp.float32)
    contract_g = weight_grad(active_low, upstream)
    contract_b = column_sum(upstream)
    hidden_low = gelu_pull(project_back(upstream, contract_weight))[0].astype(jnp.bfloat16)
    expand_g = weight_grad(second_low, hidden_low)
    expand_b = column_sum(hidden_low)
    norm_grad, late_gain_g, late_shift_g = norm_back(
        project_back(hidden_low, expand_weight),
        second_normed,
        second_inverse,
        late_gain.astype(jnp.float32),
    )
    middle_grad = grad_out + norm_grad
    branch_low = middle_grad.astype(jnp.bfloat16)
    output_g = weight_grad(attention_low, branch_low)
    output_b = column_sum(branch_low)
    grad_heads = split_heads(project_back(branch_low, output_weight).astype(jnp.bfloat16))
    delta = jnp.transpose(jnp.sum(grad_heads.astype(jnp.float32) * attention, axis=-1), (0, 2, 1))

    def turn_step(number, carried):
        key_block, value_block, key_acc, value_acc, query_acc = carried
        source = (my_index - number) % group_size
        allowed = visible(source * block_len, block_len)
        use_key, use_value = (key_block, value_block)
        key_sum = key_acc
        value_sum = value_acc
        query_sum = query_acc
        probs = jnp.where(allowed, jnp.exp(scores_of(use_key) - log_total[..., None]), 0.0)
        value_sum = value_sum + jnp.einsum(
            "rhqk,rqhe->rkhe",
            probs.astype(jnp.bfloat16),
            grad_heads,
            preferred_element_type=jnp.float32,
        ).reshape(row_count, block_len, features)
        prob_grad = jnp.einsum(
            "rqhe,rkhe->rhqk",
            grad_heads,
            split_heads(use_value),
            preferred_element_type=jnp.float32,
        )
        score_grad = (probs * (prob_grad - delta[..., None])).astype(jnp.bfloat16)
        query_sum = (
            query_sum
            + jnp.einsum(
                "rhqk,rkhe->rqhe",
                score_grad,
                split_heads(use_key),
                preferred_element_type=jnp.float32,
            )
            * scale_factor
        )
        key_sum = key_sum + (
            jnp.einsum(
                "rhqk,rqhe->rkhe", score_grad, query_heads, preferred_element_type=jnp.float32
            )
            * scale_factor
        ).reshape(row_count, block_len, features)
        key_acc = key_sum
        value_acc = value_sum
        key_block, value_block = passed_along((key_block, value_block), "blk", 1)
        key_acc, value_acc = (
            passed_along(key_acc.astype(jnp.bfloat16), "blk", 1).astype(key_acc.dtype),
            passed_along(value_acc.astype(jnp.bfloat16), "blk", 1).astype(value_acc.dtype),
        )
        return (key_block, value_block, key_acc, value_acc, query_sum)

    zero_rows = jnp.zeros((row_count, block_len, features), jnp.float32)
    carried = (
        key_rows,
        value_rows,
        zero_rows,
        zero_rows,
        jnp.zeros((row_count, block_len, head_count, head_size), jnp.float32),
    )
    carried = lax.fori_loop(0, group_size, turn_step, carried)
    query_low = carried[4].reshape(row_count, block_len, features).astype(jnp.bfloat16)
    key_low = carried[2].astype(jnp.bfloat16)
    value_low = carried[3].astype(jnp.bfloat16)
    query_g = weight_grad(first_low, query_low)
    key_g = weight_grad(first_low, key_low)
    value_g = weight_grad(first_low, value_low)
    query_b = column_sum(query_low)
    value_b = column_sum(value_low)
    first_grad = (
        project_back(query_low, query_weight)
        + project_back(key_low, key_weight)
        + project_back(value_low, value_weight)
    )
    input_grad, early_gain_g, early_shift_g = norm_back(
        first_grad, first_normed, first_inverse, early_gain.astype(jnp.float32)
    )
    token_grad = (middle_grad + input_grad).astype(jnp.bfloat16)
    local_grads = (
        early_gain_g,
        early_shift_g,
        query_g,
        query_b,
        key_g,
        value_g,
        value_b,
        output_g,
        output_b,
        late_gain_g,
        late_shift_g,
        expand_g,
        expand_b,
        contract_g,
        contract_b,
    )
    owners = lax.axis_size("dp")
    laid_out = jnp.concatenate([member.reshape(owners, -1) for member in local_grads], axis=1)
    shares = lax.psum_scatter(laid_out.astype(jnp.bfloat16), "dp", scatter_dimension=0, tiled=True)
    summed = lax.psum(shares, "blk").astype(jnp.float32)
    pieces = []
    offset = 0
    for member in local_grads:
        width = member.size // owners
        own_shape = (member.shape[0] // owners,) + member.shape[1:]
        pieces.append(summed[0, offset : offset + width].reshape(own_shape))
        offset = offset + width
    return (block_out, token_grad) + tuple(pieces)


def solution(mesh):
    placed = (
        P("dp", "blk", None),
        P(),
        P(),
        P(),
        P(),
        P(),
        P(),
        P(),
        P(),
        P(),
        P(),
        P(),
        P(),
        P(),
        P(),
        P(),
        P("dp", "blk", None),
        P("dp", None),
        P("dp", None),
    )
    narrow = mesh.shape["dp"] == 8 and mesh.shape["blk"] == 4
    return jax.shard_map(
        fast_local if narrow else general_local,
        mesh=mesh,
        in_specs=placed,
        out_specs=(
            P("dp", "blk", None),
            P("dp", "blk", None),
            P("dp"),
            P("dp"),
            P("dp", None),
            P("dp"),
            P("dp", None),
            P("dp", None),
            P("dp"),
            P("dp", None),
            P("dp"),
            P("dp"),
            P("dp"),
            P("dp", None),
            P("dp"),
            P("dp", None),
            P("dp"),
        ),
        check_vma=False,
    )
```

```python
import functools
import itertools
import types

import jax
import jax.numpy as jnp
from jax import lax
from jax.experimental import pallas as pl
from jax.experimental.pallas import tpu as pltpu
from jax.sharding import PartitionSpec as P

HEADS = 12
EPSILON = 1e-05
MASKED = -1e30
F32 = jnp.float32
BF16 = jnp.bfloat16
MESH = pl.DeviceIdType.MESH
TOK = 128
PIECES = 2


def mm(left, right, left_dim, right_dim):
    return lax.dot_general(
        left, right, (((left_dim,), (right_dim,)), ((), ())), preferred_element_type=F32
    )


def norm_stats(value):
    centred = value - jnp.mean(value, axis=-1, keepdims=True)
    inverse = lax.rsqrt(jnp.mean(centred * centred, axis=-1, keepdims=True) + EPSILON)
    return centred * inverse, inverse


def norm_pull(grad, normed, inverse, gain):
    scaled = grad * gain
    return inverse * (
        scaled
        - jnp.mean(scaled, axis=-1, keepdims=True)
        - normed * jnp.mean(scaled * normed, axis=-1, keepdims=True)
    )


def row_of(ref):
    return ref[...].astype(F32).reshape(1, ref.shape[0])


def by_rows(start, count, step, body, unroll=2):
    @pl.loop(0, count // step, unroll=unroll)
    def _(index):
        body(pl.multiple_of(start + index * step, step))


def folded(value):
    rows, columns = value.shape
    return jnp.sum(value.reshape(rows // 8, 8, columns), axis=0)


def halving_scratch(name, width):
    sizes = {"_buf": 8, "_r1": 4, "_s1": 4, "_r2": 3, "_s2": 2}
    return {name + key: pltpu.VMEM((size, 96, width), BF16) for key, size in sizes.items()}


def fast_scratch():
    row, d = 4 * TOK, 768
    vm = pltpu.VMEM
    return dict(
        x_all=vm((row, d), BF16),
        u_all=vm((row, d), BF16),
        wab=vm((d, 576), BF16),
        wb_tile=vm((3, d, 128), BF16),
        wo=vm((d, d), BF16),
        w1=vm((d, d), BF16),
        w2=vm((d, d), BF16),
        first=vm((row, d), BF16),
        normed=vm((row, d), F32),
        first_t=vm((d, row), BF16),
        qh=vm((3, row, 64), BF16),
        kh=vm((3, row, 64), BF16),
        vh=vm((3, row, 64), BF16),
        kt=vm((3, 64, row), BF16),
        vt=vm((3, 64, row), BF16),
        mask=vm((row, row), F32),
        st=vm((row, row), F32),
        pf=vm((3, row, row), F32),
        pb=vm((3, row, row), BF16),
        sg=vm((row, row), BF16),
        at=vm((d, row), BF16),
        mid=vm((row, d), F32),
        second=vm((row, d), BF16),
        hid=vm((row, d), F32),
        ga=vm((row, d), F32),
        act=vm((row, d), BF16),
        gh=vm((row, d), BF16),
        part=vm((row, d), F32),
        part_out=vm((row, d), F32),
        rs_send=vm((3, 3, TOK, d), BF16),
        rs_recv=vm((3, 3, TOK, d), BF16),
        g_mid=vm((TOK, d), F32),
        gb=vm((row, d), BF16),
        gbt=vm((row, 256), BF16),
        go=vm((3, row, 64), BF16),
        go_pair=vm((row, 128), BF16),
        go_send=vm((TOK, 512), BF16),
        third_send=vm((4, TOK, 64), BF16),
        gqkv=vm((row, 576), BF16),
        c_send=vm((384, d), BF16),
        c_own=vm((384, d), F32),
        c_recv=vm((3, 384, d), BF16),
        c_sum=vm((2, 384, d), BF16),
        **halving_scratch("e1", 384),
        **halving_scratch("e2", 384),
        **halving_scratch("wa", 384),
        **halving_scratch("wb", 384),
        sv=vm((4, 8, d), F32),
        sv_recv=vm((3, 8, d), F32),
        **{"v_" + name: vm((4 * d if name == "expand_bias" else d,), BF16) for name in VECTORS},
        v_clip_ids=vm((1, row), jnp.int32),
        v_block_order=pltpu.SMEM((1, 4), jnp.int32),
        block_out=vm((TOK, d), BF16),
        token_grad=vm((TOK, d), BF16),
        ffc=vm((384, d), BF16),
        e1g=vm((4, 96, 384), BF16),
        e2g=vm((4, 96, 384), BF16),
        wag=vm((4, 96, 384), BF16),
        wbg=vm((4, 96, 384), BF16),
        svg=vm((4, 8, d), F32),
        local_sem=pltpu.SemaphoreType.DMA((32,)),
        send_sem=pltpu.SemaphoreType.DMA((128,)),
        recv_sem=pltpu.SemaphoreType.DMA((128,)),
    )


INPUTS = [
    "tokens",
    "early_gain",
    "early_shift",
    "query_weight",
    "query_bias",
    "key_weight",
    "value_weight",
    "value_bias",
    "output_weight",
    "output_bias",
    "late_gain",
    "late_shift",
    "expand_weight",
    "expand_bias",
    "contract_weight",
    "contract_bias",
    "upstream",
    "clip_ids",
    "block_order",
]
VECTORS = [
    "early_gain",
    "early_shift",
    "query_bias",
    "value_bias",
    "output_bias",
    "late_gain",
    "late_shift",
    "expand_bias",
    "contract_bias",
]
RESULTS = ["block_out", "token_grad", "ffc", "e1g", "e2g", "wag", "wbg", "svg"]


def layer_kernel(names, *refs):
    r = types.SimpleNamespace(**dict(zip(names, refs)))
    d_model = 768
    row = 4 * TOK
    dp, blk = lax.axis_index("dp"), lax.axis_index("blk")
    core, chip = blk % 2, blk // 2
    sibling, across = blk + 1 - 2 * core, (blk + 2) % 4
    y, z = dp % 2, dp // 2
    z0, z1 = z % 2, z // 2
    to_core = {"dp": dp, "blk": sibling}
    to_x = {"dp": dp, "blk": across}
    to_y = {"dp": dp + 1 - 2 * y, "blk": blk}
    to_z0 = {"dp": dp + 2 - 4 * z0, "blk": blk}
    to_z1 = {"dp": (dp + 4) % 8, "blk": blk}
    far = (sibling + 2) % 4
    to_far = {"dp": dp, "blk": far}
    peers = (to_core, to_x, to_far, to_y, to_z0, to_z1)
    numbers = itertools.count()
    sent = []

    def remote(source, target, peer):
        number = next(numbers)
        assert number < 128
        return pltpu.make_async_remote_copy(
            src_ref=source,
            dst_ref=target,
            send_sem=r.send_sem.at[number],
            recv_sem=r.recv_sem.at[number],
            device_id=peer,
            device_id_type=MESH,
        )

    def send(source, target, peer):
        copy = remote(source, target, peer)
        copy.start()
        sent.append(copy)
        return copy

    def rows_at(ref, size, base=0):
        return lambda index: ref.at[pl.ds(pl.multiple_of(base + index * size, size), size)]

    def gather(source, place):
        over_x = send(source, place(blk), to_x)
        over_core = send(source, place(blk), to_core)
        return over_x, over_core, place

    def forward(gathering):
        over_x, over_core, place = gathering
        over_x.wait_recv()
        return send(place(across), place(across), to_core)

    written = []

    def write_out(name):
        copy = pltpu.make_async_copy(
            getattr(r, name), getattr(r, "out_" + name), r.local_sem.at[24 + len(written)]
        )
        copy.start()
        written.append(copy)

    half = 512 + 128 * chip
    tile_at = pl.ds(pl.multiple_of(128 * blk, 128), 128)
    half_at = pl.ds(pl.multiple_of(half, 128), 128)
    ff_at = pl.ds(pl.multiple_of(768 * blk, 128), 768)
    own_rows = pl.ds(pl.multiple_of(TOK * blk, TOK), TOK)
    local = [
        (r.tokens.at[0], r.x_all.at[own_rows]),
        (r.query_weight.at[:, tile_at], r.wab.at[:, 0:128]),
        (r.key_weight.at[:, tile_at], r.wab.at[:, 128:256]),
        (r.value_weight.at[:, tile_at], r.wab.at[:, 256:384]),
        (r.query_weight.at[:, half_at], r.wb_tile.at[0]),
        (r.key_weight.at[:, half_at], r.wb_tile.at[1]),
        (r.value_weight.at[:, half_at], r.wb_tile.at[2]),
        (r.output_weight, r.wo),
        (r.upstream.at[0], r.u_all.at[own_rows]),
        (r.contract_weight.at[ff_at], r.w2),
        (r.expand_weight.at[:, ff_at], r.w1),
    ]
    local += [
        (getattr(r, name), getattr(r, "v_" + name))
        for name in VECTORS + ["clip_ids", "block_order"]
    ]
    loads = []
    for number, (source, target) in enumerate(local):
        copy = pltpu.make_async_copy(source, target, r.local_sem.at[number])
        copy.start()
        loads.append(copy)

    barrier = pltpu.get_barrier_semaphore()
    for peer in peers:
        pl.semaphore_signal(barrier, inc=1, device_id=peer, device_id_type=MESH)
    pl.semaphore_wait(barrier, len(peers))

    tokens_in = gather(r.tokens.at[0], rows_at(r.x_all, TOK))
    upstream_in = gather(r.upstream.at[0], rows_at(r.u_all, TOK))

    for copy in loads[11:]:
        copy.wait()
    early_gain, early_shift = row_of(r.v_early_gain), row_of(r.v_early_shift)
    late_gain, late_shift = row_of(r.v_late_gain), row_of(r.v_late_shift)

    def picked(vector, size, base, width):
        total = jnp.zeros((1, width), F32)
        for index in range(4):
            begin = base + size * index
            total = total + jnp.where(blk == index, vector[:, begin : begin + width], 0.0)
        return total

    query_bias, value_bias = row_of(r.v_query_bias), row_of(r.v_value_bias)
    bias_qkv = jnp.concatenate(
        [
            picked(query_bias, 128, 0, 128),
            jnp.zeros((1, 128), F32),
            picked(value_bias, 128, 0, 128),
            picked(query_bias, 64, 512, 64),
            jnp.zeros((1, 64), F32),
            picked(value_bias, 64, 512, 64),
        ],
        axis=1,
    )

    lane = lax.broadcasted_iota(jnp.int32, (1, TOK), 1)
    keys_of, low_of = [], []
    for index in range(4):
        place = r.v_block_order[0, index]
        clip = jnp.zeros((1, TOK), jnp.int32)
        for other in range(4):
            clip = clip + jnp.where(
                place == other, r.v_clip_ids[0:1, other * TOK : (other + 1) * TOK], 0
            )
        low_of.append((clip * row).astype(F32))
        keys_of.append((clip * row + place * TOK + lane).astype(F32))
    for key in range(4):
        column = jnp.broadcast_to(keys_of[key], (TOK, TOK)).T
        for query in range(4):
            allowed = (column <= keys_of[query]) & (column >= low_of[query])
            r.mask[key * TOK : (key + 1) * TOK, query * TOK : (query + 1) * TOK] = jnp.where(
                allowed, 0.0, MASKED
            )

    for copy in loads[1:7]:
        copy.wait()
    for index in range(3):
        tile = r.wb_tile[index].astype(F32)
        piece = jnp.where(core == 1, tile[:, 64:128], tile[:, 0:64])
        r.wab[:, 384 + 64 * index : 448 + 64 * index] = piece.astype(BF16)

    def early_norm(start):
        def body(at):
            normed, _ = norm_stats(r.x_all[pl.ds(at, 32), :].astype(F32))
            r.normed[pl.ds(at, 32), :] = normed
            r.first[pl.ds(at, 32), :] = (normed * early_gain + early_shift).astype(BF16)

        by_rows(start, TOK, 32, body, 4)

    def project(start):
        at = pl.ds(pl.multiple_of(start, 2 * TOK), 2 * TOK)
        out = mm(r.first[at, :], r.wab[...], 1, 0) + bias_qkv
        for head, offset, step in ((0, 0, 128), (1, 64, 128), (2, 384, 64)):
            query = out[:, offset : offset + 64]
            r.qh[head, at, :] = (query * 0.125).astype(BF16)
            r.kh[head, at, :] = out[:, offset + step : offset + step + 64].astype(BF16)
            r.vh[head, at, :] = out[:, offset + 2 * step : offset + 2 * step + 64].astype(BF16)

    loads[0].wait()
    early_norm(TOK * blk)
    tokens_in[1].wait_recv()
    early_norm(TOK * sibling)
    project(2 * TOK * chip)
    token_forward = forward(tokens_in)
    early_norm(TOK * across)
    token_forward.wait_recv()
    early_norm(TOK * ((sibling + 2) % 4))
    project(2 * TOK * (1 - chip))

    def attend(head):
        r.st[...] = mm(r.kh[head], r.qh[head], 1, 1)

        @pl.loop(0, 4, unroll=2)
        def _(strip):
            at = pl.ds(pl.multiple_of(strip * TOK, TOK), TOK)
            scores = r.st[:, at] + r.mask[:, at]
            powers = jnp.exp(scores - jnp.max(scores, axis=0, keepdims=True))
            probs = powers * (1.0 / jnp.sum(powers, axis=0, keepdims=True))
            r.pf[head, :, at] = probs
            r.pb[head, :, at] = probs.astype(BF16)

        r.vt[head] = r.vh[head].T
        return mm(r.vt[head], r.pb[head], 1, 0).astype(BF16)

    places = (
        lambda index: pl.multiple_of(128 * index, 64),
        lambda index: pl.multiple_of(128 * index + 64, 64),
        lambda index: pl.multiple_of(512 + 64 * index, 64),
    )

    def head_at(head):
        return lambda index: r.at.at[pl.ds(places[head](index), 64)]

    def attend_and_send(head):
        r.at[pl.ds(places[head](blk), 64), :] = attend(head)
        return gather(head_at(head)(blk), head_at(head))

    start_pair = pl.multiple_of(128 * blk, 128)
    heads_in = [attend_and_send(0)]
    upstream_forward = forward(upstream_in)
    heads_in += [attend_and_send(1), attend_and_send(2)]

    loads[8].wait()
    loads[9].wait()
    upstream_in[1].wait_recv()
    upstream_forward.wait_recv()
    head_forwards = []
    for tile in range(3):
        at = slice(256 * tile, 256 * (tile + 1))
        r.ga[:, at] = mm(r.u_all[...], r.w2[at, :], 1, 1)
        head_forwards.append(forward(heads_in[tile]))
    r.first_t[...] = r.first[...].T
    for head in range(3):
        r.kt[head] = r.kh[head].T
    loads[7].wait()
    loads[10].wait()
    for head in range(3):
        heads_in[head][1].wait_recv()
        head_forwards[head].wait_recv()

    output_bias = row_of(r.v_output_bias)

    @pl.loop(0, 2)
    def _(tile):
        at = pl.ds(pl.multiple_of(tile * 256, 256), 256)
        r.mid[at, :] = mm(r.at[:, at], r.wo[...], 0, 0)

    def late_norm(at):
        at = pl.ds(at, 32)
        middle = r.mid[at, :] + r.x_all[at, :].astype(F32) + output_bias
        r.mid[at, :] = middle
        normed, _ = norm_stats(middle)
        r.second[at, :] = (normed * late_gain + late_shift).astype(BF16)

    by_rows(0, row, 32, late_norm, 4)

    for tile in range(3):
        at = slice(256 * tile, 256 * (tile + 1))
        r.hid[:, at] = mm(r.second[...], r.w1[:, at], 1, 0)

    expand_bias = picked(row_of(r.v_expand_bias), 768, 0, 768)
    first_factor = 0.7978845608028654
    third_factor = 0.044715

    def gelu(at):
        at = pl.ds(at, 16)
        hidden = r.hid[at, :] + expand_bias
        square = hidden * hidden
        bent = jnp.tanh(first_factor * hidden * (1.0 + third_factor * square))
        grown = 0.5 * (1.0 + bent)
        r.act[at, :] = (hidden * grown).astype(BF16)
        slope = grown + (0.5 * first_factor) * hidden * (1.0 - bent * bent) * (
            1.0 + (3.0 * third_factor) * square
        )
        r.gh[at, :] = (r.ga[at, :] * slope).astype(BF16)

    by_rows(0, row, 16, gelu, 4)

    def contract_half(which):
        at = pl.ds(pl.multiple_of(384 * which, 384), 384)
        return mm(r.act[:, at], r.u_all[...], 0, 0)

    piece = 384 // PIECES
    pieces = [pl.ds(p * piece, piece) for p in range(PIECES)]

    r.c_send[...] = contract_half(1 - y).astype(BF16)
    c_y = [send(r.c_send.at[at], r.c_recv.at[0, at], to_y) for at in pieces]

    def block_rows(block):
        return pl.ds(pl.multiple_of(block * TOK, TOK), TOK)

    def two_blocks(ref, first, second):
        return jnp.concatenate([ref[block_rows(first), :], ref[block_rows(second), :]], axis=0)

    def scatter_send(number, index):
        return send(r.rs_send.at[number, index], r.rs_recv.at[number, index], to_core)

    def part_pair(grads, weight, first, second):
        @pl.loop(0, 3)
        def _(tile):
            at = pl.ds(pl.multiple_of(tile * 256, 256), 256)
            value = mm(two_blocks(grads, first, second), weight[at, :], 1, 1)
            r.part[block_rows(first), at] = value[0:TOK]
            r.part[block_rows(second), at] = value[TOK : 2 * TOK]

    def part_start(number, grads, weight):
        part_pair(grads, weight, far, sibling)
        copies = scatter_start(number, r.part)
        part_pair(grads, weight, across, blk)
        return copies

    def scatter_start(number, part):
        copies = [None, None]
        for index, block in ((1, far), (0, sibling)):
            r.rs_send[number, index] = part[block_rows(block), :].astype(BF16)
            copies[index] = scatter_send(number, index)
        return copies

    def scatter_middle(number, part, copies):
        at = pl.ds(pl.multiple_of(across * TOK, TOK), TOK)
        copies[1].wait_recv()
        r.rs_send[number, 2] = (part[at, :] + r.rs_recv[number, 1].astype(F32)).astype(BF16)
        copies.append(send(r.rs_send.at[number, 2], r.rs_recv.at[number, 2], to_x))

    def scatter_end(copies):
        copies[0].wait_recv()
        copies[2].wait_recv()

    def scattered(number, part, at, size):
        own = pl.ds(pl.multiple_of(blk * TOK + at, size), size)
        here = pl.ds(at, size)
        return (
            part[own, :]
            + r.rs_recv[number, 0, here, :].astype(F32)
            + r.rs_recv[number, 2, here, :].astype(F32)
        )

    def added(target, left, right):
        rows = target.shape[0]

        @pl.loop(0, rows // 32, unroll=3)
        def _(index):
            at = pl.ds(pl.multiple_of(index * 32, 32), 32)
            target[at, :] = (left[at, :].astype(F32) + right[at, :].astype(F32)).astype(target.dtype)

    along_y, along_z0, along_z1 = (y, 1, to_y), (z0, 2, to_z0), (z1, 4, to_z1)

    def halving(name, stages):
        buf, r1, s1, r2, s2 = (
            getattr(r, name + key) for key in ("_buf", "_r1", "_s1", "_r2", "_s2")
        )
        own = [bit * weight for bit, weight, _ in stages]
        other = [(1 - bit) * weight for bit, weight, _ in stages]
        rest = [
            later + last
            for later in (other[1], own[1])
            for last in (other[2], own[2])
        ]
        copies = {}

        def start1():
            copies[1] = [
                send(buf.at[other[0] + rest[index]], r1.at[index], stages[0][2])
                for index in range(4)
            ]

        def end1(*indices):
            for index in indices:
                copies[1][index].wait_recv()
                added(s1.at[index], buf.at[own[0] + rest[index]], r1.at[index])

        def start2():
            copies[2] = [send(s1.at[index], r2.at[index], stages[1][2]) for index in range(2)]

        def start3():
            copies[2][0].wait_recv()
            added(s2.at[0], s1.at[2], r2.at[0])
            copies[3] = send(s2.at[0], r2.at[2], stages[2][2])
            copies[2][1].wait_recv()
            added(s2.at[1], s1.at[3], r2.at[1])

        def finish(target):
            copies[3].wait_recv()
            added(target.at[blk], s2.at[1], r2.at[2])
            place = lambda index: target.at[index]
            return gather(place(blk), place)

        return types.SimpleNamespace(
            start1=start1, end1=end1, start2=start2, start3=start3, finish=finish
        )

    e1 = halving("e1", (along_z0, along_z1, along_y))
    e2 = halving("e2", (along_y, along_z0, along_z1))
    wa = halving("wa", (along_y, along_z0, along_z1))
    wb = halving("wb", (along_y, along_z0, along_z1))

    def expand_part(target, columns):
        for which in range(2):
            block = mm(r.second[:, 384 * which : 384 * (which + 1)], r.gh[:, columns], 0, 0)
            target[4 * which : 4 * which + 4] = block.astype(BF16).reshape(4, 96, 384)

    second_sum = part_start(0, r.gh, r.w1)
    scatter_middle(0, r.part, second_sum)
    expand_part(r.e1_buf, slice(0, 384))
    e1.start1()
    r.c_own[...] = contract_half(y)
    expand_part(r.e2_buf, slice(384, 768))
    e2.start1()

    for tile in range(3):
        at = slice(256 * tile, 256 * (tile + 1))
        r.part_out[:, at] = mm(r.act[...], r.w2[:, at], 1, 0)

    out_sum = scatter_start(1, r.part_out)

    scatter_end(second_sum)
    own_start = blk * TOK
    r.sv[0] = jnp.zeros((8, d_model), F32)

    def late_pull(index, carry):
        gain_sum, shift_sum, output_sum, contract_sum = carry
        at = pl.multiple_of(index * 32, 32)
        own = pl.ds(pl.multiple_of(own_start + at, 32), 32)
        grad = scattered(0, r.part, at, 32)
        normed, inverse = norm_stats(r.mid[own, :])
        upstream = r.u_all[own, :].astype(F32)
        middle = upstream + norm_pull(grad, normed, inverse, late_gain)
        r.g_mid[pl.ds(at, 32), :] = middle
        low = middle.astype(BF16)
        r.gb[own, :] = low
        return (
            gain_sum + folded(grad * normed),
            shift_sum + folded(grad),
            output_sum + folded(low.astype(F32)),
            contract_sum + folded(upstream),
        )

    nothing = jnp.zeros((8, d_model), F32)
    sums = lax.fori_loop(0, TOK // 32, late_pull, (nothing,) * 4, unroll=2)

    pulled = mm(r.gb[own_rows, :], r.wo[...], 1, 1)
    r.go_send[...] = pulled[:, 0:512].astype(BF16)
    for index in range(4):
        r.third_send[index] = pulled[:, 512 + 64 * index : 576 + 64 * index].astype(BF16)
    head_grads = []
    for block, peer in ((far, to_far), (across, to_x), (sibling, to_core)):
        lanes = pl.ds(pl.multiple_of(128 * block, 128), 128)
        head_grads.append(send(r.go_send.at[:, lanes], r.go_pair.at[own_rows], peer))
        head_grads.append(send(r.third_send.at[block], r.go.at[2, own_rows], peer))
    r.go_pair[own_rows, :] = r.go_send[:, tile_at]
    r.go[2, own_rows, :] = r.third_send[blk]
    branch_at = rows_at(r.gb, TOK)
    branch_in = gather(branch_at(blk), branch_at)
    for index, value in zip((3, 4, 2, 5), sums):
        r.sv[0, index : index + 1, :] = jnp.sum(value, axis=0, keepdims=True)

    e1.end1(0, 1)
    e1.start2()

    root0, root1 = blk % 2, blk // 2
    keeps0 = z0 == root0
    keeps1 = z1 == root1
    is_root = z == blk
    is_across = z == across
    c_z0 = [remote(r.c_sum.at[0, at], r.c_recv.at[1, at], to_z0) for at in pieces]
    c_z1 = [remote(r.c_sum.at[1, at], r.c_recv.at[2, at], to_z1) for at in pieces]
    c_x = [remote(r.ffc.at[at], r.ffc.at[at], to_x) for at in pieces]
    c_core = [remote(r.ffc.at[at], r.ffc.at[at], to_core) for at in pieces]

    def contract_y_end(p):
        c_y[p].wait_recv()
        added(r.c_sum.at[0, pieces[p]], r.c_own.at[pieces[p]], r.c_recv.at[0, pieces[p]])

        @pl.when(jnp.logical_not(keeps0))
        def _():
            c_z0[p].start()

    def contract_z0_end(p):
        @pl.when(keeps0)
        def _():
            c_z0[p].wait_recv()
            added(r.c_sum.at[1, pieces[p]], r.c_sum.at[0, pieces[p]], r.c_recv.at[1, pieces[p]])

            @pl.when(jnp.logical_not(keeps1))
            def _():
                c_z1[p].start()

    def contract_z1_end(p):
        @pl.when(is_root)
        def _():
            c_z1[p].wait_recv()
            added(r.ffc.at[pieces[p]], r.c_sum.at[1, pieces[p]], r.c_recv.at[2, pieces[p]])
            c_x[p].start()
            c_core[p].start()

    e1.end1(2, 3)
    contract_y_end(0)

    def expand_sum(index, carry):
        at = pl.ds(pl.multiple_of(index * 32, 32), 32)
        return carry + folded(r.gh[at, :].astype(F32))

    r.sv[0, 6:7, :] = jnp.sum(
        lax.fori_loop(0, row // 32, expand_sum, nothing, unroll=4), axis=0, keepdims=True
    )
    for copy in head_grads:
        copy.wait_recv()
    r.go[0] = r.go_pair[:, 0:64]
    r.go[1] = r.go_pair[:, 64:128]

    def attend_back(head, offset, step):
        r.st[...] = mm(r.vh[head], r.go[head], 1, 1)

        @pl.loop(0, 4, unroll=2)
        def _(strip):
            at = pl.ds(pl.multiple_of(strip * TOK, TOK), TOK)
            probs, grad = r.pf[head, :, at], r.st[:, at]
            delta = jnp.sum(probs * grad, axis=0, keepdims=True)
            r.sg[:, at] = (probs * (grad - delta)).astype(BF16)

        query = mm(r.kt[head], r.sg[...], 1, 0) * 0.125
        r.gqkv[:, offset : offset + 64] = query.T.astype(BF16)
        r.gqkv[:, offset + step : offset + step + 64] = mm(
            r.sg[...], r.qh[head], 1, 0
        ).astype(BF16)
        r.gqkv[:, offset + 2 * step : offset + 2 * step + 64] = mm(
            r.pb[head], r.go[head], 1, 0
        ).astype(BF16)

    halves = [(slice(4 * w, 4 * w + 4), slice(384 * w, 384 * (w + 1))) for w in range(2)]
    contract_y_end(1)
    attend_back(0, 0, 128)
    contract_z0_end(0)
    attend_back(1, 64, 128)
    for blocks, at in halves:
        block = mm(r.first_t[at, :], r.gqkv[:, 0:384], 1, 0)
        r.wa_buf[blocks] = block.astype(BF16).reshape(4, 96, 384)
    wa.start1()
    scatter_middle(1, r.part_out, out_sum)
    branch_forward = forward(branch_in)
    e1.start3()
    attend_back(2, 384, 64)
    contract_z0_end(1)
    e2.end1(0, 1)
    e2.start2()

    def qkv_sum(index, carry):
        gain_sum, shift_sum, bias_sum = carry
        at = pl.ds(pl.multiple_of(index * 32, 32), 32)
        part = r.part[at, :]
        return (
            gain_sum + folded(part * r.normed[at, :]),
            shift_sum + folded(part),
            bias_sum + folded(r.gqkv[at, :].astype(F32)),
        )

    first_sum = part_start(2, r.gqkv, r.wab)
    scatter_middle(2, r.part, first_sum)
    sums = lax.fori_loop(
        0, row // 32, qkv_sum, (nothing, nothing, jnp.zeros((8, 576), F32)), unroll=2
    )
    for index in range(2):
        r.sv[0, index : index + 1, :] = jnp.sum(sums[index], axis=0, keepdims=True)
    total = jnp.sum(sums[2], axis=0, keepdims=True)
    r.sv[0, 7:8, 0:384] = total[:, 0:384]
    r.sv[0, 7:8, 512:704] = total[:, 384:576]
    v_y = send(r.sv.at[0], r.sv_recv.at[0], to_y)

    branch_in[1].wait_recv()
    branch_forward.wait_recv()
    r.gbt[:, 0:128] = r.gb[:, tile_at]
    r.gbt[:, 128:256] = r.gb[:, half_at]
    for blocks, at in halves:
        block = mm(r.first_t[at, :], r.gqkv[:, 384:576], 1, 0)
        r.wb_buf[blocks, :, 0:192] = block.astype(BF16).reshape(4, 96, 192)
        block = mm(r.at[at, :], r.gbt[...], 1, 0)
        chosen = jnp.where(core == 1, block[:, 192:256], block[:, 128:192])
        r.wb_buf[blocks, :, 192:256] = chosen.astype(BF16).reshape(4, 96, 64)
        r.wb_buf[blocks, :, 256:384] = block[:, 0:128].astype(BF16).reshape(4, 96, 128)
    wb.start1()
    contract_z1_end(0)
    e2.end1(2, 3)

    scatter_end(out_sum)
    contract_bias = row_of(r.v_contract_bias)

    @pl.loop(0, TOK // 32, unroll=2)
    def _(index):
        at = pl.multiple_of(index * 32, 32)
        own = pl.ds(pl.multiple_of(own_start + at, 32), 32)
        value = scattered(1, r.part_out, at, 32) + r.mid[own, :] + contract_bias
        r.block_out[pl.ds(at, 32), :] = value.astype(BF16)

    write_out("block_out")
    v_y.wait_recv()
    r.sv[1] = r.sv[0] + r.sv_recv[0]
    v_z0 = send(r.sv.at[1], r.sv_recv.at[1], to_z0)
    wa.end1(0, 1)
    wa.start2()
    wa.end1(2, 3)
    e2.start3()

    scatter_end(first_sum)

    @pl.loop(0, TOK // 32, unroll=2)
    def _(index):
        at = pl.multiple_of(index * 32, 32)
        own = pl.ds(pl.multiple_of(own_start + at, 32), 32)
        here = pl.ds(at, 32)
        grad = scattered(2, r.part, at, 32)
        normed, inverse = norm_stats(r.x_all[own, :].astype(F32))
        pulled = norm_pull(grad, normed, inverse, early_gain)
        r.token_grad[here, :] = (r.g_mid[here, :] + pulled).astype(BF16)

    write_out("token_grad")
    e1_in = e1.finish(r.e1g)
    v_z0.wait_recv()
    r.sv[2] = r.sv[1] + r.sv_recv[1]
    v_z1 = send(r.sv.at[2], r.sv_recv.at[2], to_z1)
    contract_z1_end(1)
    wb.end1(0, 1)
    wb.start2()
    wb.end1(2, 3)
    e2_in = e2.finish(r.e2g)
    wa.start3()

    @pl.when(is_across)
    def _():
        for p in range(PIECES):
            c_x[p].wait_recv()
            c_core[p].start()

    e1_forward = forward(e1_in)
    v_z1.wait_recv()
    r.svg[blk] = r.sv[2] + r.sv_recv[2]
    v_at = lambda index: r.svg.at[index]
    v_in = gather(v_at(blk), v_at)
    wb.start3()
    e2_forward = forward(e2_in)
    wa_in = wa.finish(r.wag)

    @pl.when(jnp.logical_not(jnp.logical_or(is_root, is_across)))
    def _():
        for p in range(PIECES):
            c_core[p].wait_recv()

    write_out("ffc")
    v_forward = forward(v_in)
    wb_in = wb.finish(r.wbg)
    wa_forward = forward(wa_in)
    wb_forward = forward(wb_in)
    for name, gathering, copy in (
        ("e1g", e1_in, e1_forward),
        ("e2g", e2_in, e2_forward),
        ("svg", v_in, v_forward),
        ("wag", wa_in, wa_forward),
        ("wbg", wb_in, wb_forward),
    ):
        gathering[1].wait_recv()
        copy.wait_recv()
        write_out(name)

    for copy in written:
        copy.wait()

    for copy in sent:
        copy.wait_send()

    @pl.when(jnp.logical_not(keeps0))
    def _():
        for copy in c_z0:
            copy.wait_send()

    @pl.when(jnp.logical_and(keeps0, jnp.logical_not(keeps1)))
    def _():
        for copy in c_z1:
            copy.wait_send()

    @pl.when(is_root)
    def _():
        for copy in c_x:
            copy.wait_send()

    @pl.when(jnp.logical_or(is_root, is_across))
    def _():
        for copy in c_core:
            copy.wait_send()


def write_kernel(*refs):
    count, sources, outs = len(RESULTS), refs[: len(RESULTS)], refs[len(RESULTS) :][:17]
    held, made = refs[count + 17 :][:count], refs[2 * count + 17 :][:15]
    in_sem, out_sem = refs[-2:]
    (gain_early, shift_early, query_grad, bias_query, key_grad, value_grad) = made[:6]
    (bias_value, output_grad, bias_output, gain_late, shift_late, expand_grad, bias_expand) = made[6:13]
    contract_grad, bias_contract = made[13:]
    dp = lax.axis_index("dp")
    loads = [
        pltpu.make_async_copy(source, target, in_sem.at[number])
        for number, (source, target) in enumerate(zip(sources, held))
    ]
    for number in (3, 4, 2, 5, 6, 7, 0, 1):
        loads[number].start()
    block_out, token_grad, ffc, e1g, e2g, wag, wbg, svg = held
    left = []

    def leave(target):
        number = [item is target for item in made].index(True)
        copy = pltpu.make_async_copy(target, outs[number + 2], out_sem.at[number + 2])
        copy.start()
        left.append(copy)

    for copy in loads[3:5]:
        copy.wait()
    for index in range(4):
        expand_grad[:, 768 * index : 768 * index + 384] = e1g[index].astype(F32)
        expand_grad[:, 768 * index + 384 : 768 * (index + 1)] = e2g[index].astype(F32)
    leave(expand_grad)
    loads[2].wait()
    contract_grad[...] = ffc[...].astype(F32)
    leave(contract_grad)
    for copy in loads[5:7]:
        copy.wait()
    for number, target in enumerate((query_grad, key_grad, value_grad, output_grad)):
        for index in range(4):
            wide = slice(128 * index, 128 * (index + 1))
            narrow = slice(512 + 64 * index, 576 + 64 * index)
            if number < 3:
                target[:, wide] = wag[index, :, 128 * number : 128 * (number + 1)].astype(F32)
            else:
                target[:, wide] = wbg[index, :, 256:384].astype(F32)
            target[:, narrow] = wbg[index, :, 64 * number : 64 * (number + 1)].astype(F32)
        leave(target)
    loads[7].wait()
    summed = svg[0] + svg[1] + svg[2] + svg[3]
    query_row = jnp.concatenate(
        [svg[i, 7:8, 0:128] for i in range(4)] + [svg[i, 7:8, 512:576] for i in range(4)], axis=1
    )
    value_row = jnp.concatenate(
        [svg[i, 7:8, 256:384] for i in range(4)] + [svg[i, 7:8, 640:704] for i in range(4)], axis=1
    )
    rows = jnp.concatenate([summed[0:6], query_row, value_row], axis=0)
    turned = pltpu.roll(rows, 768 - 96 * dp, 1)
    targets = (gain_early, shift_early, bias_output, gain_late, shift_late, bias_contract)
    for number, target in enumerate(targets + (bias_query, bias_value)):
        target[...] = turned[number, 0:96]
        leave(target)
    hidden = jnp.zeros((8, 768), F32)
    for index in range(4):
        hidden = hidden + jnp.where(dp // 2 == index, svg[index], 0.0)
    bias_expand[...] = pltpu.roll(hidden, 768 - 384 * (dp % 2), 1)[6, 0:384]
    leave(bias_expand)
    for number, value in enumerate((block_out, token_grad)):
        loads[number].wait()
        copy = pltpu.make_async_copy(value, outs[number].at[0], out_sem.at[number])
        copy.start()
        left.append(copy)
    for copy in left:
        copy.wait()


def fast_local(*arguments):
    scratch = fast_scratch()
    away = pl.BlockSpec(memory_space=pl.ANY)
    shape = jax.ShapeDtypeStruct
    results = (
        shape((TOK, 768), BF16),
        shape((TOK, 768), BF16),
        shape((384, 768), BF16),
        shape((4, 96, 384), BF16),
        shape((4, 96, 384), BF16),
        shape((4, 96, 384), BF16),
        shape((4, 96, 384), BF16),
        shape((4, 8, 768), F32),
    )
    names = INPUTS + ["out_" + name for name in RESULTS] + list(scratch)
    moved = pl.pallas_call(
        functools.partial(layer_kernel, names),
        name="layer",
        out_shape=results,
        in_specs=[away] * len(INPUTS),
        out_specs=(away,) * len(results),
        scratch_shapes=list(scratch.values()),
        compiler_params=pltpu.CompilerParams(
            collective_id=0, has_side_effects=True, vmem_limit_bytes=56 << 20
        ),
    )(*arguments)
    outs = (
        [shape((1, TOK, 768), BF16)] * 2
        + [shape((96,), F32)] * 2
        + [shape((96, 768), F32), shape((96,), F32), shape((96, 768), F32), shape((96, 768), F32)]
        + [shape((96,), F32), shape((96, 768), F32)]
        + [shape((96,), F32)] * 3
        + [shape((96, 3072), F32), shape((384,), F32), shape((384, 768), F32), shape((96,), F32)]
    )
    return pl.pallas_call(
        write_kernel,
        name="write",
        out_shape=tuple(outs),
        in_specs=[away] * len(results),
        out_specs=(away,) * len(outs),
        scratch_shapes=[pltpu.VMEM(item.shape, item.dtype) for item in results]
        + [pltpu.VMEM(item.shape, item.dtype) for item in outs[2:]]
        + [pltpu.SemaphoreType.DMA((8,)), pltpu.SemaphoreType.DMA((17,))],
        compiler_params=pltpu.CompilerParams(vmem_limit_bytes=60 << 20),
    )(*moved)


def passed_along(value, axis, steps):
    count = lax.axis_size(axis)
    pairs = [(source, (source + steps) % count) for source in range(count)]
    return lax.ppermute(value, axis, pairs)


def layer_norm(inputs, gain, shift):
    average = jnp.mean(inputs, axis=-1, keepdims=True)
    centred = inputs - average
    inverse = lax.rsqrt(jnp.mean(centred * centred, axis=-1, keepdims=True) + EPSILON)
    normed = centred * inverse
    return (normed * gain + shift, normed, inverse)


def norm_back(grad_out, normed, inverse, gain):
    scaled = grad_out * gain
    inner = (
        scaled
        - jnp.mean(scaled, axis=-1, keepdims=True)
        - normed * jnp.mean(scaled * normed, axis=-1, keepdims=True)
    )
    return (
        inverse * inner,
        jnp.sum(grad_out * normed, axis=(0, 1)),
        jnp.sum(grad_out, axis=(0, 1)),
    )


def project(inputs, weight):
    return jnp.einsum("rtd,de->rte", inputs, weight, preferred_element_type=jnp.float32)


def project_back(grad_rows, weight):
    return jnp.einsum("rte,de->rtd", grad_rows, weight, preferred_element_type=jnp.float32)


def weight_grad(inputs, grad_rows):
    return jnp.einsum("rtd,rte->de", inputs, grad_rows, preferred_element_type=jnp.float32)


def column_sum(grad_rows):
    return jnp.sum(grad_rows.astype(jnp.float32), axis=(0, 1))


def general_local(
    tokens,
    early_gain,
    early_shift,
    query_weight,
    query_bias,
    key_weight,
    value_weight,
    value_bias,
    output_weight,
    output_bias,
    late_gain,
    late_shift,
    expand_weight,
    expand_bias,
    contract_weight,
    contract_bias,
    upstream,
    clip_ids,
    block_order,
):
    row_count, block_len, features = tokens.shape
    head_count = HEADS
    head_size = features // head_count
    scale_factor = float(head_size) ** (-0.5)
    my_index = lax.axis_index("blk")
    group_size = lax.axis_size("blk")

    def positions(begin, length):
        stored = begin + jnp.arange(length, dtype=jnp.int32)
        logical = (
            jnp.take(block_order, stored // block_len, axis=1) * block_len + stored % block_len
        )
        return (logical, jnp.take_along_axis(clip_ids, logical, axis=1))

    query_pos, query_clip = positions(my_index * block_len, block_len)

    def visible(begin, length):
        key_pos, key_clip = positions(begin, length)
        allowed = (key_pos[:, None, :] <= query_pos[:, :, None]) & (
            key_clip[:, None, :] == query_clip[:, :, None]
        )
        return allowed[:, None]

    def split_heads(array):
        return array.reshape(row_count, array.shape[1], head_count, head_size)

    inputs = tokens.astype(jnp.float32)
    first_full, first_normed, first_inverse = layer_norm(
        inputs, early_gain.astype(jnp.float32), early_shift.astype(jnp.float32)
    )
    first_low = first_full.astype(jnp.bfloat16)
    queries = (project(first_low, query_weight) + query_bias.astype(jnp.float32)).astype(
        jnp.bfloat16
    )
    key_rows = project(first_low, key_weight).astype(jnp.bfloat16)
    value_rows = (project(first_low, value_weight) + value_bias.astype(jnp.float32)).astype(
        jnp.bfloat16
    )
    query_heads = split_heads(queries)

    def scores_of(key_block):
        return (
            jnp.einsum(
                "rqhe,rkhe->rhqk",
                query_heads,
                split_heads(key_block),
                preferred_element_type=jnp.float32,
            )
            * scale_factor
        )

    def absorb(carry, key_block, value_block, begin):
        allowed = visible(begin, key_block.shape[1])
        maximum, denominator, numerator = carry
        scores = jnp.where(allowed, scores_of(key_block), MASKED)
        new_max = jnp.maximum(maximum, jnp.max(scores, axis=-1))
        weights = jnp.where(allowed, jnp.exp(scores - new_max[..., None]), 0.0)
        factor = jnp.exp(maximum - new_max)
        update = jnp.einsum(
            "rhqk,rkhe->rqhe",
            weights.astype(jnp.bfloat16),
            split_heads(value_block),
            preferred_element_type=jnp.float32,
        )
        numerator = numerator * jnp.transpose(factor, (0, 2, 1))[..., None] + update
        return (new_max, denominator * factor + jnp.sum(weights, axis=-1), numerator)

    start_state = (
        jnp.full((row_count, head_count, block_len), MASKED, jnp.float32),
        jnp.zeros((row_count, head_count, block_len), jnp.float32),
        jnp.zeros((row_count, block_len, head_count, head_size), jnp.float32),
    )
    key_piece = lax.all_gather(key_rows, "blk", axis=1, tiled=True)
    value_piece = lax.all_gather(value_rows, "blk", axis=1, tiled=True)
    length = key_piece.shape[1]
    stride = min(length, block_len)

    def one_block(number, running):
        offset = number * stride
        return absorb(
            running,
            lax.dynamic_slice_in_dim(key_piece, offset, stride, 1),
            lax.dynamic_slice_in_dim(value_piece, offset, stride, 1),
            offset,
        )

    maximum, denominator, numerator = lax.fori_loop(0, length // stride, one_block, start_state)
    log_total = maximum + jnp.log(denominator)
    attention = numerator / jnp.transpose(denominator, (0, 2, 1))[..., None]
    attention_low = attention.reshape(row_count, block_len, features).astype(jnp.bfloat16)
    middle = inputs + project(attention_low, output_weight) + output_bias.astype(jnp.float32)
    second_full, second_normed, second_inverse = layer_norm(
        middle, late_gain.astype(jnp.float32), late_shift.astype(jnp.float32)
    )
    second_low = second_full.astype(jnp.bfloat16)
    hidden = project(second_low, expand_weight) + expand_bias.astype(jnp.float32)
    active_full, gelu_pull = jax.vjp(
        lambda values_in: jax.nn.gelu(values_in, approximate=True), hidden
    )
    active_low = active_full.astype(jnp.bfloat16)
    block_out = (
        middle + project(active_low, contract_weight) + contract_bias.astype(jnp.float32)
    ).astype(jnp.bfloat16)
    grad_out = upstream.astype(jnp.float32)
    contract_g = weight_grad(active_low, upstream)
    contract_b = column_sum(upstream)
    hidden_low = gelu_pull(project_back(upstream, contract_weight))[0].astype(jnp.bfloat16)
    expand_g = weight_grad(second_low, hidden_low)
    expand_b = column_sum(hidden_low)
    norm_grad, late_gain_g, late_shift_g = norm_back(
        project_back(hidden_low, expand_weight),
        second_normed,
        second_inverse,
        late_gain.astype(jnp.float32),
    )
    middle_grad = grad_out + norm_grad
    branch_low = middle_grad.astype(jnp.bfloat16)
    output_g = weight_grad(attention_low, branch_low)
    output_b = column_sum(branch_low)
    grad_heads = split_heads(project_back(branch_low, output_weight).astype(jnp.bfloat16))
    delta = jnp.transpose(jnp.sum(grad_heads.astype(jnp.float32) * attention, axis=-1), (0, 2, 1))

    def turn_step(number, carried):
        key_block, value_block, key_acc, value_acc, query_acc = carried
        source = (my_index - number) % group_size
        allowed = visible(source * block_len, block_len)
        use_key, use_value = (key_block, value_block)
        key_sum = key_acc
        value_sum = value_acc
        query_sum = query_acc
        probs = jnp.where(allowed, jnp.exp(scores_of(use_key) - log_total[..., None]), 0.0)
        value_sum = value_sum + jnp.einsum(
            "rhqk,rqhe->rkhe",
            probs.astype(jnp.bfloat16),
            grad_heads,
            preferred_element_type=jnp.float32,
        ).reshape(row_count, block_len, features)
        prob_grad = jnp.einsum(
            "rqhe,rkhe->rhqk",
            grad_heads,
            split_heads(use_value),
            preferred_element_type=jnp.float32,
        )
        score_grad = (probs * (prob_grad - delta[..., None])).astype(jnp.bfloat16)
        query_sum = (
            query_sum
            + jnp.einsum(
                "rhqk,rkhe->rqhe",
                score_grad,
                split_heads(use_key),
                preferred_element_type=jnp.float32,
            )
            * scale_factor
        )
        key_sum = key_sum + (
            jnp.einsum(
                "rhqk,rqhe->rkhe", score_grad, query_heads, preferred_element_type=jnp.float32
            )
            * scale_factor
        ).reshape(row_count, block_len, features)
        key_acc = key_sum
        value_acc = value_sum
        key_block, value_block = passed_along((key_block, value_block), "blk", 1)
        key_acc, value_acc = (
            passed_along(key_acc.astype(jnp.bfloat16), "blk", 1).astype(key_acc.dtype),
            passed_along(value_acc.astype(jnp.bfloat16), "blk", 1).astype(value_acc.dtype),
        )
        return (key_block, value_block, key_acc, value_acc, query_sum)

    zero_rows = jnp.zeros((row_count, block_len, features), jnp.float32)
    carried = (
        key_rows,
        value_rows,
        zero_rows,
        zero_rows,
        jnp.zeros((row_count, block_len, head_count, head_size), jnp.float32),
    )
    carried = lax.fori_loop(0, group_size, turn_step, carried)
    query_low = carried[4].reshape(row_count, block_len, features).astype(jnp.bfloat16)
    key_low = carried[2].astype(jnp.bfloat16)
    value_low = carried[3].astype(jnp.bfloat16)
    query_g = weight_grad(first_low, query_low)
    key_g = weight_grad(first_low, key_low)
    value_g = weight_grad(first_low, value_low)
    query_b = column_sum(query_low)
    value_b = column_sum(value_low)
    first_grad = (
        project_back(query_low, query_weight)
        + project_back(key_low, key_weight)
        + project_back(value_low, value_weight)
    )
    input_grad, early_gain_g, early_shift_g = norm_back(
        first_grad, first_normed, first_inverse, early_gain.astype(jnp.float32)
    )
    token_grad = (middle_grad + input_grad).astype(jnp.bfloat16)
    local_grads = (
        early_gain_g,
        early_shift_g,
        query_g,
        query_b,
        key_g,
        value_g,
        value_b,
        output_g,
        output_b,
        late_gain_g,
        late_shift_g,
        expand_g,
        expand_b,
        contract_g,
        contract_b,
    )
    owners = lax.axis_size("dp")
    laid_out = jnp.concatenate([member.reshape(owners, -1) for member in local_grads], axis=1)
    shares = lax.psum_scatter(laid_out.astype(jnp.bfloat16), "dp", scatter_dimension=0, tiled=True)
    summed = lax.psum(shares, "blk").astype(jnp.float32)
    pieces = []
    offset = 0
    for member in local_grads:
        width = member.size // owners
        own_shape = (member.shape[0] // owners,) + member.shape[1:]
        pieces.append(summed[0, offset : offset + width].reshape(own_shape))
        offset = offset + width
    return (block_out, token_grad) + tuple(pieces)


def solution(mesh):
    placed = (
        P("dp", "blk", None),
        P(),
        P(),
        P(),
        P(),
        P(),
        P(),
        P(),
        P(),
        P(),
        P(),
        P(),
        P(),
        P(),
        P(),
        P(),
        P("dp", "blk", None),
        P("dp", None),
        P("dp", None),
    )
    narrow = mesh.shape["dp"] == 8 and mesh.shape["blk"] == 4
    return jax.shard_map(
        fast_local if narrow else general_local,
        mesh=mesh,
        in_specs=placed,
        out_specs=(
            P("dp", "blk", None),
            P("dp", "blk", None),
            P("dp"),
            P("dp"),
            P("dp", None),
            P("dp"),
            P("dp", None),
            P("dp", None),
            P("dp"),
            P("dp", None),
            P("dp"),
            P("dp"),
            P("dp"),
            P("dp", None),
            P("dp"),
            P("dp", None),
            P("dp"),
        ),
        check_vma=False,
    )
```

```python
import functools
import itertools
import types

import jax
import jax.numpy as jnp
from jax import lax
from jax.experimental import pallas as pl
from jax.experimental.pallas import tpu as pltpu
from jax.sharding import PartitionSpec as P

HEADS = 12
EPSILON = 1e-05
MASKED = -1e30
F32 = jnp.float32
BF16 = jnp.bfloat16
MESH = pl.DeviceIdType.MESH
TOK = 128
PIECES = 2


def mm(left, right, left_dim, right_dim):
    return lax.dot_general(
        left, right, (((left_dim,), (right_dim,)), ((), ())), preferred_element_type=F32
    )


def norm_stats(value):
    centred = value - jnp.mean(value, axis=-1, keepdims=True)
    inverse = lax.rsqrt(jnp.mean(centred * centred, axis=-1, keepdims=True) + EPSILON)
    return centred * inverse, inverse


def norm_pull(grad, normed, inverse, gain):
    scaled = grad * gain
    return inverse * (
        scaled
        - jnp.mean(scaled, axis=-1, keepdims=True)
        - normed * jnp.mean(scaled * normed, axis=-1, keepdims=True)
    )


def row_of(ref):
    return ref[...].astype(F32).reshape(1, ref.shape[0])


def by_rows(start, count, step, body, unroll=2):
    @pl.loop(0, count // step, unroll=unroll)
    def _(index):
        body(pl.multiple_of(start + index * step, step))


def folded(value):
    rows, columns = value.shape
    return jnp.sum(value.reshape(rows // 8, 8, columns), axis=0)


def halving_scratch(name, width):
    sizes = {"_buf": 8, "_r1": 4, "_s1": 4, "_r2": 3, "_s2": 2}
    return {name + key: pltpu.VMEM((size, 96, width), BF16) for key, size in sizes.items()}


def fast_scratch():
    row, d = 4 * TOK, 768
    vm = pltpu.VMEM
    return dict(
        x_all=vm((row, d), BF16),
        u_all=vm((row, d), BF16),
        wab=vm((d, 576), BF16),
        wb_tile=vm((3, d, 128), BF16),
        wo=vm((d, d), BF16),
        w1=vm((d, d), BF16),
        w2=vm((d, d), BF16),
        first=vm((row, d), BF16),
        normed=vm((row, d), F32),
        first_t=vm((d, row), BF16),
        qh=vm((3, row, 64), BF16),
        kh=vm((3, row, 64), BF16),
        vh=vm((3, row, 64), BF16),
        kt=vm((3, 64, row), BF16),
        vt=vm((3, 64, row), BF16),
        mask=vm((row, row), F32),
        st=vm((row, row), F32),
        pf=vm((3, row, row), F32),
        pb=vm((3, row, row), BF16),
        sg=vm((row, row), BF16),
        at=vm((d, row), BF16),
        mid=vm((row, d), F32),
        second=vm((row, d), BF16),
        hid=vm((row, d), F32),
        ga=vm((row, d), F32),
        act=vm((row, d), BF16),
        gh=vm((row, d), BF16),
        part=vm((row, d), F32),
        part_out=vm((row, d), F32),
        rs_send=vm((3, 3, TOK, d), BF16),
        rs_recv=vm((3, 3, TOK, d), BF16),
        g_mid=vm((TOK, d), F32),
        gb=vm((row, d), BF16),
        gbt=vm((row, 256), BF16),
        go=vm((3, row, 64), BF16),
        go_pair=vm((row, 128), BF16),
        go_send=vm((TOK, 512), BF16),
        third_send=vm((4, TOK, 64), BF16),
        gqkv=vm((row, 576), BF16),
        c_send=vm((384, d), BF16),
        c_own=vm((384, d), F32),
        c_recv=vm((3, 384, d), BF16),
        c_sum=vm((2, 384, d), BF16),
        **halving_scratch("e1", 384),
        **halving_scratch("e2", 384),
        **halving_scratch("wa", 384),
        **halving_scratch("wb", 384),
        sv=vm((4, 8, d), F32),
        sv_recv=vm((3, 8, d), F32),
        **{"v_" + name: vm((4 * d if name == "expand_bias" else d,), BF16) for name in VECTORS},
        v_clip_ids=vm((1, row), jnp.int32),
        v_block_order=pltpu.SMEM((1, 4), jnp.int32),
        block_out=vm((TOK, d), BF16),
        token_grad=vm((TOK, d), BF16),
        ffc=vm((384, d), BF16),
        e1g=vm((4, 96, 384), BF16),
        e2g=vm((4, 96, 384), BF16),
        wag=vm((4, 96, 384), BF16),
        wbg=vm((4, 96, 384), BF16),
        svg=vm((4, 8, d), F32),
        local_sem=pltpu.SemaphoreType.DMA((32,)),
        send_sem=pltpu.SemaphoreType.DMA((128,)),
        recv_sem=pltpu.SemaphoreType.DMA((128,)),
    )


INPUTS = [
    "tokens",
    "early_gain",
    "early_shift",
    "query_weight",
    "query_bias",
    "key_weight",
    "value_weight",
    "value_bias",
    "output_weight",
    "output_bias",
    "late_gain",
    "late_shift",
    "expand_weight",
    "expand_bias",
    "contract_weight",
    "contract_bias",
    "upstream",
    "clip_ids",
    "block_order",
]
VECTORS = [
    "early_gain",
    "early_shift",
    "query_bias",
    "value_bias",
    "output_bias",
    "late_gain",
    "late_shift",
    "expand_bias",
    "contract_bias",
]
RESULTS = ["block_out", "token_grad", "ffc", "e1g", "e2g", "wag", "wbg", "svg"]


def layer_kernel(names, *refs):
    r = types.SimpleNamespace(**dict(zip(names, refs)))
    d_model = 768
    row = 4 * TOK
    dp, blk = lax.axis_index("dp"), lax.axis_index("blk")
    core, chip = blk % 2, blk // 2
    sibling, across = blk + 1 - 2 * core, (blk + 2) % 4
    y, z = dp % 2, dp // 2
    z0, z1 = z % 2, z // 2
    to_core = {"dp": dp, "blk": sibling}
    to_x = {"dp": dp, "blk": across}
    to_y = {"dp": dp + 1 - 2 * y, "blk": blk}
    to_z0 = {"dp": dp + 2 - 4 * z0, "blk": blk}
    to_z1 = {"dp": (dp + 4) % 8, "blk": blk}
    far = (sibling + 2) % 4
    to_far = {"dp": dp, "blk": far}
    peers = (to_core, to_x, to_far, to_y, to_z0, to_z1)
    numbers = itertools.count()
    sent = []

    def remote(source, target, peer):
        number = next(numbers)
        assert number < 128
        return pltpu.make_async_remote_copy(
            src_ref=source,
            dst_ref=target,
            send_sem=r.send_sem.at[number],
            recv_sem=r.recv_sem.at[number],
            device_id=peer,
            device_id_type=MESH,
        )

    def send(source, target, peer):
        copy = remote(source, target, peer)
        copy.start()
        sent.append(copy)
        return copy

    def rows_at(ref, size, base=0):
        return lambda index: ref.at[pl.ds(pl.multiple_of(base + index * size, size), size)]

    def gather(source, place):
        over_x = send(source, place(blk), to_x)
        over_core = send(source, place(blk), to_core)
        return over_x, over_core, place

    def forward(gathering):
        over_x, over_core, place = gathering
        over_x.wait_recv()
        return send(place(across), place(across), to_core)

    written = []

    def write_out(name):
        copy = pltpu.make_async_copy(
            getattr(r, name), getattr(r, "out_" + name), r.local_sem.at[24 + len(written)]
        )
        copy.start()
        written.append(copy)

    half = 512 + 128 * chip
    tile_at = pl.ds(pl.multiple_of(128 * blk, 128), 128)
    half_at = pl.ds(pl.multiple_of(half, 128), 128)
    ff_at = pl.ds(pl.multiple_of(768 * blk, 128), 768)
    own_rows = pl.ds(pl.multiple_of(TOK * blk, TOK), TOK)
    local = [
        (r.tokens.at[0], r.x_all.at[own_rows]),
        (r.query_weight.at[:, tile_at], r.wab.at[:, 0:128]),
        (r.key_weight.at[:, tile_at], r.wab.at[:, 128:256]),
        (r.value_weight.at[:, tile_at], r.wab.at[:, 256:384]),
        (r.query_weight.at[:, half_at], r.wb_tile.at[0]),
        (r.key_weight.at[:, half_at], r.wb_tile.at[1]),
        (r.value_weight.at[:, half_at], r.wb_tile.at[2]),
        (r.output_weight, r.wo),
        (r.upstream.at[0], r.u_all.at[own_rows]),
        (r.contract_weight.at[ff_at], r.w2),
        (r.expand_weight.at[:, ff_at], r.w1),
    ]
    local += [
        (getattr(r, name), getattr(r, "v_" + name))
        for name in VECTORS + ["clip_ids", "block_order"]
    ]
    loads = []
    for number, (source, target) in enumerate(local):
        copy = pltpu.make_async_copy(source, target, r.local_sem.at[number])
        copy.start()
        loads.append(copy)

    barrier = pltpu.get_barrier_semaphore()
    for peer in peers:
        pl.semaphore_signal(barrier, inc=1, device_id=peer, device_id_type=MESH)
    pl.semaphore_wait(barrier, len(peers))

    tokens_in = gather(r.tokens.at[0], rows_at(r.x_all, TOK))
    upstream_in = gather(r.upstream.at[0], rows_at(r.u_all, TOK))

    for copy in loads[11:]:
        copy.wait()
    early_gain, early_shift = row_of(r.v_early_gain), row_of(r.v_early_shift)
    late_gain, late_shift = row_of(r.v_late_gain), row_of(r.v_late_shift)

    def picked(vector, size, base, width):
        total = jnp.zeros((1, width), F32)
        for index in range(4):
            begin = base + size * index
            total = total + jnp.where(blk == index, vector[:, begin : begin + width], 0.0)
        return total

    query_bias, value_bias = row_of(r.v_query_bias), row_of(r.v_value_bias)
    bias_qkv = jnp.concatenate(
        [
            picked(query_bias, 128, 0, 128),
            jnp.zeros((1, 128), F32),
            picked(value_bias, 128, 0, 128),
            picked(query_bias, 64, 512, 64),
            jnp.zeros((1, 64), F32),
            picked(value_bias, 64, 512, 64),
        ],
        axis=1,
    )

    lane = lax.broadcasted_iota(jnp.int32, (1, TOK), 1)
    keys_of, low_of = [], []
    for index in range(4):
        place = r.v_block_order[0, index]
        clip = jnp.zeros((1, TOK), jnp.int32)
        for other in range(4):
            clip = clip + jnp.where(
                place == other, r.v_clip_ids[0:1, other * TOK : (other + 1) * TOK], 0
            )
        low_of.append((clip * row).astype(F32))
        keys_of.append((clip * row + place * TOK + lane).astype(F32))
    for key in range(4):
        column = jnp.broadcast_to(keys_of[key], (TOK, TOK)).T
        for query in range(4):
            allowed = (column <= keys_of[query]) & (column >= low_of[query])
            r.mask[key * TOK : (key + 1) * TOK, query * TOK : (query + 1) * TOK] = jnp.where(
                allowed, 0.0, MASKED
            )

    for copy in loads[1:7]:
        copy.wait()
    for index in range(3):
        tile = r.wb_tile[index].astype(F32)
        piece = jnp.where(core == 1, tile[:, 64:128], tile[:, 0:64])
        r.wab[:, 384 + 64 * index : 448 + 64 * index] = piece.astype(BF16)

    def early_norm(start):
        def body(at):
            normed, _ = norm_stats(r.x_all[pl.ds(at, 32), :].astype(F32))
            r.normed[pl.ds(at, 32), :] = normed
            r.first[pl.ds(at, 32), :] = (normed * early_gain + early_shift).astype(BF16)

        by_rows(start, TOK, 32, body, 4)

    def project(start):
        at = pl.ds(pl.multiple_of(start, 2 * TOK), 2 * TOK)
        out = mm(r.first[at, :], r.wab[...], 1, 0) + bias_qkv
        for head, offset, step in ((0, 0, 128), (1, 64, 128), (2, 384, 64)):
            query = out[:, offset : offset + 64]
            r.qh[head, at, :] = (query * 0.125).astype(BF16)
            r.kh[head, at, :] = out[:, offset + step : offset + step + 64].astype(BF16)
            r.vh[head, at, :] = out[:, offset + 2 * step : offset + 2 * step + 64].astype(BF16)

    loads[0].wait()
    early_norm(TOK * blk)
    tokens_in[1].wait_recv()
    early_norm(TOK * sibling)
    project(2 * TOK * chip)
    token_forward = forward(tokens_in)
    early_norm(TOK * across)
    token_forward.wait_recv()
    early_norm(TOK * ((sibling + 2) % 4))
    project(2 * TOK * (1 - chip))

    def attend(head):
        r.st[...] = mm(r.kh[head], r.qh[head], 1, 1)

        @pl.loop(0, 4, unroll=2)
        def _(strip):
            at = pl.ds(pl.multiple_of(strip * TOK, TOK), TOK)
            scores = r.st[:, at] + r.mask[:, at]
            powers = jnp.exp(scores - jnp.max(scores, axis=0, keepdims=True))
            probs = powers * (1.0 / jnp.sum(powers, axis=0, keepdims=True))
            r.pf[head, :, at] = probs
            r.pb[head, :, at] = probs.astype(BF16)

        r.vt[head] = r.vh[head].T
        return mm(r.vt[head], r.pb[head], 1, 0).astype(BF16)

    places = (
        lambda index: pl.multiple_of(128 * index, 64),
        lambda index: pl.multiple_of(128 * index + 64, 64),
        lambda index: pl.multiple_of(512 + 64 * index, 64),
    )

    def head_at(head):
        return lambda index: r.at.at[pl.ds(places[head](index), 64)]

    def attend_and_send(head):
        r.at[pl.ds(places[head](blk), 64), :] = attend(head)
        return gather(head_at(head)(blk), head_at(head))

    start_pair = pl.multiple_of(128 * blk, 128)
    heads_in = [attend_and_send(0)]
    upstream_forward = forward(upstream_in)
    heads_in += [attend_and_send(1), attend_and_send(2)]

    loads[8].wait()
    loads[9].wait()
    upstream_in[1].wait_recv()
    upstream_forward.wait_recv()
    head_forwards = []
    for tile in range(3):
        at = slice(256 * tile, 256 * (tile + 1))
        r.ga[:, at] = mm(r.u_all[...], r.w2[at, :], 1, 1)
        head_forwards.append(forward(heads_in[tile]))
    r.first_t[...] = r.first[...].T
    for head in range(3):
        r.kt[head] = r.kh[head].T
    loads[7].wait()
    loads[10].wait()
    for head in range(3):
        heads_in[head][1].wait_recv()
        head_forwards[head].wait_recv()

    output_bias = row_of(r.v_output_bias)

    @pl.loop(0, 2)
    def _(tile):
        at = pl.ds(pl.multiple_of(tile * 256, 256), 256)
        r.mid[at, :] = mm(r.at[:, at], r.wo[...], 0, 0)

    def late_norm(at):
        at = pl.ds(at, 32)
        middle = r.mid[at, :] + r.x_all[at, :].astype(F32) + output_bias
        r.mid[at, :] = middle
        normed, _ = norm_stats(middle)
        r.second[at, :] = (normed * late_gain + late_shift).astype(BF16)

    by_rows(0, row, 32, late_norm, 4)

    for tile in range(3):
        at = slice(256 * tile, 256 * (tile + 1))
        r.hid[:, at] = mm(r.second[...], r.w1[:, at], 1, 0)

    expand_bias = picked(row_of(r.v_expand_bias), 768, 0, 768)
    first_factor = 0.7978845608028654
    third_factor = 0.044715

    def gelu(at):
        at = pl.ds(at, 16)
        hidden = r.hid[at, :] + expand_bias
        square = hidden * hidden
        bent = jnp.tanh(first_factor * hidden * (1.0 + third_factor * square))
        grown = 0.5 * (1.0 + bent)
        r.act[at, :] = (hidden * grown).astype(BF16)
        slope = grown + (0.5 * first_factor) * hidden * (1.0 - bent * bent) * (
            1.0 + (3.0 * third_factor) * square
        )
        r.gh[at, :] = (r.ga[at, :] * slope).astype(BF16)

    by_rows(0, row, 16, gelu, 4)

    def contract_half(which):
        at = pl.ds(pl.multiple_of(384 * which, 384), 384)
        return mm(r.act[:, at], r.u_all[...], 0, 0)

    piece = 384 // PIECES
    pieces = [pl.ds(p * piece, piece) for p in range(PIECES)]

    r.c_send[...] = contract_half(1 - y).astype(BF16)
    c_y = [send(r.c_send.at[at], r.c_recv.at[0, at], to_y) for at in pieces]

    def block_rows(block):
        return pl.ds(pl.multiple_of(block * TOK, TOK), TOK)

    def two_blocks(ref, first, second):
        return jnp.concatenate([ref[block_rows(first), :], ref[block_rows(second), :]], axis=0)

    def scatter_send(number, index):
        return send(r.rs_send.at[number, index], r.rs_recv.at[number, index], to_core)

    def part_pair(grads, weight, first, second):
        @pl.loop(0, 3)
        def _(tile):
            at = pl.ds(pl.multiple_of(tile * 256, 256), 256)
            value = mm(two_blocks(grads, first, second), weight[at, :], 1, 1)
            r.part[block_rows(first), at] = value[0:TOK]
            r.part[block_rows(second), at] = value[TOK : 2 * TOK]

    def part_start(number, grads, weight):
        part_pair(grads, weight, far, sibling)
        copies = scatter_start(number, r.part)
        part_pair(grads, weight, across, blk)
        return copies

    def scatter_start(number, part):
        copies = [None, None]
        for index, block in ((1, far), (0, sibling)):
            r.rs_send[number, index] = part[block_rows(block), :].astype(BF16)
            copies[index] = scatter_send(number, index)
        return copies

    def scatter_middle(number, part, copies):
        at = pl.ds(pl.multiple_of(across * TOK, TOK), TOK)
        copies[1].wait_recv()
        r.rs_send[number, 2] = (part[at, :] + r.rs_recv[number, 1].astype(F32)).astype(BF16)
        copies.append(send(r.rs_send.at[number, 2], r.rs_recv.at[number, 2], to_x))

    def scatter_end(copies):
        copies[0].wait_recv()
        copies[2].wait_recv()

    def scattered(number, part, at, size):
        own = pl.ds(pl.multiple_of(blk * TOK + at, size), size)
        here = pl.ds(at, size)
        return (
            part[own, :]
            + r.rs_recv[number, 0, here, :].astype(F32)
            + r.rs_recv[number, 2, here, :].astype(F32)
        )

    def added(target, left, right):
        rows = target.shape[0]

        @pl.loop(0, rows // 32, unroll=3)
        def _(index):
            at = pl.ds(pl.multiple_of(index * 32, 32), 32)
            target[at, :] = (left[at, :].astype(F32) + right[at, :].astype(F32)).astype(target.dtype)

    along_y, along_z0, along_z1 = (y, 1, to_y), (z0, 2, to_z0), (z1, 4, to_z1)

    def halving(name, stages):
        buf, r1, s1, r2, s2 = (
            getattr(r, name + key) for key in ("_buf", "_r1", "_s1", "_r2", "_s2")
        )
        own = [bit * weight for bit, weight, _ in stages]
        other = [(1 - bit) * weight for bit, weight, _ in stages]
        rest = [
            later + last
            for later in (other[1], own[1])
            for last in (other[2], own[2])
        ]
        copies = {}

        def start1():
            copies[1] = [
                send(buf.at[other[0] + rest[index]], r1.at[index], stages[0][2])
                for index in range(4)
            ]

        def end1(*indices):
            for index in indices:
                copies[1][index].wait_recv()
                added(s1.at[index], buf.at[own[0] + rest[index]], r1.at[index])

        def start2():
            copies[2] = [send(s1.at[index], r2.at[index], stages[1][2]) for index in range(2)]

        def start3():
            copies[2][0].wait_recv()
            added(s2.at[0], s1.at[2], r2.at[0])
            copies[3] = send(s2.at[0], r2.at[2], stages[2][2])
            copies[2][1].wait_recv()
            added(s2.at[1], s1.at[3], r2.at[1])

        def finish(target):
            copies[3].wait_recv()
            added(target.at[blk], s2.at[1], r2.at[2])
            place = lambda index: target.at[index]
            return gather(place(blk), place)

        return types.SimpleNamespace(
            start1=start1, end1=end1, start2=start2, start3=start3, finish=finish
        )

    e1 = halving("e1", (along_z0, along_z1, along_y))
    e2 = halving("e2", (along_y, along_z0, along_z1))
    wa = halving("wa", (along_y, along_z0, along_z1))
    wb = halving("wb", (along_y, along_z0, along_z1))

    def expand_part(target, columns):
        for which in range(2):
            block = mm(r.second[:, 384 * which : 384 * (which + 1)], r.gh[:, columns], 0, 0)
            target[4 * which : 4 * which + 4] = block.astype(BF16).reshape(4, 96, 384)

    second_sum = part_start(0, r.gh, r.w1)
    scatter_middle(0, r.part, second_sum)
    expand_part(r.e1_buf, slice(0, 384))
    e1.start1()
    r.c_own[...] = contract_half(y)
    expand_part(r.e2_buf, slice(384, 768))
    e2.start1()

    for tile in range(3):
        at = slice(256 * tile, 256 * (tile + 1))
        r.part_out[:, at] = mm(r.act[...], r.w2[:, at], 1, 0)

    out_sum = scatter_start(1, r.part_out)

    scatter_end(second_sum)
    own_start = blk * TOK
    r.sv[0] = jnp.zeros((8, d_model), F32)

    def late_pull(index, carry):
        gain_sum, shift_sum, output_sum, contract_sum = carry
        at = pl.multiple_of(index * 32, 32)
        own = pl.ds(pl.multiple_of(own_start + at, 32), 32)
        grad = scattered(0, r.part, at, 32)
        normed, inverse = norm_stats(r.mid[own, :])
        upstream = r.u_all[own, :].astype(F32)
        middle = upstream + norm_pull(grad, normed, inverse, late_gain)
        r.g_mid[pl.ds(at, 32), :] = middle
        low = middle.astype(BF16)
        r.gb[own, :] = low
        return (
            gain_sum + folded(grad * normed),
            shift_sum + folded(grad),
            output_sum + folded(low.astype(F32)),
            contract_sum + folded(upstream),
        )

    nothing = jnp.zeros((8, d_model), F32)
    sums = lax.fori_loop(0, TOK // 32, late_pull, (nothing,) * 4, unroll=4)

    pulled = mm(r.gb[own_rows, :], r.wo[...], 1, 1)
    r.go_send[...] = pulled[:, 0:512].astype(BF16)
    for index in range(4):
        r.third_send[index] = pulled[:, 512 + 64 * index : 576 + 64 * index].astype(BF16)
    head_grads = []
    for block, peer in ((far, to_far), (across, to_x), (sibling, to_core)):
        lanes = pl.ds(pl.multiple_of(128 * block, 128), 128)
        head_grads.append(send(r.go_send.at[:, lanes], r.go_pair.at[own_rows], peer))
        head_grads.append(send(r.third_send.at[block], r.go.at[2, own_rows], peer))
    r.go_pair[own_rows, :] = r.go_send[:, tile_at]
    r.go[2, own_rows, :] = r.third_send[blk]
    branch_at = rows_at(r.gb, TOK)
    branch_in = gather(branch_at(blk), branch_at)
    for index, value in zip((3, 4, 2, 5), sums):
        r.sv[0, index : index + 1, :] = jnp.sum(value, axis=0, keepdims=True)

    e1.end1(0, 1)
    e1.start2()

    root0, root1 = blk % 2, blk // 2
    keeps0 = z0 == root0
    keeps1 = z1 == root1
    is_root = z == blk
    is_across = z == across
    c_z0 = [remote(r.c_sum.at[0, at], r.c_recv.at[1, at], to_z0) for at in pieces]
    c_z1 = [remote(r.c_sum.at[1, at], r.c_recv.at[2, at], to_z1) for at in pieces]
    c_x = [remote(r.ffc.at[at], r.ffc.at[at], to_x) for at in pieces]
    c_core = [remote(r.ffc.at[at], r.ffc.at[at], to_core) for at in pieces]

    def contract_y_end(p):
        c_y[p].wait_recv()
        added(r.c_sum.at[0, pieces[p]], r.c_own.at[pieces[p]], r.c_recv.at[0, pieces[p]])

        @pl.when(jnp.logical_not(keeps0))
        def _():
            c_z0[p].start()

    def contract_z0_end(p):
        @pl.when(keeps0)
        def _():
            c_z0[p].wait_recv()
            added(r.c_sum.at[1, pieces[p]], r.c_sum.at[0, pieces[p]], r.c_recv.at[1, pieces[p]])

            @pl.when(jnp.logical_not(keeps1))
            def _():
                c_z1[p].start()

    def contract_z1_end(p):
        @pl.when(is_root)
        def _():
            c_z1[p].wait_recv()
            added(r.ffc.at[pieces[p]], r.c_sum.at[1, pieces[p]], r.c_recv.at[2, pieces[p]])
            c_x[p].start()
            c_core[p].start()

    e1.end1(2, 3)
    contract_y_end(0)

    def expand_sum(index, carry):
        at = pl.ds(pl.multiple_of(index * 32, 32), 32)
        return carry + folded(r.gh[at, :].astype(F32))

    r.sv[0, 6:7, :] = jnp.sum(
        lax.fori_loop(0, row // 32, expand_sum, nothing, unroll=4), axis=0, keepdims=True
    )
    for copy in head_grads:
        copy.wait_recv()
    r.go[0] = r.go_pair[:, 0:64]
    r.go[1] = r.go_pair[:, 64:128]

    def attend_back(head, offset, step):
        r.st[...] = mm(r.vh[head], r.go[head], 1, 1)

        @pl.loop(0, 4, unroll=2)
        def _(strip):
            at = pl.ds(pl.multiple_of(strip * TOK, TOK), TOK)
            probs, grad = r.pf[head, :, at], r.st[:, at]
            delta = jnp.sum(probs * grad, axis=0, keepdims=True)
            r.sg[:, at] = (probs * (grad - delta)).astype(BF16)

        query = mm(r.kt[head], r.sg[...], 1, 0) * 0.125
        r.gqkv[:, offset : offset + 64] = query.T.astype(BF16)
        r.gqkv[:, offset + step : offset + step + 64] = mm(
            r.sg[...], r.qh[head], 1, 0
        ).astype(BF16)
        r.gqkv[:, offset + 2 * step : offset + 2 * step + 64] = mm(
            r.pb[head], r.go[head], 1, 0
        ).astype(BF16)

    halves = [(slice(4 * w, 4 * w + 4), slice(384 * w, 384 * (w + 1))) for w in range(2)]
    contract_y_end(1)
    attend_back(0, 0, 128)
    contract_z0_end(0)
    attend_back(1, 64, 128)
    for blocks, at in halves:
        block = mm(r.first_t[at, :], r.gqkv[:, 0:384], 1, 0)
        r.wa_buf[blocks] = block.astype(BF16).reshape(4, 96, 384)
    wa.start1()
    scatter_middle(1, r.part_out, out_sum)
    branch_forward = forward(branch_in)
    e1.start3()
    attend_back(2, 384, 64)
    contract_z0_end(1)
    e2.end1(0, 1)
    e2.start2()

    def qkv_sum(index, carry):
        gain_sum, shift_sum, bias_sum = carry
        at = pl.ds(pl.multiple_of(index * 32, 32), 32)
        part = r.part[at, :]
        return (
            gain_sum + folded(part * r.normed[at, :]),
            shift_sum + folded(part),
            bias_sum + folded(r.gqkv[at, :].astype(F32)),
        )

    first_sum = part_start(2, r.gqkv, r.wab)
    scatter_middle(2, r.part, first_sum)
    sums = lax.fori_loop(
        0, row // 32, qkv_sum, (nothing, nothing, jnp.zeros((8, 576), F32)), unroll=4
    )
    for index in range(2):
        r.sv[0, index : index + 1, :] = jnp.sum(sums[index], axis=0, keepdims=True)
    total = jnp.sum(sums[2], axis=0, keepdims=True)
    r.sv[0, 7:8, 0:384] = total[:, 0:384]
    r.sv[0, 7:8, 512:704] = total[:, 384:576]
    v_y = send(r.sv.at[0], r.sv_recv.at[0], to_y)

    branch_in[1].wait_recv()
    branch_forward.wait_recv()
    r.gbt[:, 0:128] = r.gb[:, tile_at]
    r.gbt[:, 128:256] = r.gb[:, half_at]
    for blocks, at in halves:
        block = mm(r.first_t[at, :], r.gqkv[:, 384:576], 1, 0)
        r.wb_buf[blocks, :, 0:192] = block.astype(BF16).reshape(4, 96, 192)
        block = mm(r.at[at, :], r.gbt[...], 1, 0)
        chosen = jnp.where(core == 1, block[:, 192:256], block[:, 128:192])
        r.wb_buf[blocks, :, 192:256] = chosen.astype(BF16).reshape(4, 96, 64)
        r.wb_buf[blocks, :, 256:384] = block[:, 0:128].astype(BF16).reshape(4, 96, 128)
    wb.start1()
    contract_z1_end(0)
    e2.end1(2, 3)

    scatter_end(out_sum)
    contract_bias = row_of(r.v_contract_bias)

    @pl.loop(0, TOK // 32, unroll=4)
    def _(index):
        at = pl.multiple_of(index * 32, 32)
        own = pl.ds(pl.multiple_of(own_start + at, 32), 32)
        value = scattered(1, r.part_out, at, 32) + r.mid[own, :] + contract_bias
        r.block_out[pl.ds(at, 32), :] = value.astype(BF16)

    write_out("block_out")
    v_y.wait_recv()
    r.sv[1] = r.sv[0] + r.sv_recv[0]
    v_z0 = send(r.sv.at[1], r.sv_recv.at[1], to_z0)
    wa.end1(0, 1)
    wa.start2()
    wa.end1(2, 3)
    e2.start3()

    scatter_end(first_sum)

    @pl.loop(0, TOK // 32, unroll=4)
    def _(index):
        at = pl.multiple_of(index * 32, 32)
        own = pl.ds(pl.multiple_of(own_start + at, 32), 32)
        here = pl.ds(at, 32)
        grad = scattered(2, r.part, at, 32)
        normed, inverse = norm_stats(r.x_all[own, :].astype(F32))
        pulled = norm_pull(grad, normed, inverse, early_gain)
        r.token_grad[here, :] = (r.g_mid[here, :] + pulled).astype(BF16)

    write_out("token_grad")
    e1_in = e1.finish(r.e1g)
    v_z0.wait_recv()
    r.sv[2] = r.sv[1] + r.sv_recv[1]
    v_z1 = send(r.sv.at[2], r.sv_recv.at[2], to_z1)
    contract_z1_end(1)
    wb.end1(0, 1)
    wb.start2()
    wb.end1(2, 3)
    e2_in = e2.finish(r.e2g)
    wa.start3()

    @pl.when(is_across)
    def _():
        for p in range(PIECES):
            c_x[p].wait_recv()
            c_core[p].start()

    e1_forward = forward(e1_in)
    v_z1.wait_recv()
    r.svg[blk] = r.sv[2] + r.sv_recv[2]
    v_at = lambda index: r.svg.at[index]
    v_in = gather(v_at(blk), v_at)
    wb.start3()
    e2_forward = forward(e2_in)
    wa_in = wa.finish(r.wag)

    @pl.when(jnp.logical_not(jnp.logical_or(is_root, is_across)))
    def _():
        for p in range(PIECES):
            c_core[p].wait_recv()

    write_out("ffc")
    v_forward = forward(v_in)
    wb_in = wb.finish(r.wbg)
    wa_forward = forward(wa_in)
    wb_forward = forward(wb_in)
    for name, gathering, copy in (
        ("e1g", e1_in, e1_forward),
        ("e2g", e2_in, e2_forward),
        ("svg", v_in, v_forward),
        ("wag", wa_in, wa_forward),
        ("wbg", wb_in, wb_forward),
    ):
        gathering[1].wait_recv()
        copy.wait_recv()
        write_out(name)

    for copy in written:
        copy.wait()

    for copy in sent:
        copy.wait_send()

    @pl.when(jnp.logical_not(keeps0))
    def _():
        for copy in c_z0:
            copy.wait_send()

    @pl.when(jnp.logical_and(keeps0, jnp.logical_not(keeps1)))
    def _():
        for copy in c_z1:
            copy.wait_send()

    @pl.when(is_root)
    def _():
        for copy in c_x:
            copy.wait_send()

    @pl.when(jnp.logical_or(is_root, is_across))
    def _():
        for copy in c_core:
            copy.wait_send()


def write_kernel(*refs):
    count, sources, outs = len(RESULTS), refs[: len(RESULTS)], refs[len(RESULTS) :][:17]
    held, made = refs[count + 17 :][:count], refs[2 * count + 17 :][:15]
    in_sem, out_sem = refs[-2:]
    (gain_early, shift_early, query_grad, bias_query, key_grad, value_grad) = made[:6]
    (bias_value, output_grad, bias_output, gain_late, shift_late, expand_grad, bias_expand) = made[6:13]
    contract_grad, bias_contract = made[13:]
    dp = lax.axis_index("dp")
    loads = [
        pltpu.make_async_copy(source, target, in_sem.at[number])
        for number, (source, target) in enumerate(zip(sources, held))
    ]
    for number in (3, 4, 2, 5, 6, 7, 0, 1):
        loads[number].start()
    block_out, token_grad, ffc, e1g, e2g, wag, wbg, svg = held
    left = []

    def leave(target):
        number = [item is target for item in made].index(True)
        copy = pltpu.make_async_copy(target, outs[number + 2], out_sem.at[number + 2])
        copy.start()
        left.append(copy)

    for copy in loads[3:5]:
        copy.wait()
    for index in range(4):
        expand_grad[:, 768 * index : 768 * index + 384] = e1g[index].astype(F32)
        expand_grad[:, 768 * index + 384 : 768 * (index + 1)] = e2g[index].astype(F32)
    leave(expand_grad)
    loads[2].wait()
    contract_grad[...] = ffc[...].astype(F32)
    leave(contract_grad)
    for copy in loads[5:7]:
        copy.wait()
    for number, target in enumerate((query_grad, key_grad, value_grad, output_grad)):
        for index in range(4):
            wide = slice(128 * index, 128 * (index + 1))
            narrow = slice(512 + 64 * index, 576 + 64 * index)
            if number < 3:
                target[:, wide] = wag[index, :, 128 * number : 128 * (number + 1)].astype(F32)
            else:
                target[:, wide] = wbg[index, :, 256:384].astype(F32)
            target[:, narrow] = wbg[index, :, 64 * number : 64 * (number + 1)].astype(F32)
        leave(target)
    loads[7].wait()
    summed = svg[0] + svg[1] + svg[2] + svg[3]
    query_row = jnp.concatenate(
        [svg[i, 7:8, 0:128] for i in range(4)] + [svg[i, 7:8, 512:576] for i in range(4)], axis=1
    )
    value_row = jnp.concatenate(
        [svg[i, 7:8, 256:384] for i in range(4)] + [svg[i, 7:8, 640:704] for i in range(4)], axis=1
    )
    rows = jnp.concatenate([summed[0:6], query_row, value_row], axis=0)
    turned = pltpu.roll(rows, 768 - 96 * dp, 1)
    targets = (gain_early, shift_early, bias_output, gain_late, shift_late, bias_contract)
    for number, target in enumerate(targets + (bias_query, bias_value)):
        target[...] = turned[number, 0:96]
        leave(target)
    hidden = jnp.zeros((8, 768), F32)
    for index in range(4):
        hidden = hidden + jnp.where(dp // 2 == index, svg[index], 0.0)
    bias_expand[...] = pltpu.roll(hidden, 768 - 384 * (dp % 2), 1)[6, 0:384]
    leave(bias_expand)
    for number, value in enumerate((block_out, token_grad)):
        loads[number].wait()
        copy = pltpu.make_async_copy(value, outs[number].at[0], out_sem.at[number])
        copy.start()
        left.append(copy)
    for copy in left:
        copy.wait()


def fast_local(*arguments):
    scratch = fast_scratch()
    away = pl.BlockSpec(memory_space=pl.ANY)
    shape = jax.ShapeDtypeStruct
    results = (
        shape((TOK, 768), BF16),
        shape((TOK, 768), BF16),
        shape((384, 768), BF16),
        shape((4, 96, 384), BF16),
        shape((4, 96, 384), BF16),
        shape((4, 96, 384), BF16),
        shape((4, 96, 384), BF16),
        shape((4, 8, 768), F32),
    )
    names = INPUTS + ["out_" + name for name in RESULTS] + list(scratch)
    moved = pl.pallas_call(
        functools.partial(layer_kernel, names),
        name="layer",
        out_shape=results,
        in_specs=[away] * len(INPUTS),
        out_specs=(away,) * len(results),
        scratch_shapes=list(scratch.values()),
        compiler_params=pltpu.CompilerParams(
            collective_id=0, has_side_effects=True, vmem_limit_bytes=56 << 20
        ),
    )(*arguments)
    outs = (
        [shape((1, TOK, 768), BF16)] * 2
        + [shape((96,), F32)] * 2
        + [shape((96, 768), F32), shape((96,), F32), shape((96, 768), F32), shape((96, 768), F32)]
        + [shape((96,), F32), shape((96, 768), F32)]
        + [shape((96,), F32)] * 3
        + [shape((96, 3072), F32), shape((384,), F32), shape((384, 768), F32), shape((96,), F32)]
    )
    return pl.pallas_call(
        write_kernel,
        name="write",
        out_shape=tuple(outs),
        in_specs=[away] * len(results),
        out_specs=(away,) * len(outs),
        scratch_shapes=[pltpu.VMEM(item.shape, item.dtype) for item in results]
        + [pltpu.VMEM(item.shape, item.dtype) for item in outs[2:]]
        + [pltpu.SemaphoreType.DMA((8,)), pltpu.SemaphoreType.DMA((17,))],
        compiler_params=pltpu.CompilerParams(vmem_limit_bytes=60 << 20),
    )(*moved)


def passed_along(value, axis, steps):
    count = lax.axis_size(axis)
    pairs = [(source, (source + steps) % count) for source in range(count)]
    return lax.ppermute(value, axis, pairs)


def layer_norm(inputs, gain, shift):
    average = jnp.mean(inputs, axis=-1, keepdims=True)
    centred = inputs - average
    inverse = lax.rsqrt(jnp.mean(centred * centred, axis=-1, keepdims=True) + EPSILON)
    normed = centred * inverse
    return (normed * gain + shift, normed, inverse)


def norm_back(grad_out, normed, inverse, gain):
    scaled = grad_out * gain
    inner = (
        scaled
        - jnp.mean(scaled, axis=-1, keepdims=True)
        - normed * jnp.mean(scaled * normed, axis=-1, keepdims=True)
    )
    return (
        inverse * inner,
        jnp.sum(grad_out * normed, axis=(0, 1)),
        jnp.sum(grad_out, axis=(0, 1)),
    )


def project(inputs, weight):
    return jnp.einsum("rtd,de->rte", inputs, weight, preferred_element_type=jnp.float32)


def project_back(grad_rows, weight):
    return jnp.einsum("rte,de->rtd", grad_rows, weight, preferred_element_type=jnp.float32)


def weight_grad(inputs, grad_rows):
    return jnp.einsum("rtd,rte->de", inputs, grad_rows, preferred_element_type=jnp.float32)


def column_sum(grad_rows):
    return jnp.sum(grad_rows.astype(jnp.float32), axis=(0, 1))


def general_local(
    tokens,
    early_gain,
    early_shift,
    query_weight,
    query_bias,
    key_weight,
    value_weight,
    value_bias,
    output_weight,
    output_bias,
    late_gain,
    late_shift,
    expand_weight,
    expand_bias,
    contract_weight,
    contract_bias,
    upstream,
    clip_ids,
    block_order,
):
    row_count, block_len, features = tokens.shape
    head_count = HEADS
    head_size = features // head_count
    scale_factor = float(head_size) ** (-0.5)
    my_index = lax.axis_index("blk")
    group_size = lax.axis_size("blk")

    def positions(begin, length):
        stored = begin + jnp.arange(length, dtype=jnp.int32)
        logical = (
            jnp.take(block_order, stored // block_len, axis=1) * block_len + stored % block_len
        )
        return (logical, jnp.take_along_axis(clip_ids, logical, axis=1))

    query_pos, query_clip = positions(my_index * block_len, block_len)

    def visible(begin, length):
        key_pos, key_clip = positions(begin, length)
        allowed = (key_pos[:, None, :] <= query_pos[:, :, None]) & (
            key_clip[:, None, :] == query_clip[:, :, None]
        )
        return allowed[:, None]

    def split_heads(array):
        return array.reshape(row_count, array.shape[1], head_count, head_size)

    inputs = tokens.astype(jnp.float32)
    first_full, first_normed, first_inverse = layer_norm(
        inputs, early_gain.astype(jnp.float32), early_shift.astype(jnp.float32)
    )
    first_low = first_full.astype(jnp.bfloat16)
    queries = (project(first_low, query_weight) + query_bias.astype(jnp.float32)).astype(
        jnp.bfloat16
    )
    key_rows = project(first_low, key_weight).astype(jnp.bfloat16)
    value_rows = (project(first_low, value_weight) + value_bias.astype(jnp.float32)).astype(
        jnp.bfloat16
    )
    query_heads = split_heads(queries)

    def scores_of(key_block):
        return (
            jnp.einsum(
                "rqhe,rkhe->rhqk",
                query_heads,
                split_heads(key_block),
                preferred_element_type=jnp.float32,
            )
            * scale_factor
        )

    def absorb(carry, key_block, value_block, begin):
        allowed = visible(begin, key_block.shape[1])
        maximum, denominator, numerator = carry
        scores = jnp.where(allowed, scores_of(key_block), MASKED)
        new_max = jnp.maximum(maximum, jnp.max(scores, axis=-1))
        weights = jnp.where(allowed, jnp.exp(scores - new_max[..., None]), 0.0)
        factor = jnp.exp(maximum - new_max)
        update = jnp.einsum(
            "rhqk,rkhe->rqhe",
            weights.astype(jnp.bfloat16),
            split_heads(value_block),
            preferred_element_type=jnp.float32,
        )
        numerator = numerator * jnp.transpose(factor, (0, 2, 1))[..., None] + update
        return (new_max, denominator * factor + jnp.sum(weights, axis=-1), numerator)

    start_state = (
        jnp.full((row_count, head_count, block_len), MASKED, jnp.float32),
        jnp.zeros((row_count, head_count, block_len), jnp.float32),
        jnp.zeros((row_count, block_len, head_count, head_size), jnp.float32),
    )
    key_piece = lax.all_gather(key_rows, "blk", axis=1, tiled=True)
    value_piece = lax.all_gather(value_rows, "blk", axis=1, tiled=True)
    length = key_piece.shape[1]
    stride = min(length, block_len)

    def one_block(number, running):
        offset = number * stride
        return absorb(
            running,
            lax.dynamic_slice_in_dim(key_piece, offset, stride, 1),
            lax.dynamic_slice_in_dim(value_piece, offset, stride, 1),
            offset,
        )

    maximum, denominator, numerator = lax.fori_loop(0, length // stride, one_block, start_state)
    log_total = maximum + jnp.log(denominator)
    attention = numerator / jnp.transpose(denominator, (0, 2, 1))[..., None]
    attention_low = attention.reshape(row_count, block_len, features).astype(jnp.bfloat16)
    middle = inputs + project(attention_low, output_weight) + output_bias.astype(jnp.float32)
    second_full, second_normed, second_inverse = layer_norm(
        middle, late_gain.astype(jnp.float32), late_shift.astype(jnp.float32)
    )
    second_low = second_full.astype(jnp.bfloat16)
    hidden = project(second_low, expand_weight) + expand_bias.astype(jnp.float32)
    active_full, gelu_pull = jax.vjp(
        lambda values_in: jax.nn.gelu(values_in, approximate=True), hidden
    )
    active_low = active_full.astype(jnp.bfloat16)
    block_out = (
        middle + project(active_low, contract_weight) + contract_bias.astype(jnp.float32)
    ).astype(jnp.bfloat16)
    grad_out = upstream.astype(jnp.float32)
    contract_g = weight_grad(active_low, upstream)
    contract_b = column_sum(upstream)
    hidden_low = gelu_pull(project_back(upstream, contract_weight))[0].astype(jnp.bfloat16)
    expand_g = weight_grad(second_low, hidden_low)
    expand_b = column_sum(hidden_low)
    norm_grad, late_gain_g, late_shift_g = norm_back(
        project_back(hidden_low, expand_weight),
        second_normed,
        second_inverse,
        late_gain.astype(jnp.float32),
    )
    middle_grad = grad_out + norm_grad
    branch_low = middle_grad.astype(jnp.bfloat16)
    output_g = weight_grad(attention_low, branch_low)
    output_b = column_sum(branch_low)
    grad_heads = split_heads(project_back(branch_low, output_weight).astype(jnp.bfloat16))
    delta = jnp.transpose(jnp.sum(grad_heads.astype(jnp.float32) * attention, axis=-1), (0, 2, 1))

    def turn_step(number, carried):
        key_block, value_block, key_acc, value_acc, query_acc = carried
        source = (my_index - number) % group_size
        allowed = visible(source * block_len, block_len)
        use_key, use_value = (key_block, value_block)
        key_sum = key_acc
        value_sum = value_acc
        query_sum = query_acc
        probs = jnp.where(allowed, jnp.exp(scores_of(use_key) - log_total[..., None]), 0.0)
        value_sum = value_sum + jnp.einsum(
            "rhqk,rqhe->rkhe",
            probs.astype(jnp.bfloat16),
            grad_heads,
            preferred_element_type=jnp.float32,
        ).reshape(row_count, block_len, features)
        prob_grad = jnp.einsum(
            "rqhe,rkhe->rhqk",
            grad_heads,
            split_heads(use_value),
            preferred_element_type=jnp.float32,
        )
        score_grad = (probs * (prob_grad - delta[..., None])).astype(jnp.bfloat16)
        query_sum = (
            query_sum
            + jnp.einsum(
                "rhqk,rkhe->rqhe",
                score_grad,
                split_heads(use_key),
                preferred_element_type=jnp.float32,
            )
            * scale_factor
        )
        key_sum = key_sum + (
            jnp.einsum(
                "rhqk,rqhe->rkhe", score_grad, query_heads, preferred_element_type=jnp.float32
            )
            * scale_factor
        ).reshape(row_count, block_len, features)
        key_acc = key_sum
        value_acc = value_sum
        key_block, value_block = passed_along((key_block, value_block), "blk", 1)
        key_acc, value_acc = (
            passed_along(key_acc.astype(jnp.bfloat16), "blk", 1).astype(key_acc.dtype),
            passed_along(value_acc.astype(jnp.bfloat16), "blk", 1).astype(value_acc.dtype),
        )
        return (key_block, value_block, key_acc, value_acc, query_sum)

    zero_rows = jnp.zeros((row_count, block_len, features), jnp.float32)
    carried = (
        key_rows,
        value_rows,
        zero_rows,
        zero_rows,
        jnp.zeros((row_count, block_len, head_count, head_size), jnp.float32),
    )
    carried = lax.fori_loop(0, group_size, turn_step, carried)
    query_low = carried[4].reshape(row_count, block_len, features).astype(jnp.bfloat16)
    key_low = carried[2].astype(jnp.bfloat16)
    value_low = carried[3].astype(jnp.bfloat16)
    query_g = weight_grad(first_low, query_low)
    key_g = weight_grad(first_low, key_low)
    value_g = weight_grad(first_low, value_low)
    query_b = column_sum(query_low)
    value_b = column_sum(value_low)
    first_grad = (
        project_back(query_low, query_weight)
        + project_back(key_low, key_weight)
        + project_back(value_low, value_weight)
    )
    input_grad, early_gain_g, early_shift_g = norm_back(
        first_grad, first_normed, first_inverse, early_gain.astype(jnp.float32)
    )
    token_grad = (middle_grad + input_grad).astype(jnp.bfloat16)
    local_grads = (
        early_gain_g,
        early_shift_g,
        query_g,
        query_b,
        key_g,
        value_g,
        value_b,
        output_g,
        output_b,
        late_gain_g,
        late_shift_g,
        expand_g,
        expand_b,
        contract_g,
        contract_b,
    )
    owners = lax.axis_size("dp")
    laid_out = jnp.concatenate([member.reshape(owners, -1) for member in local_grads], axis=1)
    shares = lax.psum_scatter(laid_out.astype(jnp.bfloat16), "dp", scatter_dimension=0, tiled=True)
    summed = lax.psum(shares, "blk").astype(jnp.float32)
    pieces = []
    offset = 0
    for member in local_grads:
        width = member.size // owners
        own_shape = (member.shape[0] // owners,) + member.shape[1:]
        pieces.append(summed[0, offset : offset + width].reshape(own_shape))
        offset = offset + width
    return (block_out, token_grad) + tuple(pieces)


def solution(mesh):
    placed = (
        P("dp", "blk", None),
        P(),
        P(),
        P(),
        P(),
        P(),
        P(),
        P(),
        P(),
        P(),
        P(),
        P(),
        P(),
        P(),
        P(),
        P(),
        P("dp", "blk", None),
        P("dp", None),
        P("dp", None),
    )
    narrow = mesh.shape["dp"] == 8 and mesh.shape["blk"] == 4
    return jax.shard_map(
        fast_local if narrow else general_local,
        mesh=mesh,
        in_specs=placed,
        out_specs=(
            P("dp", "blk", None),
            P("dp", "blk", None),
            P("dp"),
            P("dp"),
            P("dp", None),
            P("dp"),
            P("dp", None),
            P("dp", None),
            P("dp"),
            P("dp", None),
            P("dp"),
            P("dp"),
            P("dp"),
            P("dp", None),
            P("dp"),
            P("dp", None),
            P("dp"),
        ),
        check_vma=False,
    )
```
